32 devices in a mesh: section: 2 (over core), dp: 4 (over z), tensor: 4 (over y, x).
Axes of the slice: x: 2, y: 2, z: 4, core: 2. Of those that a mesh axis runs over, the one named last changes fastest.
Arguments:
- x_in: bfloat16 [2, 1536, 4, 1536], P(None, 'tensor', 'dp'), may hold values from -6 to 6
- d_out: bfloat16 [2, 1536, 4, 1536], P(None, 'tensor', 'dp'), may hold values from -6 to 6
- doc_lengths: int32 [2, 4, 3], P(None, 'dp'), may hold values from 1 to 1024, 1536 in all within a row
- token_mask: int32 [2, 1536, 4], P(None, None, 'dp'), may hold values 0 or 1
- gain_in: float32 [2, 1536], P('section'), may hold values from 0.5 to 1.5
- w_zx: bfloat16 [2, 1536, 2, 3072], P('section', 'dp', None, 'tensor'), may hold values from -0.15625 to 0.15625
- w_bcdt: bfloat16 [2, 1536, 304], P('section', 'dp'), may hold values from -0.15625 to 0.15625
- conv_x: float32 [2, 5, 3072], P('section', None, 'tensor'), may hold values from -3 to 3
- conv_bc: float32 [2, 5, 256], P('section'), may hold values from -3 to 3
- dt_bias: float32 [2, 48], P('section', 'tensor'), may hold values from -4 to -1
- a_log: float32 [2, 48], P('section', 'tensor'), may hold values from -4.6 to 1
- d_skip: float32 [2, 48], P('section', 'tensor'), may hold values from 0.5 to 1.5
- gain_inner: float32 [2, 3072], P('section', 'tensor'), may hold values from 0.5 to 1.5
- w_out: bfloat16 [2, 3072, 1536], P('section', 'tensor', 'dp'), may hold values from -0.109375 to 0.109375
Outputs:
- out_act: float32 [2, 1536, 4, 1536], P(None, 'tensor', 'dp')
- grad_in: float32 [2, 1536, 4, 1536], P(None, 'tensor', 'dp', 'section')
- grad_gain_in: float32 [2, 1536], P('section')
- grad_w_zx: float32 [2, 1536, 2, 3072], P('section', 'dp', None, 'tensor')
- grad_w_bcdt: float32 [2, 1536, 304], P('section', 'dp')
- grad_conv_x: float32 [2, 5, 3072], P('section', None, 'tensor')
- grad_conv_bc: float32 [2, 5, 256], P('section')
- grad_dt_bias: float32 [2, 48], P('section', 'tensor')
- grad_a_log: float32 [2, 48], P('section', 'tensor')
- grad_d_skip: float32 [2, 48], P('section', 'tensor')
- grad_gain_inner: float32 [2, 3072], P('section', 'tensor')
- grad_w_out: float32 [2, 3072, 1536], P('section', 'tensor', 'dp')
The draws below stay inside these ranges and needn't reach their ends.
Inputs may be any that keep to these rules, and one draw needn't show every extreme that they name: `doc_lengths`: in each slot the 3 lengths add up to 1536, and the longest is exactly 1024.
All inputs are finite; a program needn't handle non-finite values. No bound on the sum of `token_mask` on one device may be relied on, other than what follows from the above.
Results may differ from the reference program's by a relative error of at most 0.012.
The reference program's roundings to bfloat16 on the way count: a program that leaves them out, or rounds other values in their place, can miss the bound.
Values may be sent and summed in bfloat16 or wider, within the bound.
No kernel may reach another device: no remote copies, remote signals or barrier semaphores. Data moves between devices by JAX's collectives and lax.ppermute only.
A program may use at most 448 MiB of HBM per device.

```python
import math
from functools import partial
import jax
import jax.numpy as jnp
import numpy as np
from jax import lax

D = 1536
DI = 3072
H = 48
NSTATE = 128
KCONV = 4
SEQ = 1536
LONGEST = 1024
DOCS = 3
MB = 2
SLOTS = 4
BCDT = 304


def place_ends(drawn, key, low, high):
    longest = drawn.shape.index(max(drawn.shape))
    spots = []
    for shift in (0, 1):
        where = [jax.random.randint(jax.random.fold_in(key, axis), (), 0, length) for axis, length in enumerate(drawn.shape)]
        where[longest] = (where[longest] + shift) % drawn.shape[longest]
        spots.append(tuple(where))
    return drawn.at[spots[0]].set(low).at[spots[1]].set(high)


def levels(rng, dims, split, low, largest):
    factor_of = 1.0
    for axis_at, parts in split:
        draws = jax.random.uniform(jax.random.fold_in(jax.random.fold_in(rng, 6), axis_at), (parts,), jnp.float32, low / len(split), largest / len(split))
        factor_of = factor_of * jnp.repeat(jnp.exp(draws), dims[axis_at] // parts).reshape((-1,) + (1,) * (len(dims) - 1 - axis_at))
    return factor_of


def length_profile(count, total, most, slope):
    loads = [(1 << 20) // math.isqrt(standing ** slope) + 1 for standing in range(2, count + 1)]
    spare, counts = total - most - (count - 1), [1] * (count - 1)
    while spare > 0:
        movable = [i for i in range(count - 1) if counts[i] < most]
        pool, remaining = sum([loads[i] for i in movable]), spare
        for i in movable:
            extra = min(most - counts[i], max(1, remaining * loads[i] // pool), spare)
            counts[i] = counts[i] + extra
            spare = spare - extra
    return np.array([most] + counts)


def uneven_parts(own_key, count, total, bound, lean):
    if count == 2:
        one = jax.random.randint(own_key, (), max(1, total - bound), min(bound, total - 1) + 1)
        return jnp.stack([one, total - one])
    tallies = jnp.asarray(length_profile(count, total, bound, lean), jnp.int32)
    couples = (count - 1) // 2
    giver, sink = tallies[1:1 + 2 * couples:2], tallies[2:2 + 2 * couples:2]
    slack = jnp.minimum(giver - 1, bound - sink)
    passed = jax.random.randint(jax.random.fold_in(own_key, 1), (couples,), 0, 1 << 20) % (slack + 1)
    tallies = tallies.at[1:1 + 2 * couples:2].set(giver - passed).at[2:2 + 2 * couples:2].set(sink + passed)
    return tallies[jax.random.permutation(jax.random.fold_in(own_key, 2), count)]


def bell_draw(stream_key, extent, scale, bound, shards=(), kind=jnp.bfloat16):
    values = jax.random.normal(stream_key, extent, jnp.float32) * scale
    if len(shards) > 0:
        values = levels(stream_key, extent, shards, -0.22, 0.18) * values
    return jnp.clip(values, min=-bound, max=bound).astype(kind)


def setup_inputs(seed: int = 0) -> dict:
    key_list = jax.random.split(jax.random.key(seed), 15)
    x_in = bell_draw(key_list[0], (MB, SEQ, SLOTS, D), 1.0, 6.0, ((1, 4), (2, 4)))
    d_out = bell_draw(key_list[1], (MB, SEQ, SLOTS, D), 1.0, 6.0, ((1, 4), (2, 4)))
    doc_lengths = jax.vmap(lambda own: uneven_parts(own, DOCS, SEQ, LONGEST, 2))(jax.random.split(key_list[2], MB * SLOTS)).reshape((MB, SLOTS, DOCS)).astype(jnp.int32)
    token_mask = place_ends((jax.random.randint(key_list[3], (MB, SEQ, SLOTS), 0, 8) < 7).astype(jnp.int32), jax.random.fold_in(key_list[3], 1), 0, 1)
    gain_in = jnp.clip(1.0 + 0.1 * jax.random.normal(key_list[4], (2, D), jnp.float32), 0.5, 1.5)
    w_zx = bell_draw(key_list[5], (2, D, 2, DI), D ** -0.5, 0.15625, ((0, 2), (1, 4), (3, 4)))
    w_bcdt = bell_draw(key_list[6], (2, D, BCDT), D ** -0.5, 0.15625, ((0, 2), (1, 4)))
    conv_x = bell_draw(key_list[7], (2, KCONV + 1, DI), KCONV ** -0.5, 3.0, ((0, 2), (2, 4)), jnp.float32)
    conv_bc = bell_draw(key_list[8], (2, KCONV + 1, 2 * NSTATE), KCONV ** -0.5, 3.0, ((0, 2),), jnp.float32)
    dt_bias = jnp.clip(-4.0 + 3.0 * jax.random.uniform(key_list[9], (2, H), jnp.float32) ** levels(key_list[9], (2, H), ((0, 2), (1, 4)), -0.2, 0.2), -4.0, -1.0)
    a_log = jnp.clip(-4.6 + 5.6 * jax.random.uniform(key_list[10], (2, H), jnp.float32) ** levels(key_list[10], (2, H), ((0, 2), (1, 4)), -0.2, 0.2), -4.6, 1.0)
    d_skip = jnp.clip(0.5 + 1.0 * jax.random.uniform(key_list[11], (2, H), jnp.float32) ** levels(key_list[11], (2, H), ((0, 2), (1, 4)), -0.2, 0.2), 0.5, 1.5)
    gain_inner = jnp.clip(1.0 + 0.1 * jax.random.normal(key_list[12], (2, DI), jnp.float32), 0.5, 1.5)
    w_out = bell_draw(key_list[13], (2, DI, D), DI ** -0.5, 0.109375, ((0, 2), (1, 4), (2, 4)))
    return dict(x_in=x_in, d_out=d_out, doc_lengths=doc_lengths, token_mask=token_mask, gain_in=gain_in, w_zx=w_zx, w_bcdt=w_bcdt, conv_x=conv_x, conv_bc=conv_bc, dt_bias=dt_bias, a_log=a_log, d_skip=d_skip, gain_inner=gain_inner, w_out=w_out)


EPS = 1e-05
PRECISE = lax.Precision.HIGHEST

@jax.custom_vjp
def low(v):
    return lax.optimization_barrier(v.astype(jnp.bfloat16)).astype(jnp.float32)

@jax.custom_vjp
def low_back(v):
    return v

def low_keep(v):
    return (low(v), None)

def low_pass(kept, grad):
    return (grad,)

def back_keep(v):
    return (v, None)

def back_low(kept, grad):
    return (low(grad),)
low.defvjp(low_keep, low_pass)
low_back.defvjp(back_keep, back_low)

def conv_taps(signal, taps, doc_ids):
    reach = taps.shape[0] - 1
    length = signal.shape[0]
    summed = taps[reach] + taps[reach - 1] * signal
    for offset in range(1, reach):
        shifted = jnp.concatenate([jnp.zeros_like(signal[:offset]), signal[:length - offset]], 0)
        moved_ids = jnp.concatenate([jnp.full_like(doc_ids[:offset], -1), doc_ids[:length - offset]], 0)
        same_doc = (moved_ids == doc_ids).astype(jnp.float32)[..., None]
        summed = summed + taps[reach - 1 - offset] * shifted * same_doc
    return summed

def slot_layer(residual, live_row, doc_ids, weights, final_layer):
    gain_in, w_zx, w_bcdt, conv_x, conv_bc, dt_bias, a_log, d_skip, gain_inner, w_out = weights
    length = residual.shape[0]
    state_count = conv_bc.shape[1] // 2
    head_count = dt_bias.shape[0]
    row_scale = lax.rsqrt(lax.optimization_barrier(jnp.mean(residual * residual, -1, keepdims=True)) + EPS)
    normed = low(residual * row_scale * gain_in)
    proj_zx = low_back(jnp.einsum('ld,dkc->lkc', normed, w_zx, precision=PRECISE))
    proj_bcd = jnp.dot(normed, w_bcdt, precision=PRECISE)
    live_col = live_row[:, None]
    conv_out = low(jax.nn.silu(conv_taps(proj_zx[:, 1] * live_col, conv_x, doc_ids)))
    bc_out = low(jax.nn.silu(conv_taps(proj_bcd[:, :2 * state_count] * live_col, conv_bc, doc_ids)))
    steps_dt = jax.nn.softplus(proj_bcd[:, 2 * state_count:] + dt_bias) * live_col
    log_decay = -jnp.exp(a_log) * steps_dt
    cumulative = jnp.cumsum(log_decay, 0)
    heads_in = conv_out.reshape(length, head_count, -1)
    scores = jnp.dot(bc_out[:, state_count:], bc_out[:, :state_count].T, precision=PRECISE)
    places = jnp.arange(length)
    usable = (places[:, None] >= places[None, :]) & (doc_ids[:, None] == doc_ids[None, :])

    def one_head(head_args):
        cum_head, dt_head, in_head = head_args
        spread = cum_head[:, None] - cum_head[None, :]
        mixing = jnp.where(usable, jnp.exp(jnp.where(usable, spread, 0.0)), 0.0) * scores * dt_head[None, :]
        return jnp.dot(mixing, in_head, precision=PRECISE)
    mixed = lax.map(jax.checkpoint(one_head), (cumulative.T, steps_dt.T, heads_in.transpose(1, 0, 2)))
    outputs = mixed.transpose(1, 0, 2) + d_skip[:, None] * heads_in
    gated = outputs.reshape(length, -1) * jax.nn.silu(proj_zx[:, 0])
    inner_inv = lax.rsqrt(lax.optimization_barrier(jnp.mean(gated * gated, -1, keepdims=True)) + EPS)
    normed_out = low(gated * inner_inv * gain_inner)
    summed = residual + jnp.dot(normed_out, w_out, precision=PRECISE)
    if final_layer:
        return summed
    return low_back(low(summed))

def slot_apply(slot_args, weights, final_layer):
    return slot_layer(slot_args[0], slot_args[1], slot_args[2], weights, final_layer)

def reference(x_in, d_out, doc_lengths, token_mask, gain_in, w_zx, w_bcdt, conv_x, conv_bc, dt_bias, a_log, d_skip, gain_inner, w_out):
    weights = tuple((member.astype(jnp.float32) for member in (gain_in, w_zx, w_bcdt, conv_x, conv_bc, dt_bias, a_log, d_skip, gain_inner, w_out)))
    micro_count, length, slot_count, model_width = x_in.shape
    doc_ends = jnp.cumsum(doc_lengths, -1)
    places = jnp.arange(length, dtype=jnp.int32)
    doc_ids = lax.optimization_barrier(jnp.sum((places[None, None, :, None] >= doc_ends[:, :, None, :-1]).astype(jnp.int32), -1)).reshape(-1, length)
    live_rows = token_mask.transpose(0, 2, 1).astype(jnp.float32).reshape(-1, length)

    def forward(inputs, params):
        hidden = inputs.transpose(0, 2, 1, 3).reshape(micro_count * slot_count, length, model_width)
        for section_no in range(2):
            section_params = tuple((member[section_no] for member in params))
            run_slot = jax.checkpoint(partial(slot_apply, weights=section_params, final_layer=section_no == 1))
            hidden = lax.map(run_slot, (hidden, live_rows, doc_ids))
        return hidden.reshape(micro_count, slot_count, length, model_width).transpose(0, 2, 1, 3)
    result, pull_back = jax.vjp(forward, x_in.astype(jnp.float32), weights)
    grad_input, grad_weights = pull_back(d_out.astype(jnp.float32))
    return (result, grad_input, grad_weights[0], grad_weights[1], grad_weights[2], grad_weights[3], grad_weights[4], grad_weights[5], grad_weights[6], grad_weights[7], grad_weights[8], grad_weights[9])
```

```python
from functools import partial

import jax
import jax.numpy as jnp
from jax import lax
from jax.experimental import pallas as pl
from jax.experimental.pallas import tpu as pltpu
from jax.sharding import PartitionSpec as P

EPS = 1e-05
F32 = jnp.float32
BF16 = jnp.bfloat16
HEAD = 64
CHUNK = 128
LANES = 128
VMEM_LIMIT = 56 * 1024 * 1024
NN = (((1,), (0,)), ((), ()))
NT = (((1,), (1,)), ((), ()))
TN = (((0,), (0,)), ((), ()))


def mm(left, right, dims=NN):
    return lax.dot_general(left, right, dims, preferred_element_type=F32)


def sigmoid(value):
    return 0.5 * jnp.tanh(0.5 * value) + 0.5


def softplus(value):
    return jnp.maximum(value, 0.0) + jnp.log1p(jnp.exp(-jnp.abs(value)))


def iota(shape, dim):
    return lax.broadcasted_iota(jnp.int32, shape, dim)


def split_two(value):
    high = value.astype(BF16)
    return high, (value - high.astype(F32)).astype(BF16)


def split_three(value):
    high = value.astype(BF16)
    rest = value - high.astype(F32)
    mid = rest.astype(BF16)
    return high, mid, (rest - mid.astype(F32)).astype(BF16)


def fold_rows(value):
    rows = value.shape[0]
    return jnp.sum(value.reshape(rows // 8, 8, value.shape[1]), 0)


def doc_of(places, e0, e1):
    return (places >= e0).astype(jnp.int32) + (places >= e1).astype(jnp.int32)


def same_behind(places, steps, e0, e1):
    crossed = ((places >= e0) & (places < e0 + steps)) | ((places >= e1) & (places < e1 + steps))
    return jnp.where(crossed, 0.0, 1.0)


def same_ahead(places, steps, e0, e1):
    crossed = ((places < e0) & (places >= e0 - steps)) | ((places < e1) & (places >= e1 - steps))
    return jnp.where(crossed, 0.0, 1.0)


def chunk_decays(log_decay, tri):
    high, mid, low = split_three(log_decay)
    cum = mm(jnp.concatenate([tri, tri, tri], 1), jnp.concatenate([high, mid, low], 0))
    return cum, cum.T


def column(values, at):
    return jnp.broadcast_to(values[:, at : at + 1], (values.shape[0], LANES))


def conv_tile(ubuf, cp, tile, rows, masks):
    lanes = slice(tile * LANES, (tile + 1) * LANES)
    summed = cp[4:5, lanes] + cp[3:4, lanes] * ubuf[8 : 8 + rows, lanes]
    for steps in (1, 2, 3):
        shifted = ubuf[8 - steps : 8 - steps + rows, lanes] * masks[steps - 1]
        summed = summed + cp[3 - steps : 4 - steps, lanes] * shifted
    return summed


def fwd_kernel(with_dot, inner, state, sc, *refs):
    pieces = refs[:8]
    refs = refs[8:]
    if with_dot:
        w, cp, hp, chp, live, gno, nrm, proj, y_out, st, gn, gsend, stats, carry, ubuf, act = refs
    else:
        w, cp, hp, chp, live, nrm, proj, y_out, st, gn, gsend, stats, carry, ubuf, act = refs
    step = pl.program_id(0)
    sec, ten, e0, e1 = sc[0], sc[1], sc[2], sc[3]
    rows = nrm.shape[0]
    half = rows // 2
    wide = inner + 2 * state
    tiles = wide // LANES
    pairs = inner // LANES

    @pl.when(step == 0)
    def _():
        carry[...] = jnp.zeros_like(carry)
        ubuf[0:8, :] = jnp.zeros((8, wide), F32)

    rel = jnp.bitwise_xor(ten, step)
    mine = pl.multiple_of(sec * half, half)
    theirs = pl.multiple_of((1 - sec) * half, half)
    for k in range(4):

        @pl.when(rel == k)
        def _(k=k):
            nrm[pl.ds(mine, half), :] = pieces[k][...]
            nrm[pl.ds(theirs, half), :] = pieces[4 + k][...]

    proj[...] = mm(nrm[...], w[...])
    lv = live[...]
    places = rows * step + iota((rows, LANES), 0)
    masks = [same_behind(places, steps, e0, e1) for steps in (1, 2, 3)]
    for tile in range(tiles):
        lanes = slice(tile * LANES, (tile + 1) * LANES)
        at = slice(inner + tile * LANES, inner + (tile + 1) * LANES)
        u = proj[:, at] * lv
        proj[:, at] = u
        ubuf[8 : 8 + rows, lanes] = u
    for tile in range(tiles):
        lanes = slice(tile * LANES, (tile + 1) * LANES)
        pre = conv_tile(ubuf, cp, tile, rows, masks)
        act[:, lanes] = (pre * sigmoid(pre)).astype(BF16)
    ubuf[0:8, :] = ubuf[rows : rows + 8, :]

    low_half = iota((CHUNK, LANES), 1) < HEAD
    tri = (iota((CHUNK, CHUNK), 0) >= iota((CHUNK, CHUNK), 1)).astype(F32).astype(BF16)
    gated_sq = []
    gated_dot = []
    for c in range(rows // CHUNK):
        r0 = c * CHUNK
        at = slice(r0, r0 + CHUNK)
        base = rows * step + r0
        t_at = base + iota((CHUNK, CHUNK), 0)
        s_at = base + iota((CHUNK, CHUNK), 1)
        id_t = doc_of(t_at, e0, e1)
        usable = (t_at >= s_at) & (id_t == doc_of(s_at, e0, e1))
        id_prev = doc_of(base - 1, e0, e1)
        id_end = doc_of(base + CHUNK - 1, e0, e1)
        from_prev = jnp.where(id_t == id_prev, 1.0, 0.0)
        tail_same = jnp.where(id_t == id_end, 1.0, 0.0)
        linked = jnp.where(id_end == id_prev, 1.0, 0.0).astype(F32)
        dt = softplus(proj[at, inner + wide : inner + wide + LANES] + hp[0:1, :]) * live[at, :]
        cum, cum_t = chunk_decays(dt * hp[1:2, :], tri)
        b_in = act[at, inner : inner + state]
        c_in = act[at, inner + state : wide]
        scores = jnp.where(usable, mm(c_in, b_in, NT), 0.0)
        sq = jnp.zeros((CHUNK, LANES), F32)
        rd = jnp.zeros((CHUNK, LANES), F32)
        for k in range(pairs):
            lanes = slice(k * LANES, (k + 1) * LANES)
            mixed, cums = [], []
            for h in (2 * k, 2 * k + 1):
                cum_col = column(cum, h)
                cums.append(cum_col)
                decay = jnp.exp(jnp.minimum(cum_col - cum_t[h : h + 1, :], 0.0))
                mixed.append((decay * scores).astype(BF16))
            cum_e = jnp.where(low_half, cums[0], cums[1])
            dt_e = jnp.where(low_half, column(dt, 2 * k), column(dt, 2 * k + 1))
            x_in = act[at, lanes].astype(F32)
            xdt = x_in * dt_e
            both = jnp.concatenate([jnp.where(low_half, xdt, 0.0), jnp.where(low_half, 0.0, xdt)], 0)
            within = mm(jnp.concatenate(mixed, 1), both.astype(BF16))
            old = carry[:, lanes]
            old_low = old.astype(BF16)
            st[c, :, lanes] = old_low
            across = mm(c_in, old_low) * (jnp.exp(cum_e) * from_prev)
            cum_end = cum_e[CHUNK - 1 : CHUNK, :]
            to_end = jnp.exp(cum_end - cum_e) * tail_same
            added = mm(b_in, (xdt * to_end).astype(BF16), TN)
            carry[:, lanes] = old * (jnp.exp(cum_end) * linked) + added
            y = within + across + chp[0:1, lanes] * x_in
            y_out[at, lanes] = y
            gate = proj[at, lanes]
            gated = y * (gate * sigmoid(gate))
            scaled = gated * chp[1:2, lanes]
            gn[at, lanes] = scaled.astype(BF16)
            sq = sq + gated * gated
            if with_dot:
                rd = rd + scaled * gno[at, lanes]
        gated_sq.append(sq)
        gated_dot.append(rd)
    ones = jnp.ones((8, LANES), F32)
    exact = partial(
        lax.dot_general,
        dimension_numbers=NT,
        precision=lax.Precision.HIGHEST,
        preferred_element_type=F32,
    )
    total = exact(ones, jnp.concatenate(gated_sq, 0))
    if with_dot:
        dots = exact(ones, jnp.concatenate(gated_dot, 0))
        total = jnp.where(iota((8, rows), 0) == 0, total, dots)
    stats[...] = total
    gsend[0] = gn[pl.ds(theirs, half), :]


def run_fwd(scalars, pieces, w, cp, hp, chp, live, gno, inner, state):
    half, width = pieces[0].shape
    rows = 2 * half
    length = live.shape[0]
    steps = length // rows
    cols = w.shape[1]
    chunks = rows // CHUNK
    whole = lambda shape: pl.BlockSpec(shape, lambda i, sc: (0,) * len(shape))
    by_row = lambda n: pl.BlockSpec((rows, n), lambda i, sc: (i, 0))
    in_specs = [whole((half, width))] * 8 + [
        whole(w.shape),
        whole(cp.shape),
        whole(hp.shape),
        whole(chp.shape),
        by_row(LANES),
    ]
    operands = [*pieces, w, cp, hp, chp, live]
    if gno is not None:
        in_specs.append(by_row(inner))
        operands.append(gno)
    flops = 2 * length * width * cols + 2 * length * inner * CHUNK * 6
    return pl.pallas_call(
        partial(fwd_kernel, gno is not None, inner, state),
        out_shape=(
            jax.ShapeDtypeStruct((length, width), BF16),
            jax.ShapeDtypeStruct((length, cols), F32),
            jax.ShapeDtypeStruct((length, inner), F32),
            jax.ShapeDtypeStruct((length // CHUNK, state, inner), BF16),
            jax.ShapeDtypeStruct((length, inner), BF16),
            jax.ShapeDtypeStruct((steps, half, inner), BF16),
            jax.ShapeDtypeStruct((8, length), F32),
        ),
        grid_spec=pltpu.PrefetchScalarGridSpec(
            num_scalar_prefetch=1,
            grid=(steps,),
            in_specs=in_specs,
            out_specs=(
                by_row(width),
                by_row(cols),
                by_row(inner),
                pl.BlockSpec((chunks, state, inner), lambda i, sc: (i, 0, 0)),
                by_row(inner),
                pl.BlockSpec((1, half, inner), lambda i, sc: (i, 0, 0)),
                pl.BlockSpec((8, rows), lambda i, sc: (0, i)),
            ),
            scratch_shapes=[
                pltpu.VMEM((state, inner), F32),
                pltpu.VMEM((rows + 8, inner + 2 * state), F32),
                pltpu.VMEM((rows, inner + 2 * state), BF16),
            ],
        ),
        compiler_params=pltpu.CompilerParams(
            dimension_semantics=("arbitrary",), vmem_limit_bytes=VMEM_LIMIT
        ),
        cost_estimate=pl.CostEstimate(
            flops=2 * flops, transcendentals=length * inner * 8, bytes_accessed=24 * 1024 * 1024
        ),
        name="layer_fwd",
    )(scalars, *operands)


def bwd_kernel(inner, state, total_inner, sc, *refs):
    gno, proj, halo, y_in, st, rc, live, cp, hp, chp = refs[:10]
    gz, gzsend, no_out, gcp, ghp, gch = refs[10:16]
    dstate, ubuf, gbuf, acc_c, acc_h, acc_n, acc_d = refs[16:]
    step = pl.program_id(0)
    steps = pl.num_programs(0)
    block = steps - 1 - step
    sec, e0, e1 = sc[0], sc[2], sc[3]
    rows = y_in.shape[0]
    half = rows // 2
    wide = inner + 2 * state
    tiles = wide // LANES
    pairs = inner // LANES
    theirs = pl.multiple_of((1 - sec) * half, half)

    @pl.when(step == 0)
    def _():
        dstate[...] = jnp.zeros_like(dstate)
        gbuf[rows : rows + 8, :] = jnp.zeros((8, wide), F32)
        acc_c[...] = jnp.zeros_like(acc_c)
        acc_h[...] = jnp.zeros_like(acc_h)
        acc_n[...] = jnp.zeros_like(acc_n)
        acc_d[...] = jnp.zeros_like(acc_d)

    ubuf[0:8, :] = jnp.where(block == 0, 0.0, halo[:, inner : inner + wide])
    ubuf[8 : 8 + rows, :] = proj[:, inner : inner + wide]
    places = rows * block + iota((rows, LANES), 0)
    masks = [same_behind(places, steps_, e0, e1) for steps_ in (1, 2, 3)]

    low_half = iota((CHUNK, LANES), 1) < HEAD
    row_at = iota((CHUNK, CHUNK), 0)
    col_at = iota((CHUNK, CHUNK), 1)
    tri = (row_at >= col_at).astype(F32).astype(BF16)
    tri_rev = (row_at <= col_at).astype(F32).astype(BF16)
    tri_strict = (row_at > col_at).astype(F32).astype(BF16)
    sums = jnp.concatenate([tri_rev, tri_rev, tri_strict, tri_strict], 1)
    to_head = [
        (iota((LANES, LANES), 1) == 2 * k + (iota((LANES, LANES), 0) >= HEAD).astype(jnp.int32))
        .astype(F32)
        .astype(BF16)
        for k in range(pairs)
    ]

    for c in reversed(range(rows // CHUNK)):
        r0 = c * CHUNK
        at = slice(r0, r0 + CHUNK)
        cmasks = [m[at, :] for m in masks]
        acts, slopes = [], []
        for tile in range(tiles):
            lanes = slice(tile * LANES, (tile + 1) * LANES)
            pre = cp[4:5, lanes] + cp[3:4, lanes] * ubuf[8 + r0 : 8 + r0 + CHUNK, lanes]
            for n in (1, 2, 3):
                shifted = ubuf[8 + r0 - n : 8 + r0 - n + CHUNK, lanes] * cmasks[n - 1]
                pre = pre + cp[3 - n : 4 - n, lanes] * shifted
            sig = sigmoid(pre)
            acts.append((pre * sig).astype(BF16))
            slopes.append(sig * (1.0 + pre * (1.0 - sig)))
        b_in, c_in = acts[pairs], acts[pairs + 1]
        base = rows * block + r0
        id_s = doc_of(base + row_at, e0, e1)
        usable = (row_at <= col_at) & (id_s == doc_of(base + col_at, e0, e1))
        id_prev = doc_of(base - 1, e0, e1)
        id_end = doc_of(base + CHUNK - 1, e0, e1)
        from_prev = jnp.where(id_s == id_prev, 1.0, 0.0)
        tail_same = jnp.where(id_s == id_end, 1.0, 0.0)
        linked = jnp.where(id_end == id_prev, 1.0, 0.0).astype(F32)
        lv = live[at, :]
        dt_in = proj[at, inner + wide : inner + wide + LANES] + hp[0:1, :]
        dt = softplus(dt_in) * lv
        log_decay = dt * hp[1:2, :]
        cum, cum_t = chunk_decays(log_decay, tri)
        scores = jnp.where(usable, mm(b_in, c_in, NT), 0.0)
        inv = column(rc[at, :], 0)
        coef = column(rc[at, :], 1)
        d_scores = jnp.zeros((CHUNK, CHUNK), F32)
        gb = jnp.zeros((CHUNK, state), F32)
        gc = jnp.zeros((CHUNK, state), F32)
        r1 = jnp.zeros((CHUNK, LANES), F32)
        r2 = jnp.zeros((CHUNK, LANES), F32)
        r3 = jnp.zeros((CHUNK, LANES), F32)
        kept = jnp.zeros((8, LANES), F32)
        for k in range(pairs):
            lanes = slice(k * LANES, (k + 1) * LANES)
            gate = proj[at, lanes]
            sig = sigmoid(gate)
            silu = gate * sig
            y = y_in[at, lanes]
            gated = y * silu
            g_no = gno[at, lanes]
            gain = chp[1:2, lanes]
            skip = chp[0:1, lanes]
            scaled = gated * inv
            acc_n[:, lanes] += fold_rows(g_no * scaled)
            no_out[at, lanes] = (scaled * gain).astype(BF16)
            gg = inv * (g_no * gain) - gated * coef
            gy = gg * silu
            gz[at, lanes] = (gg * y * (sig * (1.0 + gate * (1.0 - sig)))).astype(BF16)
            x_in = acts[k].astype(F32)
            acc_d[:, lanes] += fold_rows(gy * x_in)
            dt_e = jnp.where(low_half, column(dt, 2 * k), column(dt, 2 * k + 1))
            gy_b = gy.astype(BF16)
            gy_f = gy_b.astype(F32)
            xdt_b = (x_in * dt_e).astype(BF16)
            xdt_f = xdt_b.astype(F32)
            gy_halves = [jnp.where(low_half, gy_f, 0.0).astype(BF16), jnp.where(low_half, 0.0, gy_f).astype(BF16)]
            mixed, cums = [], []
            for n in (0, 1):
                h = 2 * k + n
                cum_col = column(cum, h)
                cums.append(cum_col)
                decay = jnp.exp(jnp.minimum(cum_t[h : h + 1, :] - cum_col, 0.0))
                mixed.append((decay * scores).astype(BF16))
                d_scores = d_scores + decay * mm(xdt_b, gy_halves[n], NT)
            cum_e = jnp.where(low_half, cums[0], cums[1])
            gx_in = mm(jnp.concatenate(mixed, 1), jnp.concatenate(gy_halves, 0))
            cum_end = cum_e[CHUNK - 1 : CHUNK, :]
            to_end = jnp.exp(cum_end - cum_e) * tail_same
            entering = jnp.exp(cum_e) * from_prev
            s_in = st[c, :, lanes]
            d_out = dstate[:, lanes]
            d_out_b = d_out.astype(BF16)
            gx_st = mm(b_in, d_out_b) * to_end
            gb = gb + mm((xdt_f * to_end).astype(BF16), d_out_b, NT)
            gye = (gy * entering).astype(BF16)
            gc = gc + mm(gye, s_in, NT)
            dec = jnp.exp(cum_end) * linked
            prod = fold_rows(s_in.astype(F32) * d_out) * dec
            p_hi, p_lo = split_two(prod)
            kept = kept + mm(p_hi, to_head[k]) + mm(p_lo, to_head[k])
            dstate[:, lanes] = d_out * dec + mm(c_in, gye, TN)
            gx = gx_in + gx_st
            t_hi, t_lo = split_two(gy_f * (y - skip * x_in) - xdt_f * gx_in)
            pair2 = jnp.concatenate([to_head[k], to_head[k]], 0)
            r1 = r1 + mm(jnp.concatenate([t_hi, t_lo], 1), pair2)
            t_hi, t_lo = split_two(x_in * gx)
            r2 = r2 + mm(jnp.concatenate([t_hi, t_lo], 1), pair2)
            t_hi, t_lo = split_two(x_in * gx_st)
            r3 = r3 + mm(jnp.concatenate([t_hi, t_lo], 1), pair2)
            gbuf[at, lanes] = (gx * dt_e + gy * skip) * slopes[k]
        d_scores = jnp.where(usable, d_scores, 0.0).astype(BF16)
        gb = gb + mm(d_scores, c_in)
        gc = gc + mm(d_scores, b_in, TN)
        for n in range(state // LANES):
            b_at = slice(inner + n * LANES, inner + (n + 1) * LANES)
            c_at = slice(inner + state + n * LANES, inner + state + (n + 1) * LANES)
            gbuf[at, b_at] = gb * slopes[pairs]
            gbuf[at, c_at] = gc * slopes[pairs + 1]
        a_hi, a_lo = split_two(r1)
        b_hi, b_lo = split_two(dt * r3)
        g_ld = mm(sums, jnp.concatenate([a_hi, a_lo, b_hi, b_lo], 0)) + jnp.sum(kept, 0, keepdims=True)
        g_dt = (r2 + g_ld * hp[1:2, :]) * (sigmoid(dt_in) * lv)
        acc_h[0:8, :] += fold_rows(g_dt)
        acc_h[8:16, :] += fold_rows(g_ld * log_decay)
        gz[at, inner + wide : inner + wide + LANES] = g_dt.astype(BF16)

    ahead = [same_ahead(places, n, e0, e1) for n in (1, 2, 3)]
    lv = live[...]
    for tile in range(tiles):
        lanes = slice(tile * LANES, (tile + 1) * LANES)
        gp = gbuf[0:rows, lanes]
        gu = cp[3:4, lanes] * gp
        acc_c[24:32, lanes] += fold_rows(gp * ubuf[8 : 8 + rows, lanes])
        acc_c[32:40, lanes] += fold_rows(gp)
        for n in (1, 2, 3):
            gu = gu + cp[3 - n : 4 - n, lanes] * (gbuf[n : n + rows, lanes] * ahead[n - 1])
            shifted = ubuf[8 - n : 8 - n + rows, lanes] * masks[n - 1]
            acc_c[8 * (3 - n) : 8 * (4 - n), lanes] += fold_rows(gp * shifted)
        at = slice(inner + tile * LANES, inner + (tile + 1) * LANES)
        gz[:, at] = (gu * lv).astype(BF16)
    gbuf[rows : rows + 8, :] = gbuf[0:8, :]
    gzsend[0] = gz[pl.ds(theirs, half), :]

    @pl.when(step == steps - 1)
    def _():
        gcp[...] = jnp.zeros_like(gcp)
        ghp[...] = jnp.zeros_like(ghp)
        gch[...] = jnp.zeros_like(gch)
        for n in range(5):
            gcp[n : n + 1, :] = jnp.sum(acc_c[8 * n : 8 * n + 8, :], 0, keepdims=True)
        for n in range(2):
            ghp[n : n + 1, :] = jnp.sum(acc_h[8 * n : 8 * n + 8, :], 0, keepdims=True)
        gch[0:1, :] = jnp.sum(acc_n[...], 0, keepdims=True)
        gch[1:2, :] = jnp.sum(acc_d[...], 0, keepdims=True)


def run_bwd(scalars, gno, proj, y, st, rc, live, cp, hp, chp, inner, state, rows):
    length, cols = proj.shape
    steps = length // rows
    half = rows // 2
    chunks = rows // CHUNK
    wide = inner + 2 * state
    whole = lambda shape: pl.BlockSpec(shape, lambda i, sc: (0,) * len(shape))
    by_row = lambda n: pl.BlockSpec((rows, n), lambda i, sc: (steps - 1 - i, 0))
    flops = 2 * length * inner * CHUNK * 24
    return pl.pallas_call(
        partial(bwd_kernel, inner, state, 0),
        out_shape=(
            jax.ShapeDtypeStruct((length, cols), BF16),
            jax.ShapeDtypeStruct((steps, half, cols), BF16),
            jax.ShapeDtypeStruct((length, inner), BF16),
            jax.ShapeDtypeStruct((8, wide), F32),
            jax.ShapeDtypeStruct((8, LANES), F32),
            jax.ShapeDtypeStruct((8, inner), F32),
        ),
        grid_spec=pltpu.PrefetchScalarGridSpec(
            num_scalar_prefetch=1,
            grid=(steps,),
            in_specs=[
                by_row(inner),
                by_row(cols),
                pl.BlockSpec(
                    (8, cols),
                    lambda i, sc: (jnp.maximum((steps - 1 - i) * (rows // 8) - 1, 0), 0),
                ),
                by_row(inner),
                pl.BlockSpec((chunks, state, inner), lambda i, sc: (steps - 1 - i, 0, 0)),
                by_row(LANES),
                by_row(LANES),
                whole(cp.shape),
                whole(hp.shape),
                whole(chp.shape),
            ],
            out_specs=(
                by_row(cols),
                pl.BlockSpec((1, half, cols), lambda i, sc: (steps - 1 - i, 0, 0)),
                by_row(inner),
                whole((8, wide)),
                whole((8, LANES)),
                whole((8, inner)),
            ),
            scratch_shapes=[
                pltpu.VMEM((state, inner), F32),
                pltpu.VMEM((rows + 8, wide), F32),
                pltpu.VMEM((rows + 8, wide), F32),
                pltpu.VMEM((40, wide), F32),
                pltpu.VMEM((16, LANES), F32),
                pltpu.VMEM((8, inner), F32),
                pltpu.VMEM((8, inner), F32),
            ],
        ),
        compiler_params=pltpu.CompilerParams(
            dimension_semantics=("arbitrary",), vmem_limit_bytes=VMEM_LIMIT
        ),
        cost_estimate=pl.CostEstimate(
            flops=8 * flops, transcendentals=length * inner * 12, bytes_accessed=24 * 1024 * 1024
        ),
        name="layer_bwd",
    )(scalars, gno, proj, proj, y, st, rc, live, cp, hp, chp)


def gn_kernel(with_rc, sc, *refs):
    pieces = refs[:8]
    refs = refs[8:]
    if with_rc:
        rcs, (w, gno, gout, rc) = refs[:8], refs[8:]
    else:
        w, gno, gout = refs
    sec, ten = sc[0], sc[1]
    half = gout.shape[0] // 2
    rel = jnp.bitwise_xor(ten, pl.program_id(0))
    mine = pl.multiple_of(sec * half, half)
    theirs = pl.multiple_of((1 - sec) * half, half)
    for k in range(4):

        @pl.when(rel == k)
        def _(k=k):
            gout[pl.ds(mine, half), :] = pieces[k][...]
            gout[pl.ds(theirs, half), :] = pieces[4 + k][...]
            if with_rc:
                rc[pl.ds(mine, half), :] = rcs[k][...]
                rc[pl.ds(theirs, half), :] = rcs[4 + k][...]

    gno[...] = mm(gout[...], w[...], NT)


def run_gn(scalars, pieces, w, rcs):
    half, width = pieces[0].shape
    inner = w.shape[0]
    rows, length = 2 * half, 8 * half
    whole = lambda shape: pl.BlockSpec(shape, lambda i, sc: (0,) * len(shape))
    by_row = lambda n: pl.BlockSpec((rows, n), lambda i, sc: (i, 0))
    in_specs = [whole((half, width))] * 8
    operands = list(pieces)
    outs = [
        jax.ShapeDtypeStruct((length, inner), F32),
        jax.ShapeDtypeStruct((length, width), BF16),
    ]
    out_specs = [by_row(inner), by_row(width)]
    if rcs is not None:
        in_specs += [whole((half, LANES))] * 8
        operands += list(rcs)
        outs.append(jax.ShapeDtypeStruct((length, LANES), F32))
        out_specs.append(by_row(LANES))
    return pl.pallas_call(
        partial(gn_kernel, rcs is not None),
        out_shape=tuple(outs),
        grid_spec=pltpu.PrefetchScalarGridSpec(
            num_scalar_prefetch=1,
            grid=(length // rows,),
            in_specs=in_specs + [whole(w.shape)],
            out_specs=tuple(out_specs),
        ),
        compiler_params=pltpu.CompilerParams(
            dimension_semantics=("arbitrary",), vmem_limit_bytes=VMEM_LIMIT
        ),
        cost_estimate=pl.CostEstimate(
            flops=2 * length * width * inner, transcendentals=0, bytes_accessed=13 * 1024 * 1024
        ),
        name="grad_rows",
    )(scalars, *operands, w)


def half_kernel(dims, sc, kept, got, wa, wb, *outs):
    total = mm(kept[...], wa[...], dims) + mm(got[0], wb[...], dims)
    for k in range(4):

        @pl.when(pl.program_id(0) == k)
        def _(k=k):
            outs[k][...] = total.astype(BF16)


def run_half(scalars, full, got, wa, wb, dims):
    groups, half, depth = got.shape
    width = wa.shape[1] if dims == NN else wa.shape[0]
    whole = lambda shape: pl.BlockSpec(shape, lambda i, sc: (0,) * len(shape))
    return pl.pallas_call(
        partial(half_kernel, dims),
        out_shape=(jax.ShapeDtypeStruct((half, width), BF16),) * 4,
        grid_spec=pltpu.PrefetchScalarGridSpec(
            num_scalar_prefetch=1,
            grid=(groups,),
            in_specs=[
                pl.BlockSpec(
                    (half, depth), lambda i, sc: (2 * jnp.bitwise_xor(sc[1], i) + sc[0], 0)
                ),
                pl.BlockSpec((1, half, depth), lambda i, sc: (jnp.bitwise_xor(sc[1], i), 0, 0)),
                whole(wa.shape),
                whole(wb.shape),
            ],
            out_specs=(whole((half, width)),) * 4,
        ),
        compiler_params=pltpu.CompilerParams(
            dimension_semantics=("arbitrary",), vmem_limit_bytes=VMEM_LIMIT
        ),
        cost_estimate=pl.CostEstimate(
            flops=4 * groups * half * depth * width, transcendentals=0, bytes_accessed=8 * 1024 * 1024
        ),
        name="half_rows",
    )(scalars, full, got, wa, wb)


def norm_kernel(x, gain, out):
    v = x[...].astype(F32)
    inv = lax.rsqrt(jnp.mean(v * v, -1, keepdims=True) + EPS)
    out[...] = (v * inv * gain[0:1, :]).astype(BF16)


def owner_kernel(final, u0, u1, u2, u3, x, rcol, gain, *outs):
    total = (u0[...].astype(F32) + u1[...].astype(F32)) + (u2[...].astype(F32) + u3[...].astype(F32))
    out = x[...].astype(F32) + rcol[:, 0:1] * total
    if final:
        outs[0][...] = out
        return
    h1, normed, kept = outs
    low = out.astype(BF16)
    h1[...] = low
    kept[...] = total
    v = low.astype(F32)
    inv = lax.rsqrt(jnp.mean(v * v, -1, keepdims=True) + EPS)
    normed[...] = (v * inv * gain[0:1, :]).astype(BF16)


def owner_back_kernel(last, inner_width, g0, g1, g2, g3, v_in, g_in, gain, *refs):
    g = (g0[...].astype(F32) + g1[...].astype(F32)) + (g2[...].astype(F32) + g3[...].astype(F32))
    v = v_in[...].astype(F32)
    inv = lax.rsqrt(jnp.mean(v * v, -1, keepdims=True) + EPS)
    scaled = v * inv
    p = g * gain[0:1, :]
    out = g_in[...].astype(F32) + inv * (p - scaled * jnp.mean(p * scaled, -1, keepdims=True))
    if last:
        g_v, ggain = refs
        g_v[...] = out
    else:
        kept, rcol, g_v, rc, ggain = refs
        low = out.astype(BF16)
        g_v[...] = low
        r = rcol[:, 0:1]
        dot = jnp.sum(low.astype(F32) * kept[...], -1, keepdims=True)
        coef = r * r * r * dot / inner_width
        lane = iota(rc.shape, 1)
        rc[...] = jnp.where(lane == 0, r, coef)
    ggain[...] = fold_rows(g * scaled)


def run_plain(kernel, name, out_shape, *operands):
    return pl.pallas_call(
        kernel,
        out_shape=out_shape,
        compiler_params=pltpu.CompilerParams(vmem_limit_bytes=VMEM_LIMIT),
        cost_estimate=pl.CostEstimate(
            flops=8 * 1024 * 1024, transcendentals=0, bytes_accessed=4 * 1024 * 1024
        ),
        name=name,
    )(*operands)


def across(value, step):
    count = lax.axis_size("tensor")
    return lax.ppermute(value, "tensor", [(i, i ^ step) for i in range(count)])


def swap(value):
    return lax.ppermute(value, "section", [(0, 1), (1, 0)])


def give(value, layer):
    return lax.ppermute(value, "section", [(1 - layer, layer)])


def spread(value):
    same = [value] + [across(value, k) for k in (1, 2, 3)]
    return same + [swap(piece) for piece in same]


def all_tensor(value):
    return value + across(value, 1) + across(value, 2) + across(value, 3)


def gather_dp(value, axis):
    count = lax.axis_size("dp")
    if count != 4:
        return lax.all_gather(value, "dp", axis=axis, tiled=True)
    up, down = [value], [value]
    for _ in range(3):
        up.append(lax.ppermute(up[-1], "dp", [(i, i + 1) for i in range(3)]))
        down.append(lax.ppermute(down[-1], "dp", [(i + 1, i) for i in range(3)]))
    at = lax.axis_index("dp")
    shards = []
    for j in range(4):
        shards.append(lax.select_n(at, *[up[i - j] if j <= i else down[j - i] for i in range(4)]))
    return jnp.concatenate(shards, axis)


def scatter_dp(value, axis):
    count = lax.axis_size("dp")
    if count != 4:
        return lax.psum_scatter(value, "dp", scatter_dimension=axis, tiled=True)
    at = lax.axis_index("dp")
    size = value.shape[axis] // 4
    total = lax.dynamic_slice_in_dim(value, at * size, size, axis)
    low = value.astype(BF16)
    for k in (1, 2, 3):
        part = lax.dynamic_slice_in_dim(low, ((at + k) % 4) * size, size, axis)
        got = lax.ppermute(part, "dp", [(i, (i + k) % 4) for i in range(4)])
        total = total + got.astype(F32)
    return total


def sum_dp(value):
    if lax.axis_size("dp") != 4:
        return lax.psum(value, "dp")
    total = value
    for k in (1, 2, 3):
        total = total + lax.ppermute(value, "dp", [(i, (i + k) % 4) for i in range(4)])
    return total


def on_device(
    x_in,
    d_out,
    doc_lengths,
    token_mask,
    gain_in,
    w_zx,
    w_bcdt,
    conv_x,
    conv_bc,
    dt_bias,
    a_log,
    d_skip,
    gain_inner,
    w_out,
):
    micro_count, local_rows, _, width = x_in.shape
    length = token_mask.shape[1]
    half = local_rows // 2
    inner = conv_x.shape[2] // 2
    heads = dt_bias.shape[1] // 2
    state = conv_bc.shape[2] // 2
    chip_inner = 2 * inner
    full_inner = chip_inner * lax.axis_size("tensor")
    full_heads = w_bcdt.shape[2] - 2 * state
    sec = lax.axis_index("section")
    ten = lax.axis_index("tensor")
    first = sec == 0
    micros = range(micro_count)

    def by_layer(own, other):
        return [jnp.where(first, own, other), jnp.where(first, other, own)]

    pad_to = lambda v, n: jnp.pad(v, ((0, 0), (0, n - v.shape[1])))
    pack = jnp.concatenate(
        [
            gain_in,
            pad_to(jnp.concatenate([conv_x[0], conv_bc[0]], 1), width),
            pad_to(gain_inner, width),
            pad_to(jnp.concatenate([dt_bias, a_log, d_skip], 1), width),
        ],
        0,
    )
    packs = by_layer(pack, swap(pack))

    zx = w_zx[0].reshape(w_zx.shape[1], 2, 2, inner)
    zx_own = lax.dynamic_index_in_dim(zx, sec, 2, keepdims=False).reshape(-1, 2 * inner)
    zx_send = lax.dynamic_index_in_dim(zx, 1 - sec, 2, keepdims=False).reshape(-1, 2 * inner)
    zx_shards = by_layer(zx_own, swap(zx_send))
    wo = w_out[0].reshape(2, inner, w_out.shape[2])
    wo_own = lax.dynamic_index_in_dim(wo, sec, 0, keepdims=False)
    wo_send = lax.dynamic_index_in_dim(wo, 1 - sec, 0, keepdims=False)
    wo_shards = by_layer(wo_own, swap(wo_send))
    zx_full, wo_full = [None, None], [None, None]
    zx_full[0] = gather_dp(zx_shards[0], 0)
    bcdt = gather_dp(w_bcdt[0], 0)
    bcdts = by_layer(bcdt, swap(bcdt))
    wo_full[0] = gather_dp(wo_shards[0], 1)
    zx_full[1] = gather_dp(zx_shards[1], 0)
    wo_full[1] = gather_dp(wo_shards[1], 1)

    def head_pick(core):
        row = lax.broadcasted_iota(jnp.int32, (full_heads, LANES), 0)
        col = lax.broadcasted_iota(jnp.int32, (full_heads, LANES), 1)
        return ((row == ten * 2 * heads + core * heads + col) & (col < heads)).astype(F32)

    layers = []
    for layer in range(2):
        bc = bcdts[layer][:, : 2 * state]
        dts = bcdts[layer][:, 2 * state :]
        pick = lambda core: jnp.dot(dts, head_pick(core).astype(BF16), preferred_element_type=BF16)
        w = jnp.concatenate([zx_full[layer], bc, pick(sec)], 1)
        w_other = jnp.concatenate([swap(zx_full[layer]), bc, pick(1 - sec)], 1)
        p = packs[layer]
        lane = lambda row, start, count: lax.dynamic_slice(p, (row, start), (1, count))
        taps = jnp.concatenate(
            [lax.dynamic_slice(p, (1, sec * inner), (5, inner)), p[1:6, chip_inner : chip_inner + 2 * state]], 1
        )
        cp = jnp.pad(taps, ((0, 3), (0, 0)))
        bias = pad_to(lane(7, sec * heads, heads), LANES)
        rate = pad_to(-jnp.exp(lane(7, 2 * heads + sec * heads, heads)), LANES)
        hp = jnp.concatenate([bias, rate, jnp.zeros((6, LANES), F32)], 0)
        skip = jnp.broadcast_to(
            lane(7, 4 * heads + sec * heads, heads).reshape(heads, 1), (heads, HEAD)
        ).reshape(1, inner)
        chp = jnp.concatenate([skip, lane(6, sec * inner, inner), jnp.zeros((6, inner), F32)], 0)
        gain = jnp.broadcast_to(p[0:1], (8, width))
        layers.append(
            dict(w=w, w_other=w_other, wo=wo_full[layer], wo_other=swap(wo_full[layer]), cp=cp, hp=hp, chp=chp, gain=gain)
        )

    rows_at = lambda v, m: lax.dynamic_slice_in_dim(v[m, :, 0, :], sec * half, half, 0)
    lane0 = lax.broadcasted_iota(jnp.int32, (1, LANES), 1) == 0
    wide = lambda kind, n=1: jax.ShapeDtypeStruct((n * half, width), kind)
    small = jax.ShapeDtypeStruct((8, width), F32)

    scalars, lives, xs, gs = [], [], [], []
    for m in micros:
        e0 = doc_lengths[m, 0, 0]
        e1 = e0 + doc_lengths[m, 0, 1]
        scalars.append(jnp.stack([sec, ten, e0, e1]).astype(jnp.int32))
        lives.append(jnp.broadcast_to(token_mask[m].astype(F32), (length, LANES)))
        xs.append(rows_at(x_in, m))
        gs.append(rows_at(d_out, m))

    def forward(layer, m, pieces, gno):
        k = layers[layer]
        nrm, proj, y, st, gn, gsend, stats = run_fwd(
            scalars[m], pieces, k["w"], k["cp"], k["hp"], k["chp"], lives[m], gno, inner, state
        )
        got = swap(gsend)
        part = stats + swap(stats)
        totals = all_tensor(part)
        inv = lax.rsqrt(totals[0] / full_inner + EPS)
        rcol = jnp.broadcast_to(
            lax.dynamic_slice_in_dim(inv, ten * 2 * half + sec * half, half)[:, None], (half, LANES)
        )
        outs = run_half(scalars[m], gn, got, k["wo"], k["wo_other"], NN)
        parts = [outs[0]] + [across(outs[n], n) for n in (1, 2, 3)]
        return dict(nrm=nrm, proj=proj, y=y, st=st, totals=totals, inv=inv, rcol=rcol, parts=parts)

    def backward(layer, m, gno, rc, kept):
        k = layers[layer]
        gz, gzsend, no, gcp, ghp, gch = run_bwd(
            scalars[m], gno, kept["proj"], kept["y"], kept["st"], rc, lives[m],
            k["cp"], k["hp"], k["chp"], inner, state, 2 * half,
        )
        outs = run_half(scalars[m], gz, swap(gzsend), k["w"], k["w_other"], NT)
        parts = [outs[0]] + [across(outs[n], n) for n in (1, 2, 3)]
        return parts, gz, no, (gcp, ghp, gch)

    normed0 = [
        run_plain(norm_kernel, "norm_rows", wide(BF16), xs[m], layers[0]["gain"]) for m in micros
    ]
    pieces0 = [spread(v) for v in normed0]
    kept0 = [forward(0, m, pieces0[m], None) for m in micros]
    grad_pieces1 = [spread(g) for g in gs]
    h1, pieces1, u0 = [], [], []
    for m in micros:
        h, normed, total = run_plain(
            partial(owner_kernel, False), "owner_mid", (wide(BF16), wide(BF16), wide(F32)),
            *kept0[m]["parts"], xs[m], kept0[m]["rcol"], layers[1]["gain"],
        )
        h1.append(h)
        u0.append(total)
        pieces1.append(spread(normed))
    rows1 = [run_gn(scalars[m], grad_pieces1[m], layers[1]["wo"], None) for m in micros]
    kept1 = [forward(1, m, pieces1[m], rows1[m][0]) for m in micros]

    weight_grads = [[], []]
    small_grads = [[], []]

    def weigh(layer, m, kept, gz, no, gout):
        weight_grads[layer].append(
            (mm(kept["nrm"], gz, TN), mm(no, gout, TN))
        )

    grad_rows, rcs0, gain_grads = [], [], [[], []]
    for m in micros:
        kept = kept1[m]
        coef = kept["inv"] ** 3 * kept["totals"][1] / full_inner
        rc = jnp.where(lane0, kept["inv"][:, None], coef[:, None])
        parts, gz, no, tiny = backward(1, m, rows1[m][0], rc, kept)
        g_h1, rc0, ggain = run_plain(
            partial(owner_back_kernel, False, full_inner), "owner_back",
            (wide(BF16), jax.ShapeDtypeStruct((half, LANES), F32), small),
            *parts, h1[m], gs[m], layers[1]["gain"], u0[m], kept0[m]["rcol"],
        )
        grad_rows.append(g_h1)
        rcs0.append(rc0)
        gain_grads[1].append(ggain)
        small_grads[1].append(tiny)
        weigh(1, m, kept, gz, no, rows1[m][1])
    rows0 = [
        run_gn(scalars[m], spread(grad_rows[m]), layers[0]["wo"], spread(rcs0[m])) for m in micros
    ]
    grads_in = []
    for m in micros:
        parts, gz, no, tiny = backward(0, m, rows0[m][0], rows0[m][2], kept0[m])
        g_v, ggain = run_plain(
            partial(owner_back_kernel, True, full_inner), "owner_last", (wide(F32), small),
            *parts, xs[m], grad_rows[m], layers[0]["gain"],
        )
        grads_in.append(g_v)
        gain_grads[0].append(ggain)
        small_grads[0].append(tiny)
        weigh(0, m, kept0[m], gz, no, rows0[m][1])

    finals = []
    for m in micros:
        out = run_plain(
            partial(owner_kernel, True), "owner_out", wide(F32),
            *kept1[m]["parts"], h1[m], kept1[m]["rcol"], layers[1]["gain"],
        )
        finals.append(jnp.concatenate(by_layer(out, swap(out)), 0))
    out_act = jnp.stack(finals)[:, :, None, :]

    halves = []
    for m in micros:
        cols = grads_in[m].reshape(half, 2, width // 2)
        mine = lax.dynamic_index_in_dim(cols, sec, 1, keepdims=False)
        theirs = lax.dynamic_index_in_dim(cols, 1 - sec, 1, keepdims=False)
        halves.append(jnp.concatenate(by_layer(mine, swap(theirs)), 0))
    grad_in = jnp.stack(halves)[:, :, None, :]

    zx_parts, wo_parts, bcdt_parts, packs_out = [], [], [], []
    for layer in range(2):
        g_w = weight_grads[layer][0][0] + weight_grads[layer][1][0]
        g_wo = weight_grads[layer][0][1] + weight_grads[layer][1][1]
        zx_parts.append(scatter_dp(g_w[:, : 2 * inner], 0))
        wo_parts.append(scatter_dp(g_wo, 1))
        g_dt = lax.dot_general(
            g_w[:, 2 * inner + 2 * state :], head_pick(sec), NT,
            precision=lax.Precision.HIGHEST, preferred_element_type=F32,
        )
        bcdt_parts.append(jnp.concatenate([g_w[:, 2 * inner : 2 * inner + 2 * state], g_dt], 1))
        gcp, ghp, gch = (a + b for a, b in zip(*small_grads[layer]))
        ggain = jnp.sum(gain_grads[layer][0] + gain_grads[layer][1], 0, keepdims=True)
        g_skip = jnp.sum(gch[1].reshape(heads, HEAD), -1)
        packed = jnp.concatenate([ggain, jnp.zeros((7, width), F32)], 0)
        put = lax.dynamic_update_slice
        packed = put(packed, gcp[:5, :inner], (1, sec * inner))
        packed = put(packed, gcp[:5, inner:], (1, chip_inner))
        packed = put(packed, gch[0:1], (6, sec * inner))
        packed = put(packed, ghp[0:1, :heads], (7, sec * heads))
        packed = put(packed, ghp[1:2, :heads], (7, 2 * heads + sec * heads))
        packed = put(packed, g_skip[None], (7, 4 * heads + sec * heads))
        packs_out.append(packed)

    def own_halves(parts):
        got = [give(parts[layer], layer) for layer in range(2)]
        return jnp.where(first, parts[0], got[1]), jnp.where(first, got[0], parts[1])

    lead, trail = own_halves(zx_parts)
    grad_w_zx = jnp.stack([lead.reshape(-1, 2, inner), trail.reshape(-1, 2, inner)], 2)
    grad_w_zx = grad_w_zx.reshape(1, -1, 2, chip_inner)
    grad_w_out = jnp.concatenate(own_halves(wo_parts), 0)[None]

    got = [give(bcdt_parts[layer].astype(BF16), layer).astype(F32) for layer in range(2)]
    summed = jnp.where(first, bcdt_parts[0] + got[0], bcdt_parts[1] + got[1])
    shard = scatter_dp(summed, 0)
    low = shard.astype(BF16)
    for k in (1, 2, 3):
        shard = shard + across(low, k).astype(F32)
    grad_w_bcdt = shard[None]

    got = [give(packs_out[layer], layer) for layer in range(2)]
    mine = sum_dp(jnp.where(first, packs_out[0] + got[0], packs_out[1] + got[1]))
    shared = all_tensor(mine)
    grad_conv_x = mine[None, 1:6, :chip_inner]
    grad_conv_bc = shared[None, 1:6, chip_inner : chip_inner + 2 * state]
    head_rows = mine[7:8, : 6 * heads].reshape(3, 1, 2 * heads)
    return (
        out_act,
        grad_in,
        shared[0:1],
        grad_w_zx,
        grad_w_bcdt,
        grad_conv_x,
        grad_conv_bc,
        head_rows[0],
        head_rows[1],
        head_rows[2],
        mine[6:7, :chip_inner],
        grad_w_out,
    )


def solution(mesh):
    return jax.shard_map(
        on_device,
        mesh=mesh,
        in_specs=(
            P(None, "tensor", "dp", None),
            P(None, "tensor", "dp", None),
            P(None, "dp", None),
            P(None, None, "dp"),
            P("section", None),
            P("section", "dp", None, "tensor"),
            P("section", "dp", None),
            P("section", None, "tensor"),
            P("section", None, None),
            P("section", "tensor"),
            P("section", "tensor"),
            P("section", "tensor"),
            P("section", "tensor"),
            P("section", "tensor", "dp"),
        ),
        out_specs=(
            P(None, "tensor", "dp", None),
            P(None, "tensor", "dp", "section"),
            P("section", None),
            P("section", "dp", None, "tensor"),
            P("section", "dp", None),
            P("section", None, "tensor"),
            P("section", None, None),
            P("section", "tensor"),
            P("section", "tensor"),
            P("section", "tensor"),
            P("section", "tensor"),
            P("section", "tensor", "dp"),
        ),
        check_vma=False,
    )
```

```python
from functools import partial

import jax
import jax.numpy as jnp
from jax import lax
from jax.experimental import pallas as pl
from jax.experimental.pallas import tpu as pltpu
from jax.sharding import PartitionSpec as P

EPS = 1e-05
F32 = jnp.float32
BF16 = jnp.bfloat16
HEAD = 64
CHUNK = 128
LANES = 128
VMEM_LIMIT = 56 * 1024 * 1024
NN = (((1,), (0,)), ((), ()))
NT = (((1,), (1,)), ((), ()))
TN = (((0,), (0,)), ((), ()))


def mm(left, right, dims=NN):
    return lax.dot_general(left, right, dims, preferred_element_type=F32)


def sigmoid(value):
    return 0.5 * jnp.tanh(0.5 * value) + 0.5


def softplus(value):
    return jnp.maximum(value, 0.0) + jnp.log1p(jnp.exp(-jnp.abs(value)))


def iota(shape, dim):
    return lax.broadcasted_iota(jnp.int32, shape, dim)


def split_two(value):
    high = value.astype(BF16)
    return high, (value - high.astype(F32)).astype(BF16)


def split_three(value):
    high = value.astype(BF16)
    rest = value - high.astype(F32)
    mid = rest.astype(BF16)
    return high, mid, (rest - mid.astype(F32)).astype(BF16)


def fold_rows(value):
    rows = value.shape[0]
    return jnp.sum(value.reshape(rows // 8, 8, value.shape[1]), 0)


def doc_of(places, e0, e1):
    return (places >= e0).astype(jnp.int32) + (places >= e1).astype(jnp.int32)


def same_behind(places, steps, e0, e1):
    crossed = ((places >= e0) & (places < e0 + steps)) | ((places >= e1) & (places < e1 + steps))
    return jnp.where(crossed, 0.0, 1.0)


def same_ahead(places, steps, e0, e1):
    crossed = ((places < e0) & (places >= e0 - steps)) | ((places < e1) & (places >= e1 - steps))
    return jnp.where(crossed, 0.0, 1.0)


def chunk_decays(log_decay, tri):
    high, mid, low = split_three(log_decay)
    cum = mm(jnp.concatenate([tri, tri, tri], 1), jnp.concatenate([high, mid, low], 0))
    return cum, cum.T


def column(values, at):
    return jnp.broadcast_to(values[:, at : at + 1], (values.shape[0], LANES))


def conv_tile(ubuf, cp, tile, rows, masks):
    lanes = slice(tile * LANES, (tile + 1) * LANES)
    summed = cp[4:5, lanes] + cp[3:4, lanes] * ubuf[8 : 8 + rows, lanes]
    for steps in (1, 2, 3):
        shifted = ubuf[8 - steps : 8 - steps + rows, lanes] * masks[steps - 1]
        summed = summed + cp[3 - steps : 4 - steps, lanes] * shifted
    return summed


def bring(out, blocks, step, sec, ten, order):
    half = out.shape[0] // 2
    mine = pl.multiple_of(sec * half, half)
    theirs = pl.multiple_of((1 - sec) * half, half)
    far = (jnp.bitwise_xor(ten, step) >> (1 - order)) & 1
    width = out.shape[1]
    for k in range(2):

        @pl.when(far == k)
        def _(k=k):
            out[pl.ds(mine, half), :] = blocks[k][0, :, :width]
            out[pl.ds(theirs, half), :] = blocks[2 + k][0, :, :width]


def piece_spec(shape, order):
    return pl.BlockSpec(
        (1,) + shape[1:], lambda i, sc: ((jnp.bitwise_xor(sc[1], i) >> order) & 1, 0, 0)
    )


def fwd_kernel(with_dot, shards, inner, state, heads, order, sc, *refs):
    pieces = refs[:4]
    refs = refs[4:]
    if shards > 1:
        parts, refs, whole_w = refs[:shards], refs[shards:-1], refs[-1]

        @pl.when(pl.program_id(0) == 0)
        def _():
            size = parts[0].shape[0]
            for k in range(shards):
                at = pl.multiple_of(((sc[4] - k) & 3) * size, size)
                whole_w[pl.ds(at, size), :] = parts[k][...]

        refs = (whole_w, *refs)
    if with_dot:
        w, cp, hp, chp, live, gno, nrm, proj, y_out, st, gated_out, stats, carry, ubuf, act = refs
    else:
        w, cp, hp, chp, live, nrm, proj, y_out, st, gated_out, stats, carry, ubuf, act = refs
    step = pl.program_id(0)
    sec, ten, e0, e1 = sc[0], sc[1], sc[2], sc[3]
    rows = nrm.shape[0]
    wide = inner + 2 * state
    tiles = wide // LANES
    pairs = inner // LANES

    @pl.when(step == 0)
    def _():
        carry[...] = jnp.zeros_like(carry)
        ubuf[0:8, :] = jnp.zeros((8, wide), F32)

    bring(nrm, pieces, step, sec, ten, order)
    proj[...] = mm(nrm[...], w[...])
    lv = live[...]
    dt_at = slice(inner + wide, inner + wide + LANES)
    offset = ten * (2 * heads) + sec * heads
    proj[:, dt_at] = pltpu.roll(proj[:, dt_at], (LANES - offset) % LANES, 1) + hp[0:1, :]
    places = rows * step + iota((rows, LANES), 0)
    masks = [same_behind(places, steps, e0, e1) for steps in (1, 2, 3)]
    for tile in range(tiles):
        lanes = slice(tile * LANES, (tile + 1) * LANES)
        at = slice(inner + tile * LANES, inner + (tile + 1) * LANES)
        u = proj[:, at] * lv
        proj[:, at] = u
        ubuf[8 : 8 + rows, lanes] = u
    for tile in range(tiles):
        lanes = slice(tile * LANES, (tile + 1) * LANES)
        pre = conv_tile(ubuf, cp, tile, rows, masks)
        act[:, lanes] = (pre * sigmoid(pre)).astype(BF16)
    ubuf[0:8, :] = ubuf[rows : rows + 8, :]

    low_half = iota((CHUNK, LANES), 1) < HEAD
    tri = (iota((CHUNK, CHUNK), 0) >= iota((CHUNK, CHUNK), 1)).astype(F32).astype(BF16)
    gated_sq = []
    gated_dot = []
    for c in range(rows // CHUNK):
        r0 = c * CHUNK
        at = slice(r0, r0 + CHUNK)
        base = rows * step + r0
        t_at = base + iota((CHUNK, CHUNK), 0)
        s_at = base + iota((CHUNK, CHUNK), 1)
        id_t = doc_of(t_at, e0, e1)
        usable = (t_at >= s_at) & (id_t == doc_of(s_at, e0, e1))
        id_prev = doc_of(base - 1, e0, e1)
        id_end = doc_of(base + CHUNK - 1, e0, e1)
        from_prev = jnp.where(id_t == id_prev, 1.0, 0.0)
        tail_same = jnp.where(id_t == id_end, 1.0, 0.0)
        linked = jnp.where(id_end == id_prev, 1.0, 0.0).astype(F32)
        dt = softplus(proj[at, dt_at]) * live[at, :]
        cum, cum_t = chunk_decays(dt * hp[1:2, :], tri)
        b_in = act[at, inner : inner + state]
        c_in = act[at, inner + state : wide]
        scores = jnp.where(usable, mm(c_in, b_in, NT), 0.0)
        sq = jnp.zeros((CHUNK, LANES), F32)
        rd = jnp.zeros((CHUNK, LANES), F32)
        for k in range(pairs):
            lanes = slice(k * LANES, (k + 1) * LANES)
            mixed, cums = [], []
            for h in (2 * k, 2 * k + 1):
                cum_col = column(cum, h)
                cums.append(cum_col)
                decay = jnp.exp(jnp.minimum(cum_col - cum_t[h : h + 1, :], 0.0))
                mixed.append((decay * scores).astype(BF16))
            cum_e = jnp.where(low_half, cums[0], cums[1])
            dt_e = jnp.where(low_half, column(dt, 2 * k), column(dt, 2 * k + 1))
            x_in = act[at, lanes].astype(F32)
            xdt = x_in * dt_e
            both = jnp.concatenate([jnp.where(low_half, xdt, 0.0), jnp.where(low_half, 0.0, xdt)], 0)
            within = mm(jnp.concatenate(mixed, 1), both.astype(BF16))
            old = carry[:, lanes]
            old_low = old.astype(BF16)
            st[c, :, lanes] = old_low
            across = mm(c_in, old_low) * (jnp.exp(cum_e) * from_prev)
            cum_end = cum_e[CHUNK - 1 : CHUNK, :]
            to_end = jnp.exp(cum_end - cum_e) * tail_same
            added = mm(b_in, (xdt * to_end).astype(BF16), TN)
            carry[:, lanes] = old * (jnp.exp(cum_end) * linked) + added
            y = within + across + chp[0:1, lanes] * x_in
            y_out[at, lanes] = y
            gate = proj[at, lanes]
            gated = y * (gate * sigmoid(gate))
            gated_out[at, lanes] = gated
            sq = sq + gated * gated
            if with_dot:
                rd = rd + gated * chp[1:2, lanes] * gno[at, lanes]
        gated_sq.append(sq)
        gated_dot.append(rd)
    ones = jnp.ones((8, LANES), F32)
    exact = partial(
        lax.dot_general,
        dimension_numbers=NT,
        precision=lax.Precision.HIGHEST,
        preferred_element_type=F32,
    )
    total = exact(ones, jnp.concatenate(gated_sq, 0))
    if with_dot:
        dots = exact(ones, jnp.concatenate(gated_dot, 0))
        total = jnp.where(iota((8, rows), 0) == 0, total, dots)
    stats[...] = total


def call(kernel, name, scalars, grid, ins, outs, scratch, deps, flops, extra, moved):
    count = len(ins)
    specs = [spec for spec, _ in ins] + [pl.BlockSpec(memory_space=pl.ANY)] * len(deps)

    def body(sc, *refs):
        kernel(sc, *refs[:count], *refs[count + len(deps) :])

    return pl.pallas_call(
        body,
        out_shape=tuple(jax.ShapeDtypeStruct(shape, kind) for _, shape, kind in outs),
        grid_spec=pltpu.PrefetchScalarGridSpec(
            num_scalar_prefetch=1,
            grid=grid,
            in_specs=specs,
            out_specs=tuple(spec for spec, _, _ in outs),
            scratch_shapes=scratch,
        ),
        compiler_params=pltpu.CompilerParams(
            dimension_semantics=("arbitrary",) * len(grid), vmem_limit_bytes=VMEM_LIMIT
        ),
        cost_estimate=pl.CostEstimate(flops=flops, transcendentals=extra, bytes_accessed=moved),
        name=name,
    )(scalars, *[operand for _, operand in ins], *deps)


def whole(shape):
    return pl.BlockSpec(shape, lambda i, sc: (0,) * len(shape))


def fixed(array):
    return (whole(array.shape), array)


def bring_coef(out, blocks, width, step, sec, ten, order):
    half = out.shape[0] // 2
    mine = pl.multiple_of(sec * half, half)
    theirs = pl.multiple_of((1 - sec) * half, half)
    far = (jnp.bitwise_xor(ten, step) >> (1 - order)) & 1
    for k in range(2):

        @pl.when(far == k)
        def _(k=k):
            for at, block in ((mine, blocks[k]), (theirs, blocks[2 + k])):
                parts = block[0, :, width:].astype(F32)
                total = parts[:, 0:1] + parts[:, 1:2] + parts[:, 2:3]
                out[pl.ds(at, half), :] = jnp.broadcast_to(total, (half, LANES))


def turn_kernel(count, sc, *refs):
    parts, wo_t, w_t, wo = refs[:count], *refs[count:]
    if count == 1:
        w_t[...] = parts[0][...].T
    else:
        pick = (sc[4] - pl.program_id(0)) & 3
        for k in range(count):

            @pl.when(pick == k)
            def _(k=k):
                w_t[...] = parts[k][...].T

    wo[...] = wo_t[...].T


def run_turn(scalars, parts, wo_t, deps):
    depth, cols = wo_t.shape[0], parts[0].shape[1]
    rows = depth // 4
    by_row = lambda n: pl.BlockSpec((rows, n), lambda i, sc: (i, 0))
    by_col = lambda n: pl.BlockSpec((n, rows), lambda i, sc: (0, i))
    if len(parts) == 1:
        ins = [(by_row(cols), parts[0])]
    else:
        ins = [fixed(part) for part in parts]
    return call(
        partial(turn_kernel, len(parts)), "turn_weights", scalars, (4,),
        ins + [(by_row(wo_t.shape[1]), wo_t)],
        [
            (by_col(cols), (cols, depth), BF16),
            (by_col(wo_t.shape[1]), (wo_t.shape[1], depth), BF16),
        ],
        [], deps, 4 * 1024**3, 0, 10 * 1024 * 1024,
    )


def outer_kernel(count, start, sc, *refs):
    total = mm(refs[0][...], refs[1][...], TN)
    for k in range(1, count):
        total = total + mm(refs[2 * k][...], refs[2 * k + 1][...], TN)
    if start:
        total = total + refs[2 * count][...]
    refs[-1][...] = total


def run_outer(scalars, pairs, start, tall, deps):
    depth = pairs[0][0].shape[0]
    rows, cols = pairs[0][0].shape[1], pairs[0][1].shape[1]
    if tall:
        tile, grid = 3 * LANES, (rows // (3 * LANES),)
        cut = pl.BlockSpec((depth, tile), lambda i, sc: (0, i))
        out = pl.BlockSpec((tile, cols), lambda i, sc: (i, 0))
        ins = [item for a, b in pairs for item in ((cut, a), fixed(b))]
    else:
        tile, grid = 4 * LANES, (cols // (4 * LANES),)
        cut = pl.BlockSpec((depth, tile), lambda i, sc: (0, i))
        out = pl.BlockSpec((rows, tile), lambda i, sc: (0, i))
        ins = [item for a, b in pairs for item in (fixed(a), (cut, b))]
    if start is not None:
        ins.append((out, start))
    return call(
        partial(outer_kernel, len(pairs), start is not None), "outer_rows", scalars, grid, ins,
        [(out, (rows, cols), F32)], [], deps, 9 * 1024**3 * len(pairs), 0, 16 * 1024 * 1024,
    )[0]


def join_kernel(sc, mine, theirs, out):
    half = mine.shape[1]
    out[0, pl.ds(sc[0] * half, half), 0, :] = mine[0]
    out[0, pl.ds((1 - sc[0]) * half, half), 0, :] = theirs[0]


def run_join(scalars, mine, theirs):
    count, half, width = mine.shape
    spec = pl.BlockSpec((1, half, width), lambda i, sc: (i, 0, 0))
    return call(
        join_kernel, "join_rows", scalars, (count,), [(spec, mine), (spec, theirs)],
        [
            (
                pl.BlockSpec((1, 2 * half, 1, width), lambda i, sc: (i, 0, 0, 0)),
                (count, 2 * half, 1, width),
                F32,
            )
        ],
        [], [], 0, 0, 16 * 1024 * 1024,
    )[0]


def weave_kernel(sc, mine, theirs, out):
    size = mine.shape[1] // 2
    own = pl.ds(pl.multiple_of(sc[0] * size, LANES), size)
    other = pl.ds(pl.multiple_of((1 - sc[0]) * size, LANES), size)
    for k in range(2):
        out[:, k, own] = mine[:, k * size : (k + 1) * size]
        out[:, k, other] = theirs[:, k * size : (k + 1) * size]


def run_weave(scalars, mine, theirs):
    depth, width = mine.shape
    rows = depth if depth % 32 else depth // 4
    spec = pl.BlockSpec((rows, width), lambda i, sc: (i, 0))
    return call(
        weave_kernel, "weave_cols", scalars, (depth // rows,), [(spec, mine), (spec, theirs)],
        [(pl.BlockSpec((rows, 2, width), lambda i, sc: (i, 0, 0)), (depth, 2, width), F32)],
        [], [], 0, 0, 5 * 1024 * 1024,
    )[0]


def run_fwd(scalars, pieces, order, w, cp, hp, chp, live, gno, inner, state, heads, deps):
    half, width = pieces[0].shape[1:]
    rows = 2 * half
    length = live.shape[0]
    steps = length // rows
    cols = w[0].shape[1]
    chunks = rows // CHUNK
    by_row = lambda n: pl.BlockSpec((rows, n), lambda i, sc: (i, 0))
    ins = [(piece_spec(piece.shape, order), piece) for piece in pieces]
    ins += [fixed(part) for part in w]
    ins += [fixed(cp), fixed(hp), fixed(chp), (by_row(LANES), live)]
    joined = [pltpu.VMEM((width, cols), BF16)] if len(w) > 1 else []
    if gno is not None:
        ins.append((by_row(inner), gno))
    return call(
        partial(fwd_kernel, gno is not None, len(w), inner, state, heads, order), "layer_fwd", scalars, (steps,),
        ins,
        [
            (by_row(width), (length, width), BF16),
            (by_row(cols), (length, cols), F32),
            (by_row(inner), (length, inner), F32),
            (pl.BlockSpec((chunks, state, inner), lambda i, sc: (i, 0, 0)), (length // CHUNK, state, inner), BF16),
            (by_row(inner), (length, inner), F32),
            (pl.BlockSpec((8, rows), lambda i, sc: (0, i)), (8, length), F32),
        ],
        [
            pltpu.VMEM((state, inner), F32),
            pltpu.VMEM((rows + 8, inner + 2 * state), F32),
            pltpu.VMEM((rows, inner + 2 * state), BF16),
        ]
        + joined,
        deps, 24 * 1024**3, length * inner * 8, 24 * 1024**2,
    )


def scale_kernel(inner_width, sc, gated, sa, sb, chp, no_out, send, rc):
    rows = gated.shape[0]
    half = rows // 2
    theirs = pl.multiple_of((1 - sc[0]) * half, half)
    total = sa[...] + sb[...]
    inv = lax.rsqrt(total / inner_width + EPS)
    coef = jnp.concatenate([total[1:8], total[0:1]], 0) * (inv * inv * inv) / inner_width
    both = jnp.where(iota(total.shape, 0) == 0, inv, pltpu.roll(coef, 1, 0))
    for c in range(rows // CHUNK):
        at = slice(c * CHUNK, (c + 1) * CHUNK)
        cols = jnp.concatenate([both[:, at]] * (CHUNK // 8), 0).T
        rc[at, :] = cols
        col = column(cols, 0)
        for k in range(gated.shape[1] // LANES):
            lanes = slice(k * LANES, (k + 1) * LANES)
            no_out[at, lanes] = (gated[at, lanes] * col * chp[1:2, lanes]).astype(BF16)
    send[0] = no_out[pl.ds(theirs, half), :]


def run_scale(scalars, gated, sa, sb, chp, rows, inner_width, deps):
    length, inner = gated.shape
    steps = length // rows
    by_row = lambda n: pl.BlockSpec((rows, n), lambda i, sc: (i, 0))
    by_lane = pl.BlockSpec((8, rows), lambda i, sc: (0, i))
    return call(
        partial(scale_kernel, inner_width), "scale_rows", scalars, (steps,),
        [(by_row(inner), gated), (by_lane, sa), (by_lane, sb), fixed(chp)],
        [
            (by_row(inner), (length, inner), BF16),
            (pl.BlockSpec((1, rows // 2, inner), lambda i, sc: (i, 0, 0)), (steps, rows // 2, inner), BF16),
            (by_row(LANES), (length, LANES), F32),
        ],
        [], deps, 4 * 1024**3, 0, 8 * 1024**2,
    )


def bwd_kernel(inner, state, heads, order, sc, *refs):
    if order is None:
        gno, cc, proj, halo, y_in, st, rc, live, cp, hp, chp = refs[:11]
        refs = refs[11:]
    else:
        pieces, wo_t = refs[:4], refs[4]
        proj, halo, y_in, st, rc, live, cp, hp, chp = refs[5:14]
        gout, gno, cc = refs[14], refs[-2], refs[-1]
        refs = refs[15:-2]
    gz, gzsend, gpack, dstate, ubuf, gbuf, acc_c, acc_h, acc_n, acc_d = refs
    step = pl.program_id(0)
    steps = pl.num_programs(0)
    block = steps - 1 - step
    sec, ten, e0, e1 = sc[0], sc[1], sc[2], sc[3]
    offset = ten * (2 * heads) + sec * heads
    rows = y_in.shape[0]
    half = rows // 2
    wide = inner + 2 * state
    tiles = wide // LANES
    pairs = inner // LANES
    theirs = pl.multiple_of((1 - sec) * half, half)

    @pl.when(step == 0)
    def _():
        dstate[...] = jnp.zeros_like(dstate)
        gbuf[rows : rows + 8, :] = jnp.zeros((8, wide), F32)
        acc_c[...] = jnp.zeros_like(acc_c)
        acc_h[...] = jnp.zeros_like(acc_h)
        acc_n[...] = jnp.zeros_like(acc_n)
        acc_d[...] = jnp.zeros_like(acc_d)

    if order is not None:
        bring(gout, pieces, block, sec, ten, order)
        bring_coef(cc, pieces, gout.shape[1], block, sec, ten, order)
        gno[...] = mm(gout[...], wo_t[...])

    ubuf[0:8, :] = jnp.where(block == 0, 0.0, halo[:, inner : inner + wide])
    ubuf[8 : 8 + rows, :] = proj[:, inner : inner + wide]
    places = rows * block + iota((rows, LANES), 0)
    masks = [same_behind(places, steps_, e0, e1) for steps_ in (1, 2, 3)]

    low_half = iota((CHUNK, LANES), 1) < HEAD
    row_at = iota((CHUNK, CHUNK), 0)
    col_at = iota((CHUNK, CHUNK), 1)
    tri = (row_at >= col_at).astype(F32).astype(BF16)
    tri_rev = (row_at <= col_at).astype(F32).astype(BF16)
    tri_strict = (row_at > col_at).astype(F32).astype(BF16)
    sums = jnp.concatenate([tri_rev, tri_rev, tri_strict, tri_strict], 1)
    to_head = [
        (iota((LANES, LANES), 1) == 2 * k + (iota((LANES, LANES), 0) >= HEAD).astype(jnp.int32))
        .astype(F32)
        .astype(BF16)
        for k in range(pairs)
    ]

    for c in reversed(range(rows // CHUNK)):
        r0 = c * CHUNK
        at = slice(r0, r0 + CHUNK)
        cmasks = [m[at, :] for m in masks]
        acts, slopes = [], []
        for tile in range(tiles):
            lanes = slice(tile * LANES, (tile + 1) * LANES)
            pre = cp[4:5, lanes] + cp[3:4, lanes] * ubuf[8 + r0 : 8 + r0 + CHUNK, lanes]
            for n in (1, 2, 3):
                shifted = ubuf[8 + r0 - n : 8 + r0 - n + CHUNK, lanes] * cmasks[n - 1]
                pre = pre + cp[3 - n : 4 - n, lanes] * shifted
            sig = sigmoid(pre)
            acts.append((pre * sig).astype(BF16))
            slopes.append(sig * (1.0 + pre * (1.0 - sig)))
        b_in, c_in = acts[pairs], acts[pairs + 1]
        base = rows * block + r0
        id_s = doc_of(base + row_at, e0, e1)
        usable = (row_at <= col_at) & (id_s == doc_of(base + col_at, e0, e1))
        id_prev = doc_of(base - 1, e0, e1)
        id_end = doc_of(base + CHUNK - 1, e0, e1)
        from_prev = jnp.where(id_s == id_prev, 1.0, 0.0)
        tail_same = jnp.where(id_s == id_end, 1.0, 0.0)
        linked = jnp.where(id_end == id_prev, 1.0, 0.0).astype(F32)
        lv = live[at, :]
        dt_in = proj[at, inner + wide : inner + wide + LANES]
        dt = softplus(dt_in) * lv
        log_decay = dt * hp[1:2, :]
        cum, cum_t = chunk_decays(log_decay, tri)
        scores = jnp.where(usable, mm(b_in, c_in, NT), 0.0)
        inv = column(rc[at, :], 0)
        coef = column(cc[at, :], 1)
        d_scores = jnp.zeros((CHUNK, CHUNK), F32)
        gb = jnp.zeros((CHUNK, state), F32)
        gc = jnp.zeros((CHUNK, state), F32)
        r1 = jnp.zeros((CHUNK, LANES), F32)
        r2 = jnp.zeros((CHUNK, LANES), F32)
        r3 = jnp.zeros((CHUNK, LANES), F32)
        kept = jnp.zeros((8, LANES), F32)
        for k in range(pairs):
            lanes = slice(k * LANES, (k + 1) * LANES)
            gate = proj[at, lanes]
            sig = sigmoid(gate)
            silu = gate * sig
            y = y_in[at, lanes]
            gated = y * silu
            g_no = gno[at, lanes]
            gain = chp[1:2, lanes]
            skip = chp[0:1, lanes]
            scaled = gated * inv
            acc_n[:, lanes] += fold_rows(g_no * scaled)
            gg = inv * (g_no * gain) - gated * coef
            gy = gg * silu
            gz[at, lanes] = (gg * y * (sig * (1.0 + gate * (1.0 - sig)))).astype(BF16)
            x_in = acts[k].astype(F32)
            acc_d[:, lanes] += fold_rows(gy * x_in)
            dt_e = jnp.where(low_half, column(dt, 2 * k), column(dt, 2 * k + 1))
            gy_b = gy.astype(BF16)
            gy_f = gy_b.astype(F32)
            xdt_b = (x_in * dt_e).astype(BF16)
            xdt_f = xdt_b.astype(F32)
            gy_halves = [jnp.where(low_half, gy_f, 0.0).astype(BF16), jnp.where(low_half, 0.0, gy_f).astype(BF16)]
            mixed, cums = [], []
            for n in (0, 1):
                h = 2 * k + n
                cum_col = column(cum, h)
                cums.append(cum_col)
                decay = jnp.exp(jnp.minimum(cum_t[h : h + 1, :] - cum_col, 0.0))
                mixed.append((decay * scores).astype(BF16))
                d_scores = d_scores + decay * mm(xdt_b, gy_halves[n], NT)
            cum_e = jnp.where(low_half, cums[0], cums[1])
            gx_in = mm(jnp.concatenate(mixed, 1), jnp.concatenate(gy_halves, 0))
            cum_end = cum_e[CHUNK - 1 : CHUNK, :]
            to_end = jnp.exp(cum_end - cum_e) * tail_same
            entering = jnp.exp(cum_e) * from_prev
            s_in = st[c, :, lanes]
            d_out = dstate[:, lanes]
            d_out_b = d_out.astype(BF16)
            gx_st = mm(b_in, d_out_b) * to_end
            gb = gb + mm((xdt_f * to_end).astype(BF16), d_out_b, NT)
            gye = (gy * entering).astype(BF16)
            gc = gc + mm(gye, s_in, NT)
            dec = jnp.exp(cum_end) * linked
            prod = fold_rows(s_in.astype(F32) * d_out) * dec
            p_hi, p_lo = split_two(prod)
            kept = kept + mm(p_hi, to_head[k]) + mm(p_lo, to_head[k])
            dstate[:, lanes] = d_out * dec + mm(c_in, gye, TN)
            gx = gx_in + gx_st
            t_hi, t_lo = split_two(gy_f * (y - skip * x_in) - xdt_f * gx_in)
            pair2 = jnp.concatenate([to_head[k], to_head[k]], 0)
            r1 = r1 + mm(jnp.concatenate([t_hi, t_lo], 1), pair2)
            t_hi, t_lo = split_two(x_in * gx)
            r2 = r2 + mm(jnp.concatenate([t_hi, t_lo], 1), pair2)
            t_hi, t_lo = split_two(x_in * gx_st)
            r3 = r3 + mm(jnp.concatenate([t_hi, t_lo], 1), pair2)
            gbuf[at, lanes] = (gx * dt_e + gy * skip) * slopes[k]
        d_scores = jnp.where(usable, d_scores, 0.0).astype(BF16)
        gb = gb + mm(d_scores, c_in)
        gc = gc + mm(d_scores, b_in, TN)
        for n in range(state // LANES):
            b_at = slice(inner + n * LANES, inner + (n + 1) * LANES)
            c_at = slice(inner + state + n * LANES, inner + state + (n + 1) * LANES)
            gbuf[at, b_at] = gb * slopes[pairs]
            gbuf[at, c_at] = gc * slopes[pairs + 1]
        a_hi, a_lo = split_two(r1)
        b_hi, b_lo = split_two(dt * r3)
        g_ld = mm(sums, jnp.concatenate([a_hi, a_lo, b_hi, b_lo], 0)) + jnp.sum(kept, 0, keepdims=True)
        g_dt = (r2 + g_ld * hp[1:2, :]) * (sigmoid(dt_in) * lv)
        acc_h[0:8, :] += fold_rows(g_dt)
        acc_h[8:16, :] += fold_rows(g_ld * log_decay)
        gz[at, inner + wide : inner + wide + LANES] = pltpu.roll(g_dt, offset, 1).astype(BF16)

    ahead = [same_ahead(places, n, e0, e1) for n in (1, 2, 3)]
    lv = live[...]
    for tile in range(tiles):
        lanes = slice(tile * LANES, (tile + 1) * LANES)
        gp = gbuf[0:rows, lanes]
        gu = cp[3:4, lanes] * gp
        acc_c[24:32, lanes] += fold_rows(gp * ubuf[8 : 8 + rows, lanes])
        acc_c[32:40, lanes] += fold_rows(gp)
        for n in (1, 2, 3):
            gu = gu + cp[3 - n : 4 - n, lanes] * (gbuf[n : n + rows, lanes] * ahead[n - 1])
            shifted = ubuf[8 - n : 8 - n + rows, lanes] * masks[n - 1]
            acc_c[8 * (3 - n) : 8 * (4 - n), lanes] += fold_rows(gp * shifted)
        at = slice(inner + tile * LANES, inner + (tile + 1) * LANES)
        gz[:, at] = (gu * lv).astype(BF16)
    gbuf[rows : rows + 8, :] = gbuf[0:8, :]
    gzsend[0] = gz[pl.ds(theirs, half), :]

    @pl.when(step == steps - 1)
    def _():
        gpack[...] = jnp.zeros_like(gpack)
        own = pl.ds(pl.multiple_of(sec * inner, LANES), inner)
        for n in range(5):
            line = jnp.sum(acc_c[8 * n : 8 * n + 8, :], 0, keepdims=True)
            gpack[1 + n : 2 + n, own] = line[:, :inner]
            gpack[1 + n : 2 + n, 2 * inner : 2 * inner + 2 * state] = line[:, inner:]
        gpack[6:7, own] = jnp.sum(acc_n[...], 0, keepdims=True)
        skips = jnp.zeros((8, LANES), F32)
        for k in range(pairs):
            d_hi, d_mid, d_low = split_three(acc_d[:, k * LANES : (k + 1) * LANES])
            skips = skips + (mm(d_hi, to_head[k]) + mm(d_mid, to_head[k]) + mm(d_low, to_head[k]))
        heads_sums = [acc_h[0:8, :], acc_h[8:16, :], skips]
        for n in range(3):
            line = jnp.sum(pltpu.roll(heads_sums[n], sec * heads, 1), 0, keepdims=True)
            gpack[7 + n : 8 + n, 0:LANES] = line


def run_bwd(scalars, rows_in, order, proj, y, st, rc, live, cp, hp, chp, inner, state, heads, rows, width, deps):
    length, cols = proj.shape
    steps = length // rows
    half = rows // 2
    chunks = rows // CHUNK
    wide = inner + 2 * state
    back = lambda i: steps - 1 - i
    by_row = lambda n: pl.BlockSpec((rows, n), lambda i, sc: (back(i), 0))
    halo = pl.BlockSpec((8, cols), lambda i, sc: (jnp.maximum(back(i) * (rows // 8) - 1, 0), 0))
    scratch = [
        pltpu.VMEM((state, inner), F32),
        pltpu.VMEM((rows + 8, wide), F32),
        pltpu.VMEM((rows + 8, wide), F32),
        pltpu.VMEM((40, wide), F32),
        pltpu.VMEM((16, LANES), F32),
        pltpu.VMEM((8, inner), F32),
        pltpu.VMEM((8, inner), F32),
    ]
    if order is None:
        gno, cc = rows_in
        ins, outs = [(by_row(inner), gno), (by_row(LANES), cc)], []
    else:
        pieces, wo_t = rows_in
        shape = pieces[0].shape
        spec = pl.BlockSpec(
            (1,) + shape[1:],
            lambda i, sc: ((jnp.bitwise_xor(sc[1], back(i)) >> order) & 1, 0, 0),
        )
        ins = [(spec, piece) for piece in pieces] + [fixed(wo_t)]
        outs = [(by_row(width), (length, width), BF16)]
        scratch += [pltpu.VMEM((rows, inner), F32), pltpu.VMEM((rows, LANES), F32)]
    ins += [
        (by_row(cols), proj),
        (halo, proj),
        (by_row(inner), y),
        (pl.BlockSpec((chunks, state, inner), lambda i, sc: (back(i), 0, 0)), st),
        (by_row(LANES), rc),
        (by_row(LANES), live),
        fixed(cp),
        fixed(hp),
        fixed(chp),
    ]
    outs += [
        (by_row(cols), (length, cols), BF16),
        (pl.BlockSpec((1, half, cols), lambda i, sc: (back(i), 0, 0)), (steps, half, cols), BF16),
        (whole((16, width)), (16, width), F32),
    ]
    return call(
        partial(bwd_kernel, inner, state, heads, order), "layer_bwd", scalars, (steps,),
        ins, outs, scratch, deps, 28 * 1024**3, length * inner * 12, 24 * 1024**2,
    )


def gn_kernel(order, sc, *refs):
    pieces, w, gno, gout = refs[:4], refs[4], refs[5], refs[6]
    step, sec, ten = pl.program_id(0), sc[0], sc[1]
    bring(gout, pieces, step, sec, ten, order)
    if len(refs) > 7:
        bring_coef(refs[7], pieces, gout.shape[1], step, sec, ten, order)
    gno[...] = mm(gout[...], w[...])


def run_gn(scalars, pieces, order, w, width, deps):
    half, cols = pieces[0].shape[1:]
    inner = w.shape[1]
    rows, length = 2 * half, 8 * half
    by_row = lambda n: pl.BlockSpec((rows, n), lambda i, sc: (i, 0))
    outs = [(by_row(inner), (length, inner), F32), (by_row(width), (length, width), BF16)]
    if cols > width:
        outs.append((by_row(LANES), (length, LANES), F32))
    return call(
        partial(gn_kernel, order), "grad_rows", scalars, (length // rows,),
        [(piece_spec(piece.shape, order), piece) for piece in pieces] + [fixed(w)],
        outs, [], deps, 8 * 1024**3, 0, 18 * 1024**2,
    )


def half_kernel(axis, sc, kept, got, wa, wb, own, near, far):
    ten = sc[1]
    groups = [jnp.bitwise_xor(ten, k) for k in (0, 3 - axis, axis, 3)]
    half = own.shape[0]
    left = jnp.concatenate([kept[g, 0] for g in groups], 0)
    right = jnp.concatenate([got[g] for g in groups], 0)
    total = mm(jnp.concatenate([left, right], 1), jnp.concatenate([wa[...], wb[...]], 0))
    own[...] = total[:half]
    near[...] = total[half : 2 * half]
    far[0] = total[2 * half : 3 * half].astype(BF16)
    far[1] = total[3 * half :].astype(BF16)


def run_half(scalars, full, got, wa, wb, axis, deps):
    groups, half, depth = got.shape
    width = wa.shape[1]
    tile = 4 * LANES
    w_spec = pl.BlockSpec((depth, tile), lambda i, sc: (0, i))
    part = pl.BlockSpec((half, tile), lambda i, sc: (0, i))
    return call(
        partial(half_kernel, axis), "half_rows", scalars, (width // tile,),
        [
            (
                pl.BlockSpec((groups, 1, half, depth), lambda i, sc: (0, sc[0], 0, 0)),
                full.reshape(groups, 2, half, depth),
            ),
            fixed(got),
            (w_spec, wa),
            (w_spec, wb),
        ],
        [
            (part, (half, width), F32),
            (part, (half, width), F32),
            (pl.BlockSpec((2, half, tile), lambda i, sc: (0, 0, i)), (2, half, width), BF16),
        ],
        [], deps, 8 * 1024**3, 0, 10 * 1024**2,
    )


def norm_kernel(x, gain, out):
    v = x[...].astype(F32)
    inv = lax.rsqrt(jnp.mean(v * v, -1, keepdims=True) + EPS)
    out[...] = (v * inv * gain[0:1, :]).astype(BF16)


def owner_kernel(final, own, far, near, x, gain, *outs):
    total = own[...] + far[0].astype(F32) + near[...].astype(F32)
    out = x[...].astype(F32) + total
    if final:
        outs[0][...] = out
        return
    h1, normed, kept = outs
    low = out.astype(BF16)
    h1[...] = low
    kept[...] = total
    v = low.astype(F32)
    inv = lax.rsqrt(jnp.mean(v * v, -1, keepdims=True) + EPS)
    normed[...] = (v * inv * gain[0:1, :]).astype(BF16)


def owner_back_kernel(last, inner_width, own, far, near, v_in, g_in, gain, *refs):
    g = own[...] + far[0].astype(F32) + near[...].astype(F32)
    v = v_in[...].astype(F32)
    width = v.shape[1]
    inv = lax.rsqrt(jnp.mean(v * v, -1, keepdims=True) + EPS)
    scaled = v * inv
    p = g * gain[0:1, :]
    out = g_in[:, :width].astype(F32) + inv * (p - scaled * jnp.mean(p * scaled, -1, keepdims=True))
    if last:
        g_v, ggain = refs
        g_v[...] = out
    else:
        kept, rcol, g_v, ggain = refs
        low = out.astype(BF16)
        g_v[:, :width] = low
        r = rcol[:, 0:1]
        coef = r * r * jnp.sum(low.astype(F32) * kept[...], -1, keepdims=True) / inner_width
        shape = (v.shape[0], LANES)
        high, mid, small = [
            jnp.broadcast_to(part.astype(F32), shape) for part in split_three(coef)
        ]
        lane = iota(shape, 1)
        parts = jnp.where(lane == 0, high, jnp.where(lane == 1, mid, small))
        g_v[:, width:] = parts.astype(BF16)
    ggain[...] = jnp.zeros_like(ggain)
    ggain[0:1, :] = jnp.sum(g * scaled, 0, keepdims=True)


def run_plain(kernel, name, out_shape, operands, deps):
    count = len(operands)
    vmem = pl.BlockSpec(memory_space=pltpu.VMEM)

    def body(*refs):
        kernel(*refs[:count], *refs[count + len(deps) :])

    return pl.pallas_call(
        body,
        in_specs=[vmem] * count + [pl.BlockSpec(memory_space=pl.ANY)] * len(deps),
        out_shape=out_shape,
        compiler_params=pltpu.CompilerParams(vmem_limit_bytes=VMEM_LIMIT),
        cost_estimate=pl.CostEstimate(
            flops=3 * 1024**3, transcendentals=0, bytes_accessed=6 * 1024**2
        ),
        name=name,
    )(*operands, *deps)


def across(value, step):
    count = lax.axis_size("tensor")
    return lax.ppermute(value, "tensor", [(i, i ^ step) for i in range(count)])


def swap(value):
    return lax.ppermute(value, "section", [(0, 1), (1, 0)])


def reach(value, order):
    return value, across(value, 1 + order)


def widen(pair, order, *waits):
    near = jnp.stack([after(pair[0], *waits), pair[1]])
    return near, across(near, 2 - order)


def share(near, far):
    return [near, far, swap(near), swap(far)]


def spread(value, order):
    return share(*widen(reach(value, order), order))


def hand(outs, order):
    return outs[0], outs[1], across(outs[2], 2 - order)


def settle(held, order, *waits):
    own, near, far = held
    send = (after(near, *waits) + far[1].astype(F32)).astype(BF16)
    return own, far, across(send, 1 + order)


def all_tensor(value):
    value = value + across(value, 1)
    return value + across(value, 2)


def cycle(value, steps):
    count = lax.axis_size("dp")
    return lax.ppermute(value, "dp", [(i, (i + steps) % count) for i in range(count)])


def pieces_dp(value):
    if lax.axis_size("dp") != 4:
        return [lax.all_gather(value, "dp", axis=0, tiled=True)]
    return [value] + [cycle(value, k) for k in (1, 2, 3)]


def gather_dp(value):
    got = pieces_dp(value)
    if len(got) == 1:
        return got[0]
    at = lax.axis_index("dp")
    shards = [lax.select_n(at, *[got[(i - j) % 4] for i in range(4)]) for j in range(4)]
    return jnp.concatenate(shards, 0)


def trade(value, bit):
    return lax.ppermute(value, "dp", [(i, i ^ bit) for i in range(4)])


def deal_one(value):
    at = lax.axis_index("dp")
    odd = (at & 1) == 1
    shards = value.reshape(4, value.shape[0] // 4, value.shape[1])
    kept = jnp.where(odd, shards[1::2], shards[0::2])
    sent = jnp.where(odd, shards[0::2], shards[1::2]).astype(BF16)
    return sent, kept, trade(sent, 1)


def deal_two(kept, got):
    high = lax.axis_index("dp") >= 2
    both = kept + got.astype(F32)
    sent = jnp.where(high, both[0], both[1]).astype(BF16)
    return jnp.where(high, both[1], both[0]), trade(sent, 2)


def scatter_dp(value):
    return lax.psum_scatter(value, "dp", scatter_dimension=0, tiled=True)


def sum_dp(value):
    if lax.axis_size("dp") != 4:
        return lax.psum(value, "dp")
    return value + cycle(value, 1) + cycle(value, 2) + cycle(value, 3)


def after(value, *waits):
    return lax.optimization_barrier((value, *waits))[0]


def on_device(
    x_in,
    d_out,
    doc_lengths,
    token_mask,
    gain_in,
    w_zx,
    w_bcdt,
    conv_x,
    conv_bc,
    dt_bias,
    a_log,
    d_skip,
    gain_inner,
    w_out,
):
    micro_count, local_rows, _, width = x_in.shape
    length = token_mask.shape[1]
    half = local_rows // 2
    rows = local_rows
    inner = conv_x.shape[2] // 2
    heads = dt_bias.shape[1] // 2
    state = conv_bc.shape[2] // 2
    chip_inner = 2 * inner
    full_inner = chip_inner * lax.axis_size("tensor")
    sec = lax.axis_index("section")
    ten = lax.axis_index("tensor")
    first = sec == 0
    micros = range(micro_count)

    def by_layer(own, other):
        return [jnp.where(first, own, other), jnp.where(first, other, own)]

    pad_to = lambda v, n: jnp.pad(v, ((0, 0), (0, n - v.shape[1])))
    pack = jnp.concatenate(
        [
            gain_in,
            pad_to(jnp.concatenate([conv_x[0], conv_bc[0]], 1), width),
            pad_to(gain_inner, width),
            pad_to(jnp.concatenate([dt_bias, a_log, d_skip], 1), width),
        ],
        0,
    )
    packs = by_layer(pack, swap(pack))
    gains = [jnp.broadcast_to(p[0:1], (8, width)) for p in packs]

    gate_w, x_w = w_zx[0, :, 0, :], w_zx[0, :, 1, :]
    ends = [jnp.concatenate([gate_w[:, at], x_w[:, at]], 1) for at in (slice(inner), slice(inner, None))]
    zx_own, zx_send = by_layer(*ends)
    bc_own = pad_to(w_bcdt[0], 2 * state + LANES)
    got = swap(jnp.concatenate([zx_send, bc_own], 1))
    zx_shards = by_layer(jnp.concatenate([zx_own, bc_own], 1), got)
    wo_own, wo_send = by_layer(w_out[0, :inner].T, w_out[0, inner:].T)
    wo_shards = by_layer(wo_own, swap(wo_send))
    first_parts = pieces_dp(zx_shards[0])

    rows_at = lambda v, m: jnp.where(first, v[m, :half, 0, :], v[m, half:, 0, :])
    xs = [rows_at(x_in, m) for m in micros]
    gs = [rows_at(d_out, m) for m in micros]
    wide = lambda kind, n=0: jax.ShapeDtypeStruct((half, width + n), kind)
    small = jax.ShapeDtypeStruct((16, width), F32)
    pieces0 = [
        widen(reach(run_plain(norm_kernel, "norm_rows", wide(BF16), (xs[m], gains[0]), ()), 0), 0)
        for m in micros
    ]
    wide0 = pieces0
    pieces0 = [share(wide0[0][0], after(wide0[0][1], *first_parts[1:2]))]
    later = lambda v: lax.all_gather(after(v, *first_parts), "dp", axis=0, tiled=True)
    wo_t0, wo_t1 = later(wo_shards[0]), later(wo_shards[1])
    w1 = later(zx_shards[1])

    scalars, lives = [], []
    for m in micros:
        e0 = doc_lengths[m, 0, 0]
        e1 = e0 + doc_lengths[m, 0, 1]
        scalars.append(jnp.stack([sec, ten, e0, e1, lax.axis_index("dp")]).astype(jnp.int32))
        lives.append(jnp.broadcast_to(token_mask[m].astype(F32), (length, LANES)))
    places = scalars[0]

    layers = []
    for layer in range(2):
        p = packs[layer]
        pick = lambda row, start, count: jnp.where(
            first, p[row : row + 1, start : start + count],
            p[row : row + 1, start + count : start + 2 * count],
        )
        taps = jnp.concatenate(
            [
                jnp.where(first, p[1:6, :inner], p[1:6, inner:chip_inner]),
                p[1:6, chip_inner : chip_inner + 2 * state],
            ],
            1,
        )
        cp = jnp.pad(taps, ((0, 3), (0, 0)))
        bias = pad_to(pick(7, 0, heads), LANES)
        rate = pad_to(-jnp.exp(pick(7, 2 * heads, heads)), LANES)
        hp = jnp.concatenate([bias, rate, jnp.zeros((6, LANES), F32)], 0)
        skip = jnp.broadcast_to(pick(7, 4 * heads, heads).reshape(heads, 1), (heads, HEAD))
        chp = jnp.concatenate(
            [skip.reshape(1, inner), pick(6, 0, inner), jnp.zeros((6, inner), F32)], 0
        )
        layers.append(dict(cp=cp, hp=hp, chp=chp))
    early, late = layers

    def fwd(k, m, pieces, gno, deps):
        nrm, proj, y, st, gated, stats = run_fwd(
            scalars[m], pieces, 0, k["w"], k["cp"], k["hp"], k["chp"], lives[m], gno,
            inner, state, heads, deps,
        )
        part = stats + swap(stats)
        part = part + across(part, 1 + m)
        got = across(part, 2 - m)
        return dict(nrm=nrm, proj=proj, y=y, st=st, gated=gated, stats=stats, part=part, got=got)

    def scale(k, m, r, deps):
        r["no"], send, r["rc"] = run_scale(
            scalars[m], r["gated"], r["part"], r["got"], k["chp"], rows, full_inner, deps
        )
        r["sent"] = swap(send)

    def project(k, m, r, deps):
        return run_half(scalars[m], r["no"], r["sent"], k["wo"], k["wo_other"], 2, deps)

    def back(k, m, rows_in, order, r, deps):
        out = run_bwd(
            scalars[m], rows_in, order, r["proj"], r["y"], r["st"], r["rc"], lives[m],
            k["cp"], k["hp"], k["chp"], inner, state, heads, rows, width, deps,
        )
        gz, gzsend, gpack = out[-3:]
        return gz, swap(gzsend), gpack, out[0]

    def unproject(k, m, gz, got, deps):
        return run_half(scalars[m], gz, got, k["w_t"], k["w_t_other"], 2, deps)

    def middle(m, parts, deps):
        return run_plain(
            partial(owner_kernel, False), "owner_mid", (wide(BF16), wide(BF16), wide(F32)),
            (*parts, xs[m], gains[1]), deps,
        )

    early["w"], late["w"] = first_parts, [w1]
    near_g = [reach(after(gs[m], *first_parts), m) for m in micros]

    a0 = fwd(early, 0, pieces0[0], None, ())
    early["wo_t"], late["wo_t"] = wo_t0, wo_t1
    wide_g = [widen(near_g[m], m, a0["stats"]) for m in micros]
    pieces0.append(share(wide0[1][0], after(wide0[1][1], a0["stats"])))
    a1 = fwd(early, 1, pieces0[1], None, [a0["stats"]] + [pair[1] for pair in near_g])
    early["wo"] = wo_t0.T
    early["wo_other"] = swap(early["wo"])
    scale(early, 0, a0, [a1["stats"]])
    pieces_g = [share(*wide_g[m]) for m in micros]
    outs0 = project(early, 0, a0, ())
    held0 = hand(outs0, 0)
    scale(early, 1, a1, [outs0[0]])
    outs1 = project(early, 1, a1, [pair[1] for pair in wide_g])
    held1 = hand(outs1, 0)
    gno0, gout1_0 = run_gn(scalars[0], pieces_g[0], 0, late["wo_t"], width, [outs1[0]])
    parts0 = settle(held0, 0, gno0)
    gno1, gout1_1 = run_gn(scalars[1], pieces_g[1], 1, late["wo_t"], width, [gno0, held0[2]])
    parts1 = settle(held1, 0, gno1)
    h_0, normed_0, u_0 = middle(0, parts0, [gno1, held1[2]])
    pair0 = reach(normed_0, 0)
    h_1, normed_1, u_1 = middle(1, parts1, [normed_0])
    pair1 = reach(normed_1, 0)
    late["w_t"], late["wo"] = run_turn(places, late["w"], late["wo_t"], [normed_1])
    wide0 = widen(pair0, 0, late["wo"])
    wide1 = widen(pair1, 0, late["wo"])
    early["w_t"], _ = run_turn(places, early["w"], early["wo_t"], [late["wo"], pair0[1], pair1[1]])
    late["wo_other"] = swap(late["wo"])
    for k in layers:
        k["w_t_other"] = swap(k["w_t"])

    b0 = fwd(late, 0, share(*wide0), gno0, [early["w_t"]])
    b1 = fwd(late, 1, share(*wide1), gno1, [b0["stats"]])
    scale(late, 0, b0, [b1["stats"], early["w_t_other"]])
    gz0, got0, pack0, _ = back(late, 0, (gno0, b0["rc"]), None, b0, [b0["no"]])
    scale(late, 1, b1, [pack0])
    outs0 = unproject(late, 0, gz0, got0, [b1["no"]])
    held0 = hand(outs0, 0)
    gz1, got1, pack1, _ = back(late, 1, (gno1, b1["rc"]), None, b1, [outs0[0]])
    parts0 = settle(held0, 0, pack1)
    g_wo1 = run_outer(
        places, [(b0["no"], gout1_0), (b1["no"], gout1_1)], None, False, [pack1, held0[2]]
    )
    outs1 = unproject(late, 1, gz1, got1, [g_wo1])
    held1 = hand(outs1, 0)

    own_at = ten * rows + sec * half
    rcol = lambda r: lax.dynamic_slice_in_dim(r["rc"], own_at, half, 0)

    def turn(m, parts, h, u, r, deps):
        return run_plain(
            partial(owner_back_kernel, False, full_inner), "owner_back",
            (wide(BF16, LANES), small), (*parts, h, gs[m], gains[1], u, rcol(r)), deps,
        )

    gh_0, gain1_0 = turn(0, parts0, h_0, u_0, a0, [outs1[0]])
    pair0 = reach(gh_0, 0)
    g_w1 = run_outer(places, [(b0["nrm"], gz0), (b1["nrm"], gz1)], None, True, [gh_0])
    parts1 = settle(held1, 0, g_w1)
    wide0 = widen(pair0, 0, g_w1)
    final0 = project(late, 0, b0, [g_w1])
    gh_1, gain1_1 = turn(1, parts1, h_1, u_1, a1, [final0[0]])
    pair1 = reach(gh_1, 0)
    wide1 = widen(pair1, 0)
    turned0, turned1 = share(*wide0), share(*wide1)
    spill = lambda g, axis: lax.psum_scatter(g, "dp", scatter_dimension=axis, tiled=True)
    narrow = lambda g, axis: spill(g.astype(BF16), axis).astype(F32)
    wo1_sum = narrow(g_wo1, 1)
    zx1_sum = narrow(after(g_w1, pair0[1])[:, : 2 * inner], 0)
    tiny1 = pack0 + pack1 + gain1_0 + gain1_1
    bcdt_at = slice(2 * inner, 2 * inner + w_bcdt.shape[2])

    gz0, got0, pack0, gout0_0 = back(early, 0, (turned0, early["wo_t"]), 0, a0, [gh_1, pair1[1]])
    final1 = project(late, 1, b1, [pack0, wide1[1]])
    outs0 = unproject(early, 0, gz0, got0, [final1[0]])
    held0 = hand(outs0, 0)
    g_w0 = run_outer(places, [(a0["nrm"], gz0)], None, True, [outs0[0]])
    gno0_1, gout0_1, cc0_1 = run_gn(scalars[1], turned1, 0, early["wo_t"], width, [g_w0])
    g_wo0 = run_outer(
        places, [(a0["no"], gout0_0), (a1["no"], gout0_1)], None, False, [gno0_1]
    )
    wo0_sum = narrow(g_wo0, 1)
    hold = lambda outs: (after(outs[0], gno0_1), outs[1], after(outs[2], gno0_1))
    heldf = [hand(hold(outs), 0) for outs in (final0, final1)]
    gz1, got1, pack1, _ = back(early, 1, (gno0_1, cc0_1), None, a1, [g_wo0])
    g_w0 = run_outer(places, [(a1["nrm"], gz1)], g_w0, True, [pack1, held0[2], heldf[0][2]])
    zx0_sum = narrow(g_w0[:, : 2 * inner], 0)
    outs1 = unproject(early, 1, gz1, got1, [g_w0, heldf[1][2]])
    held1 = hand(outs1, 0)
    pair = by_layer(g_w0[:, bcdt_at], g_w1[:, bcdt_at])
    bc_got = swap(pair[1].astype(BF16))
    parts0 = settle(held0, 0, outs1[0])
    def finish(m, h, deps):
        return run_plain(
            partial(owner_kernel, True), "owner_out", wide(F32), (*partsf[m], h, gains[1]), deps
        )

    def last(m, parts, gh, deps):
        return run_plain(
            partial(owner_back_kernel, True, full_inner), "owner_last", (wide(F32), small),
            (*parts, xs[m], gh, gains[0]), deps,
        )

    paired = after(pair[0], outs1[0]) + bc_got.astype(F32)
    gv_0, gain0_0 = last(0, parts0, gh_0, [outs1[0]])
    partsf = [settle(heldf[m], 0, outs1[0]) for m in micros]
    if lax.axis_size("dp") == 4:
        _, b_kept, b_got = deal_one(paired)
        finals = [finish(0, h_0, [gv_0, b_got])]
        b_kept, b_got = deal_two(b_kept, b_got)
        shard = b_kept + b_got.astype(F32)
    else:
        shard = scatter_dp(paired)
        finals = [finish(0, h_0, [gv_0])]
    finals.append(finish(1, h_1, [finals[0], held1[2]]))
    parts1 = settle(held1, 0, finals[1])
    gv_1, gain0_1 = last(1, parts1, gh_1, ())
    tiny0 = pack0 + pack1 + gain0_0 + gain0_1

    finals = jnp.stack(finals)
    out_act = run_join(places, finals, swap(finals))
    both = jnp.stack([gv_0, gv_1])
    mine, theirs = by_layer(both[:, :, : width // 2], both[:, :, width // 2 :])
    grad_in = run_join(places, mine, swap(theirs))

    kept, sent = by_layer(tiny0, tiny1)
    mine = sum_dp(kept + swap(sent))
    shared = all_tensor(mine)
    for bit in (1, 2):
        shard = shard + across(shard.astype(BF16), bit).astype(F32)
    grad_w_bcdt = shard[None]

    def owned(parts):
        kept, sent = by_layer(parts[0], parts[1])
        return kept, swap(sent)

    grad_w_zx = run_weave(places, *owned([zx0_sum, zx1_sum]))[None]
    grad_w_out = jnp.concatenate(by_layer(*owned([wo0_sum, wo1_sum])), 0)[None]
    return (
        out_act,
        grad_in,
        shared[0:1],
        grad_w_zx,
        grad_w_bcdt,
        mine[None, 1:6, :chip_inner],
        shared[None, 1:6, chip_inner : chip_inner + 2 * state],
        mine[7:8, : 2 * heads],
        mine[8:9, : 2 * heads],
        mine[9:10, : 2 * heads],
        mine[6:7, :chip_inner],
        grad_w_out,
    )


def solution(mesh):
    return jax.shard_map(
        on_device,
        mesh=mesh,
        in_specs=(
            P(None, "tensor", "dp", None),
            P(None, "tensor", "dp", None),
            P(None, "dp", None),
            P(None, None, "dp"),
            P("section", None),
            P("section", "dp", None, "tensor"),
            P("section", "dp", None),
            P("section", None, "tensor"),
            P("section", None, None),
            P("section", "tensor"),
            P("section", "tensor"),
            P("section", "tensor"),
            P("section", "tensor"),
            P("section", "tensor", "dp"),
        ),
        out_specs=(
            P(None, "tensor", "dp", None),
            P(None, "tensor", "dp", "section"),
            P("section", None),
            P("section", "dp", None, "tensor"),
            P("section", "dp", None),
            P("section", None, "tensor"),
            P("section", None, None),
            P("section", "tensor"),
            P("section", "tensor"),
            P("section", "tensor"),
            P("section", "tensor"),
            P("section", "tensor", "dp"),
        ),
        check_vma=False,
    )
```

```python
from functools import partial

import jax
import jax.numpy as jnp
from jax import lax
from jax.experimental import pallas as pl
from jax.experimental.pallas import tpu as pltpu
from jax.sharding import PartitionSpec as P

EPS = 1e-05
F32 = jnp.float32
BF16 = jnp.bfloat16
HEAD = 64
CHUNK = 128
LANES = 128
VMEM_LIMIT = 56 * 1024 * 1024
NN = (((1,), (0,)), ((), ()))
NT = (((1,), (1,)), ((), ()))
TN = (((0,), (0,)), ((), ()))


def mm(left, right, dims=NN):
    return lax.dot_general(left, right, dims, preferred_element_type=F32)


def sigmoid(value):
    return 0.5 * jnp.tanh(0.5 * value) + 0.5


def softplus(value):
    return jnp.maximum(value, 0.0) + jnp.log1p(jnp.exp(-jnp.abs(value)))


def iota(shape, dim):
    return lax.broadcasted_iota(jnp.int32, shape, dim)


def split_two(value):
    high = value.astype(BF16)
    return high, (value - high.astype(F32)).astype(BF16)


def split_three(value):
    high = value.astype(BF16)
    rest = value - high.astype(F32)
    mid = rest.astype(BF16)
    return high, mid, (rest - mid.astype(F32)).astype(BF16)


def fold_rows(value):
    rows = value.shape[0]
    return jnp.sum(value.reshape(rows // 8, 8, value.shape[1]), 0)


def doc_of(places, e0, e1):
    return (places >= e0).astype(jnp.int32) + (places >= e1).astype(jnp.int32)


def same_behind(places, steps, e0, e1):
    crossed = ((places >= e0) & (places < e0 + steps)) | ((places >= e1) & (places < e1 + steps))
    return jnp.where(crossed, 0.0, 1.0)


def same_ahead(places, steps, e0, e1):
    crossed = ((places < e0) & (places >= e0 - steps)) | ((places < e1) & (places >= e1 - steps))
    return jnp.where(crossed, 0.0, 1.0)


def chunk_decays(log_decay, tri):
    high, mid, low = split_three(log_decay)
    cum = mm(jnp.concatenate([tri, tri, tri], 1), jnp.concatenate([high, mid, low], 0))
    return cum, cum.T


def column(values, at):
    return jnp.broadcast_to(values[:, at : at + 1], (values.shape[0], LANES))


def conv_tile(ubuf, cp, tile, rows, masks):
    lanes = slice(tile * LANES, (tile + 1) * LANES)
    summed = cp[4:5, lanes] + cp[3:4, lanes] * ubuf[8 : 8 + rows, lanes]
    for steps in (1, 2, 3):
        shifted = ubuf[8 - steps : 8 - steps + rows, lanes] * masks[steps - 1]
        summed = summed + cp[3 - steps : 4 - steps, lanes] * shifted
    return summed


def bring(out, blocks, step, sec, ten, order):
    half = out.shape[0] // 2
    mine = pl.multiple_of(sec * half, half)
    theirs = pl.multiple_of((1 - sec) * half, half)
    far = (jnp.bitwise_xor(ten, step) >> (1 - order)) & 1
    width = out.shape[1]
    for k in range(2):

        @pl.when(far == k)
        def _(k=k):
            out[pl.ds(mine, half), :] = blocks[k][0, :, :width]
            out[pl.ds(theirs, half), :] = blocks[2 + k][0, :, :width]


def piece_spec(shape, order):
    return pl.BlockSpec(
        (1,) + shape[1:], lambda i, sc: ((jnp.bitwise_xor(sc[1], i) >> order) & 1, 0, 0)
    )


def shard_place(at, k):
    place = at - k if k < 4 else at + (k - 3)
    return place, (place >= 0) & (place < 4)


def fwd_kernel(with_dot, shards, inner, state, heads, order, sc, *refs):
    gathered = order is None
    pieces, refs = (refs[:1], refs[1:]) if gathered else (refs[:4], refs[4:])
    if shards > 1:
        parts, refs, whole_w = refs[:shards], refs[shards:-1], refs[-1]

        @pl.when(pl.program_id(0) == 0)
        def _():
            size = parts[0].shape[0]
            for k in range(shards):
                place, held = shard_place(sc[4], k)

                @pl.when(held)
                def _(k=k, place=place):
                    whole_w[pl.ds(pl.multiple_of(place * size, size), size), :] = parts[k][...]

        refs = (whole_w, *refs)
    w, cp, hp, chp, live = refs[:5]
    refs = refs[5:]
    if with_dot:
        gno, refs = refs[0], refs[1:]
    if gathered:
        nrm = pieces[0]
    else:
        nrm, refs = refs[0], refs[1:]
    proj, y_out, st, gated_out, stats, carry, ubuf, act = refs
    step = pl.program_id(0)
    sec, ten, e0, e1 = sc[0], sc[1], sc[2], sc[3]
    rows = nrm.shape[0]
    wide = inner + 2 * state
    tiles = wide // LANES
    pairs = inner // LANES

    @pl.when(step == 0)
    def _():
        carry[...] = jnp.zeros_like(carry)
        ubuf[0:8, :] = jnp.zeros((8, wide), F32)

    if not gathered:
        bring(nrm, pieces, step, sec, ten, order)
    proj[...] = mm(nrm[...], w[...])
    lv = live[...]
    dt_at = slice(inner + wide, inner + wide + LANES)
    offset = ten * (2 * heads) + sec * heads
    proj[:, dt_at] = pltpu.roll(proj[:, dt_at], (LANES - offset) % LANES, 1) + hp[0:1, :]
    places = rows * step + iota((rows, LANES), 0)
    masks = [same_behind(places, steps, e0, e1) for steps in (1, 2, 3)]
    for tile in range(tiles):
        lanes = slice(tile * LANES, (tile + 1) * LANES)
        at = slice(inner + tile * LANES, inner + (tile + 1) * LANES)
        u = proj[:, at] * lv
        proj[:, at] = u
        ubuf[8 : 8 + rows, lanes] = u
    for tile in range(tiles):
        lanes = slice(tile * LANES, (tile + 1) * LANES)
        pre = conv_tile(ubuf, cp, tile, rows, masks)
        act[:, lanes] = (pre * sigmoid(pre)).astype(BF16)
    ubuf[0:8, :] = ubuf[rows : rows + 8, :]

    low_half = iota((CHUNK, LANES), 1) < HEAD
    tri = (iota((CHUNK, CHUNK), 0) >= iota((CHUNK, CHUNK), 1)).astype(F32).astype(BF16)
    gated_sq = []
    gated_dot = []
    for c in range(rows // CHUNK):
        r0 = c * CHUNK
        at = slice(r0, r0 + CHUNK)
        base = rows * step + r0
        t_at = base + iota((CHUNK, CHUNK), 0)
        s_at = base + iota((CHUNK, CHUNK), 1)
        id_t = doc_of(t_at, e0, e1)
        usable = (t_at >= s_at) & (id_t == doc_of(s_at, e0, e1))
        id_prev = doc_of(base - 1, e0, e1)
        id_end = doc_of(base + CHUNK - 1, e0, e1)
        from_prev = jnp.where(id_t == id_prev, 1.0, 0.0)
        tail_same = jnp.where(id_t == id_end, 1.0, 0.0)
        linked = jnp.where(id_end == id_prev, 1.0, 0.0).astype(F32)
        dt = softplus(proj[at, dt_at]) * live[at, :]
        cum, cum_t = chunk_decays(dt * hp[1:2, :], tri)
        b_in = act[at, inner : inner + state]
        c_in = act[at, inner + state : wide]
        scores = jnp.where(usable, mm(c_in, b_in, NT), 0.0)
        sq = jnp.zeros((CHUNK, LANES), F32)
        rd = jnp.zeros((CHUNK, LANES), F32)
        for k in range(pairs):
            lanes = slice(k * LANES, (k + 1) * LANES)
            mixed, fine, cums = [], [], []
            for h in (2 * k, 2 * k + 1):
                cum_col = column(cum, h)
                cums.append(cum_col)
                decay = jnp.exp(jnp.minimum(cum_col - cum_t[h : h + 1, :], 0.0))
                high, low = split_two(decay * scores)
                mixed.append(high)
                fine.append(low)
            cum_e = jnp.where(low_half, cums[0], cums[1])
            dt_e = jnp.where(low_half, column(dt, 2 * k), column(dt, 2 * k + 1))
            x_in = act[at, lanes].astype(F32)
            xdt = x_in * dt_e
            both = jnp.concatenate([jnp.where(low_half, xdt, 0.0), jnp.where(low_half, 0.0, xdt)], 0)
            both, both_low = split_two(both)
            mixed = jnp.concatenate(mixed, 1)
            within = mm(mixed, both)
            old = carry[:, lanes]
            old_high, old_low = split_two(old)
            st[c, :, lanes] = old_high
            entering = jnp.exp(cum_e) * from_prev
            across = mm(c_in, old_high) * entering
            cum_end = cum_e[CHUNK - 1 : CHUNK, :]
            to_end = jnp.exp(cum_end - cum_e) * tail_same
            if with_dot:
                added = mm(b_in, (xdt * to_end).astype(BF16), TN)
            else:
                into = jnp.concatenate(split_two(xdt * to_end), 0)
                added = mm(jnp.concatenate([b_in, b_in], 0), into, TN)
            carry[:, lanes] = old * (jnp.exp(cum_end) * linked) + added
            y = within + across + chp[0:1, lanes] * x_in
            y_out[at, lanes] = y
            if not with_dot:
                y = y + mm(jnp.concatenate(fine, 1), both) + mm(mixed, both_low)
                y = y + mm(c_in, old_low) * entering
            gate = proj[at, lanes]
            gated = y * (gate * sigmoid(gate))
            gated_out[at, lanes] = gated
            sq = sq + gated * gated
            if with_dot:
                rd = rd + gated * chp[1:2, lanes] * gno[at, lanes]
        gated_sq.append(sq)
        gated_dot.append(rd)
    ones = jnp.ones((8, LANES), F32)
    exact = partial(
        lax.dot_general,
        dimension_numbers=NT,
        precision=lax.Precision.HIGHEST,
        preferred_element_type=F32,
    )
    total = exact(ones, jnp.concatenate(gated_sq, 0))
    if with_dot:
        dots = exact(ones, jnp.concatenate(gated_dot, 0))
        total = jnp.where(iota((8, rows), 0) == 0, total, dots)
    stats[...] = total


def call(kernel, name, scalars, grid, ins, outs, scratch, deps, flops, extra, moved):
    count = len(ins)
    specs = [spec for spec, _ in ins] + [pl.BlockSpec(memory_space=pl.ANY)] * len(deps)

    def body(sc, *refs):
        kernel(sc, *refs[:count], *refs[count + len(deps) :])

    return pl.pallas_call(
        body,
        out_shape=tuple(jax.ShapeDtypeStruct(shape, kind) for _, shape, kind in outs),
        grid_spec=pltpu.PrefetchScalarGridSpec(
            num_scalar_prefetch=1,
            grid=grid,
            in_specs=specs,
            out_specs=tuple(spec for spec, _, _ in outs),
            scratch_shapes=scratch,
        ),
        compiler_params=pltpu.CompilerParams(
            dimension_semantics=("arbitrary",) * len(grid), vmem_limit_bytes=VMEM_LIMIT
        ),
        cost_estimate=pl.CostEstimate(flops=flops, transcendentals=extra, bytes_accessed=moved),
        name=name,
    )(scalars, *[operand for _, operand in ins], *deps)


def whole(shape):
    return pl.BlockSpec(shape, lambda i, sc: (0,) * len(shape))


def fixed(array):
    return (whole(array.shape), array)


def bring_coef(out, blocks, width, step, sec, ten, order):
    half = out.shape[0] // 2
    mine = pl.multiple_of(sec * half, half)
    theirs = pl.multiple_of((1 - sec) * half, half)
    far = (jnp.bitwise_xor(ten, step) >> (1 - order)) & 1
    for k in range(2):

        @pl.when(far == k)
        def _(k=k):
            for at, block in ((mine, blocks[k]), (theirs, blocks[2 + k])):
                parts = block[0, :, width:].astype(F32)
                total = parts[:, 0:1] + parts[:, 1:2] + parts[:, 2:3]
                out[pl.ds(at, half), :] = jnp.broadcast_to(total, (half, LANES))


def turn_kernel(count, sc, *refs):
    parts, wo_t, w_t, wo = refs[:count], *refs[count:]
    if count == 1:
        w_t[...] = parts[0][...].T
    else:
        for k in range(count):
            place, held = shard_place(sc[4], k)

            @pl.when(held & (place == pl.program_id(0)))
            def _(k=k):
                w_t[...] = parts[k][...].T

    wo[...] = wo_t[...].T


def run_turn(scalars, parts, wo_t, deps):
    depth, cols = wo_t.shape[0], parts[0].shape[1]
    rows = depth // 4
    by_row = lambda n: pl.BlockSpec((rows, n), lambda i, sc: (i, 0))
    by_col = lambda n: pl.BlockSpec((n, rows), lambda i, sc: (0, i))
    if len(parts) == 1:
        ins = [(by_row(cols), parts[0])]
    else:
        ins = [fixed(part) for part in parts]
    return call(
        partial(turn_kernel, len(parts)), "turn_weights", scalars, (4,),
        ins + [(by_row(wo_t.shape[1]), wo_t)],
        [
            (by_col(cols), (cols, depth), BF16),
            (by_col(wo_t.shape[1]), (wo_t.shape[1], depth), BF16),
        ],
        [], deps, 4 * 1024**3, 0, 10 * 1024 * 1024,
    )


def outer_kernel(count, start, sc, *refs):
    total = mm(refs[0][...], refs[1][...], TN)
    for k in range(1, count):
        total = total + mm(refs[2 * k][...], refs[2 * k + 1][...], TN)
    if start:
        total = total + refs[2 * count][...]
    refs[-1][...] = total.astype(refs[-1].dtype)


def run_outer(scalars, pairs, start, tall, kind, deps):
    depth = pairs[0][0].shape[0]
    rows, cols = pairs[0][0].shape[1], pairs[0][1].shape[1]
    tile = 3 * LANES if tall else 4 * LANES
    cut = pl.BlockSpec((depth, tile), lambda i, sc: (0, i))
    if tall:
        grid, out = (rows // tile,), pl.BlockSpec((tile, cols), lambda i, sc: (i, 0))
        ins = [item for a, b in pairs for item in ((cut, a), fixed(b))]
    else:
        grid, out = (cols // tile,), pl.BlockSpec((rows, tile), lambda i, sc: (0, i))
        ins = [item for a, b in pairs for item in (fixed(a), (cut, b))]
    if start is not None:
        ins.append((out, start))
    return call(
        partial(outer_kernel, len(pairs), start is not None), "outer_rows", scalars, grid, ins,
        [(out, (rows, cols), kind)], [], deps, 9 * 1024**3 * len(pairs), 0, 16 * 1024 * 1024,
    )[0]


def join_kernel(sc, mine, theirs, out):
    half = mine.shape[1]
    out[0, pl.ds(sc[0] * half, half), 0, :] = mine[0]
    out[0, pl.ds((1 - sc[0]) * half, half), 0, :] = theirs[0]


def run_join(scalars, mine, theirs):
    count, half, width = mine.shape
    spec = pl.BlockSpec((1, half, width), lambda i, sc: (i, 0, 0))
    return call(
        join_kernel, "join_rows", scalars, (count,), [(spec, mine), (spec, theirs)],
        [
            (
                pl.BlockSpec((1, 2 * half, 1, width), lambda i, sc: (i, 0, 0, 0)),
                (count, 2 * half, 1, width),
                F32,
            )
        ],
        [], [], 0, 0, 16 * 1024 * 1024,
    )[0]


def weave_kernel(sc, mine, theirs, out):
    size = mine.shape[1] // 2
    own = pl.ds(pl.multiple_of(sc[0] * size, LANES), size)
    other = pl.ds(pl.multiple_of((1 - sc[0]) * size, LANES), size)
    for k in range(2):
        out[:, k, own] = mine[:, k * size : (k + 1) * size].astype(F32)
        out[:, k, other] = theirs[:, k * size : (k + 1) * size].astype(F32)


def run_weave(scalars, mine, theirs):
    depth, width = mine.shape
    rows = depth if depth % 32 else depth // 4
    spec = pl.BlockSpec((rows, width), lambda i, sc: (i, 0))
    return call(
        weave_kernel, "weave_cols", scalars, (depth // rows,), [(spec, mine), (spec, theirs)],
        [(pl.BlockSpec((rows, 2, width), lambda i, sc: (i, 0, 0)), (depth, 2, width), F32)],
        [], [], 0, 0, 5 * 1024 * 1024,
    )[0]


def run_fwd(scalars, pieces, order, w, cp, hp, chp, live, gno, inner, state, heads, deps):
    width = pieces[0].shape[-1]
    length = live.shape[0]
    steps = 4
    rows = length // steps
    cols = w[0].shape[1]
    chunks = rows // CHUNK
    by_row = lambda n: pl.BlockSpec((rows, n), lambda i, sc: (i, 0))
    if order is None:
        ins, outs = [(by_row(width), pieces[0])], []
    else:
        ins = [(piece_spec(piece.shape, order), piece) for piece in pieces]
        outs = [(by_row(width), (length, width), BF16)]
    ins += [fixed(part) for part in w]
    ins += [fixed(cp), fixed(hp), fixed(chp), (by_row(LANES), live)]
    joined = [pltpu.VMEM((width, cols), BF16)] if len(w) > 1 else []
    if gno is not None:
        ins.append((by_row(inner), gno))
    return call(
        partial(fwd_kernel, gno is not None, len(w), inner, state, heads, order), "layer_fwd", scalars, (steps,),
        ins,
        outs
        + [
            (by_row(cols), (length, cols), F32),
            (by_row(inner), (length, inner), F32),
            (pl.BlockSpec((chunks, state, inner), lambda i, sc: (i, 0, 0)), (length // CHUNK, state, inner), BF16),
            (by_row(inner), (length, inner), F32),
            (pl.BlockSpec((8, rows), lambda i, sc: (0, i)), (8, length), F32),
        ],
        [
            pltpu.VMEM((state, inner), F32),
            pltpu.VMEM((rows + 8, inner + 2 * state), F32),
            pltpu.VMEM((rows, inner + 2 * state), BF16),
        ]
        + joined,
        deps, 24 * 1024**3, length * inner * 8, 24 * 1024**2,
    )


def scale_kernel(inner_width, sc, gated, s0, s1, s2, s3, chp, no_out, send, rc):
    rows = gated.shape[0]
    half = rows // 2
    theirs = pl.multiple_of((1 - sc[0]) * half, half)
    total = (s0[...] + s1[...]) + (s2[...] + s3[...])
    inv = lax.rsqrt(total / inner_width + EPS)
    coef = jnp.concatenate([total[1:8], total[0:1]], 0) * (inv * inv * inv) / inner_width
    both = jnp.where(iota(total.shape, 0) == 0, inv, pltpu.roll(coef, 1, 0))
    for c in range(rows // CHUNK):
        at = slice(c * CHUNK, (c + 1) * CHUNK)
        cols = jnp.concatenate([both[:, at]] * (CHUNK // 8), 0).T
        rc[at, :] = cols
        col = column(cols, 0)
        for k in range(gated.shape[1] // LANES):
            lanes = slice(k * LANES, (k + 1) * LANES)
            no_out[at, lanes] = (gated[at, lanes] * col * chp[1:2, lanes]).astype(BF16)
    send[0] = no_out[pl.ds(theirs, half), :]


def run_scale(scalars, gated, sums, chp, rows, inner_width, deps):
    length, inner = gated.shape
    steps = length // rows
    by_row = lambda n: pl.BlockSpec((rows, n), lambda i, sc: (i, 0))
    by_lane = pl.BlockSpec((8, rows), lambda i, sc: (0, i))
    return call(
        partial(scale_kernel, inner_width), "scale_rows", scalars, (steps,),
        [(by_row(inner), gated)] + [(by_lane, part) for part in sums] + [fixed(chp)],
        [
            (by_row(inner), (length, inner), BF16),
            (pl.BlockSpec((1, rows // 2, inner), lambda i, sc: (i, 0, 0)), (steps, rows // 2, inner), BF16),
            (by_row(LANES), (length, LANES), F32),
        ],
        [], deps, 4 * 1024**3, 0, 8 * 1024**2,
    )


def bwd_kernel(inner, state, heads, order, sc, *refs):
    if order is None:
        gno, cc, proj, halo, y_in, st, rc, live, cp, hp, chp = refs[:11]
        refs = refs[11:]
    else:
        pieces, wo_t = refs[:4], refs[4]
        proj, halo, y_in, st, rc, live, cp, hp, chp = refs[5:14]
        gout, gno, cc = refs[14], refs[-2], refs[-1]
        refs = refs[15:-2]
    gz, gzsend, gpack, dstate, ubuf, gbuf, acc_c, acc_h, acc_n, acc_d = refs
    step = pl.program_id(0)
    steps = pl.num_programs(0)
    block = steps - 1 - step
    sec, ten, e0, e1 = sc[0], sc[1], sc[2], sc[3]
    offset = ten * (2 * heads) + sec * heads
    rows = y_in.shape[0]
    half = rows // 2
    wide = inner + 2 * state
    tiles = wide // LANES
    pairs = inner // LANES
    theirs = pl.multiple_of((1 - sec) * half, half)

    @pl.when(step == 0)
    def _():
        dstate[...] = jnp.zeros_like(dstate)
        gbuf[rows : rows + 8, :] = jnp.zeros((8, wide), F32)
        acc_c[...] = jnp.zeros_like(acc_c)
        acc_h[...] = jnp.zeros_like(acc_h)
        acc_n[...] = jnp.zeros_like(acc_n)
        acc_d[...] = jnp.zeros_like(acc_d)

    if order is not None:
        bring(gout, pieces, block, sec, ten, order)
        bring_coef(cc, pieces, gout.shape[1], block, sec, ten, order)
        gno[...] = mm(gout[...], wo_t[...])

    ubuf[0:8, :] = jnp.where(block == 0, 0.0, halo[:, inner : inner + wide])
    ubuf[8 : 8 + rows, :] = proj[:, inner : inner + wide]
    places = rows * block + iota((rows, LANES), 0)
    masks = [same_behind(places, steps_, e0, e1) for steps_ in (1, 2, 3)]

    low_half = iota((CHUNK, LANES), 1) < HEAD
    row_at = iota((CHUNK, CHUNK), 0)
    col_at = iota((CHUNK, CHUNK), 1)
    tri = (row_at >= col_at).astype(F32).astype(BF16)
    tri_rev = (row_at <= col_at).astype(F32).astype(BF16)
    tri_strict = (row_at > col_at).astype(F32).astype(BF16)
    sums = jnp.concatenate([tri_rev, tri_rev, tri_strict, tri_strict], 1)
    to_head = [
        (iota((LANES, LANES), 1) == 2 * k + (iota((LANES, LANES), 0) >= HEAD).astype(jnp.int32))
        .astype(F32)
        .astype(BF16)
        for k in range(pairs)
    ]

    for c in reversed(range(rows // CHUNK)):
        r0 = c * CHUNK
        at = slice(r0, r0 + CHUNK)
        cmasks = [m[at, :] for m in masks]
        acts, slopes = [], []
        for tile in range(tiles):
            lanes = slice(tile * LANES, (tile + 1) * LANES)
            pre = cp[4:5, lanes] + cp[3:4, lanes] * ubuf[8 + r0 : 8 + r0 + CHUNK, lanes]
            for n in (1, 2, 3):
                shifted = ubuf[8 + r0 - n : 8 + r0 - n + CHUNK, lanes] * cmasks[n - 1]
                pre = pre + cp[3 - n : 4 - n, lanes] * shifted
            sig = sigmoid(pre)
            acts.append((pre * sig).astype(BF16))
            slopes.append(sig * (1.0 + pre * (1.0 - sig)))
        b_in, c_in = acts[pairs], acts[pairs + 1]
        base = rows * block + r0
        id_s = doc_of(base + row_at, e0, e1)
        usable = (row_at <= col_at) & (id_s == doc_of(base + col_at, e0, e1))
        id_prev = doc_of(base - 1, e0, e1)
        id_end = doc_of(base + CHUNK - 1, e0, e1)
        from_prev = jnp.where(id_s == id_prev, 1.0, 0.0)
        tail_same = jnp.where(id_s == id_end, 1.0, 0.0)
        linked = jnp.where(id_end == id_prev, 1.0, 0.0).astype(F32)
        lv = live[at, :]
        dt_in = proj[at, inner + wide : inner + wide + LANES]
        dt = softplus(dt_in) * lv
        log_decay = dt * hp[1:2, :]
        cum, cum_t = chunk_decays(log_decay, tri)
        scores = jnp.where(usable, mm(b_in, c_in, NT), 0.0)
        inv = column(rc[at, :], 0)
        coef = column(cc[at, :], 1)
        d_scores = jnp.zeros((CHUNK, CHUNK), F32)
        gb = jnp.zeros((CHUNK, state), F32)
        gc = jnp.zeros((CHUNK, state), F32)
        r1 = jnp.zeros((CHUNK, LANES), F32)
        r2 = jnp.zeros((CHUNK, LANES), F32)
        r3 = jnp.zeros((CHUNK, LANES), F32)
        kept = jnp.zeros((8, LANES), F32)
        for k in range(pairs):
            lanes = slice(k * LANES, (k + 1) * LANES)
            gate = proj[at, lanes]
            sig = sigmoid(gate)
            silu = gate * sig
            y = y_in[at, lanes]
            gated = y * silu
            g_no = gno[at, lanes]
            gain = chp[1:2, lanes]
            skip = chp[0:1, lanes]
            scaled = gated * inv
            acc_n[:, lanes] += fold_rows(g_no * scaled)
            gg = inv * (g_no * gain) - gated * coef
            gy = gg * silu
            gz[at, lanes] = (gg * y * (sig * (1.0 + gate * (1.0 - sig)))).astype(BF16)
            x_in = acts[k].astype(F32)
            acc_d[:, lanes] += fold_rows(gy * x_in)
            dt_e = jnp.where(low_half, column(dt, 2 * k), column(dt, 2 * k + 1))
            gy_b = gy.astype(BF16)
            gy_f = gy_b.astype(F32)
            xdt_b = (x_in * dt_e).astype(BF16)
            xdt_f = xdt_b.astype(F32)
            gy_halves = [jnp.where(low_half, gy_f, 0.0).astype(BF16), jnp.where(low_half, 0.0, gy_f).astype(BF16)]
            mixed, cums = [], []
            for n in (0, 1):
                h = 2 * k + n
                cum_col = column(cum, h)
                cums.append(cum_col)
                decay = jnp.exp(jnp.minimum(cum_t[h : h + 1, :] - cum_col, 0.0))
                mixed.append((decay * scores).astype(BF16))
                d_scores = d_scores + decay * mm(xdt_b, gy_halves[n], NT)
            cum_e = jnp.where(low_half, cums[0], cums[1])
            gx_in = mm(jnp.concatenate(mixed, 1), jnp.concatenate(gy_halves, 0))
            cum_end = cum_e[CHUNK - 1 : CHUNK, :]
            to_end = jnp.exp(cum_end - cum_e) * tail_same
            entering = jnp.exp(cum_e) * from_prev
            s_in = st[c, :, lanes]
            d_out = dstate[:, lanes]
            d_out_b = d_out.astype(BF16)
            gx_st = mm(b_in, d_out_b) * to_end
            gb = gb + mm((xdt_f * to_end).astype(BF16), d_out_b, NT)
            gye = (gy * entering).astype(BF16)
            gc = gc + mm(gye, s_in, NT)
            dec = jnp.exp(cum_end) * linked
            prod = fold_rows(s_in.astype(F32) * d_out) * dec
            p_hi, p_lo = split_two(prod)
            kept = kept + mm(p_hi, to_head[k]) + mm(p_lo, to_head[k])
            dstate[:, lanes] = d_out * dec + mm(c_in, gye, TN)
            gx = gx_in + gx_st
            t_hi, t_lo = split_two(gy_f * (y - skip * x_in) - xdt_f * gx_in)
            pair2 = jnp.concatenate([to_head[k], to_head[k]], 0)
            r1 = r1 + mm(jnp.concatenate([t_hi, t_lo], 1), pair2)
            t_hi, t_lo = split_two(x_in * gx)
            r2 = r2 + mm(jnp.concatenate([t_hi, t_lo], 1), pair2)
            t_hi, t_lo = split_two(x_in * gx_st)
            r3 = r3 + mm(jnp.concatenate([t_hi, t_lo], 1), pair2)
            gbuf[at, lanes] = (gx * dt_e + gy * skip) * slopes[k]
        d_scores = jnp.where(usable, d_scores, 0.0).astype(BF16)
        gb = gb + mm(d_scores, c_in)
        gc = gc + mm(d_scores, b_in, TN)
        for n in range(state // LANES):
            b_at = slice(inner + n * LANES, inner + (n + 1) * LANES)
            c_at = slice(inner + state + n * LANES, inner + state + (n + 1) * LANES)
            gbuf[at, b_at] = gb * slopes[pairs]
            gbuf[at, c_at] = gc * slopes[pairs + 1]
        a_hi, a_lo = split_two(r1)
        b_hi, b_lo = split_two(dt * r3)
        g_ld = mm(sums, jnp.concatenate([a_hi, a_lo, b_hi, b_lo], 0)) + jnp.sum(kept, 0, keepdims=True)
        g_dt = (r2 + g_ld * hp[1:2, :]) * (sigmoid(dt_in) * lv)
        acc_h[0:8, :] += fold_rows(g_dt)
        acc_h[8:16, :] += fold_rows(g_ld * log_decay)
        gz[at, inner + wide : inner + wide + LANES] = pltpu.roll(g_dt, offset, 1).astype(BF16)

    ahead = [same_ahead(places, n, e0, e1) for n in (1, 2, 3)]
    lv = live[...]
    for tile in range(tiles):
        lanes = slice(tile * LANES, (tile + 1) * LANES)
        gp = gbuf[0:rows, lanes]
        gu = cp[3:4, lanes] * gp
        acc_c[24:32, lanes] += fold_rows(gp * ubuf[8 : 8 + rows, lanes])
        acc_c[32:40, lanes] += fold_rows(gp)
        for n in (1, 2, 3):
            gu = gu + cp[3 - n : 4 - n, lanes] * (gbuf[n : n + rows, lanes] * ahead[n - 1])
            shifted = ubuf[8 - n : 8 - n + rows, lanes] * masks[n - 1]
            acc_c[8 * (3 - n) : 8 * (4 - n), lanes] += fold_rows(gp * shifted)
        at = slice(inner + tile * LANES, inner + (tile + 1) * LANES)
        gz[:, at] = (gu * lv).astype(BF16)
    gbuf[rows : rows + 8, :] = gbuf[0:8, :]
    gzsend[0] = gz[pl.ds(theirs, half), :]

    @pl.when(step == steps - 1)
    def _():
        gpack[...] = jnp.zeros_like(gpack)
        own = pl.ds(pl.multiple_of(sec * inner, LANES), inner)
        for n in range(5):
            line = jnp.sum(acc_c[8 * n : 8 * n + 8, :], 0, keepdims=True)
            gpack[1 + n : 2 + n, own] = line[:, :inner]
            gpack[1 + n : 2 + n, 2 * inner : 2 * inner + 2 * state] = line[:, inner:]
        gpack[6:7, own] = jnp.sum(acc_n[...], 0, keepdims=True)
        skips = jnp.zeros((8, LANES), F32)
        for k in range(pairs):
            d_hi, d_mid, d_low = split_three(acc_d[:, k * LANES : (k + 1) * LANES])
            skips = skips + (mm(d_hi, to_head[k]) + mm(d_mid, to_head[k]) + mm(d_low, to_head[k]))
        heads_sums = [acc_h[0:8, :], acc_h[8:16, :], skips]
        for n in range(3):
            line = jnp.sum(pltpu.roll(heads_sums[n], sec * heads, 1), 0, keepdims=True)
            gpack[7 + n : 8 + n, 0:LANES] = line


def run_bwd(scalars, rows_in, order, proj, y, st, rc, live, cp, hp, chp, inner, state, heads, rows, width, deps):
    length, cols = proj.shape
    steps = length // rows
    half = rows // 2
    chunks = rows // CHUNK
    wide = inner + 2 * state
    back = lambda i: steps - 1 - i
    by_row = lambda n: pl.BlockSpec((rows, n), lambda i, sc: (back(i), 0))
    halo = pl.BlockSpec((8, cols), lambda i, sc: (jnp.maximum(back(i) * (rows // 8) - 1, 0), 0))
    scratch = [
        pltpu.VMEM((state, inner), F32),
        pltpu.VMEM((rows + 8, wide), F32),
        pltpu.VMEM((rows + 8, wide), F32),
        pltpu.VMEM((40, wide), F32),
        pltpu.VMEM((16, LANES), F32),
        pltpu.VMEM((8, inner), F32),
        pltpu.VMEM((8, inner), F32),
    ]
    if order is None:
        gno, cc = rows_in
        ins, outs = [(by_row(inner), gno), (by_row(LANES), cc)], []
    else:
        pieces, wo_t = rows_in
        shape = pieces[0].shape
        spec = pl.BlockSpec(
            (1,) + shape[1:],
            lambda i, sc: ((jnp.bitwise_xor(sc[1], back(i)) >> order) & 1, 0, 0),
        )
        ins = [(spec, piece) for piece in pieces] + [fixed(wo_t)]
        outs = [(by_row(width), (length, width), BF16)]
        scratch += [pltpu.VMEM((rows, inner), F32), pltpu.VMEM((rows, LANES), F32)]
    ins += [
        (by_row(cols), proj),
        (halo, proj),
        (by_row(inner), y),
        (pl.BlockSpec((chunks, state, inner), lambda i, sc: (back(i), 0, 0)), st),
        (by_row(LANES), rc),
        (by_row(LANES), live),
        fixed(cp),
        fixed(hp),
        fixed(chp),
    ]
    outs += [
        (by_row(cols), (length, cols), BF16),
        (pl.BlockSpec((1, half, cols), lambda i, sc: (back(i), 0, 0)), (steps, half, cols), BF16),
        (whole((16, width)), (16, width), F32),
    ]
    return call(
        partial(bwd_kernel, inner, state, heads, order), "layer_bwd", scalars, (steps,),
        ins, outs, scratch, deps, 28 * 1024**3, length * inner * 12, 24 * 1024**2,
    )


def gn_kernel(order, sc, *refs):
    pieces, w, gno, gout = refs[:4], refs[4], refs[5], refs[6]
    step, sec, ten = pl.program_id(0), sc[0], sc[1]
    bring(gout, pieces, step, sec, ten, order)
    if len(refs) > 7:
        bring_coef(refs[7], pieces, gout.shape[1], step, sec, ten, order)
    gno[...] = mm(gout[...], w[...])


def run_gn(scalars, pieces, order, w, width, deps):
    half, cols = pieces[0].shape[1:]
    inner = w.shape[1]
    rows, length = 2 * half, 8 * half
    by_row = lambda n: pl.BlockSpec((rows, n), lambda i, sc: (i, 0))
    outs = [(by_row(inner), (length, inner), F32), (by_row(width), (length, width), BF16)]
    if cols > width:
        outs.append((by_row(LANES), (length, LANES), F32))
    return call(
        partial(gn_kernel, order), "grad_rows", scalars, (length // rows,),
        [(piece_spec(piece.shape, order), piece) for piece in pieces] + [fixed(w)],
        outs, [], deps, 8 * 1024**3, 0, 18 * 1024**2,
    )


def half_kernel(axis, sc, kept, got, wa, wb, *outs):
    half = got.shape[1]
    if axis:
        groups = [jnp.bitwise_xor(sc[1], k) for k in (0, 3 - axis, axis, 3)]
        left = jnp.concatenate([kept[g, 0] for g in groups], 0)
        right = jnp.concatenate([got[g] for g in groups], 0)
    else:
        kept1, got1, *outs = outs
        left = jnp.concatenate([ref[g, 0] for g in range(4) for ref in (kept, kept1)], 0)
        right = jnp.concatenate([ref[g] for g in range(4) for ref in (got, got1)], 0)
    total = mm(jnp.concatenate([left, right], 1), jnp.concatenate([wa[...], wb[...]], 0))
    if axis:
        own, near, far = outs
        own[...] = total[:half]
        near[...] = total[half : 2 * half]
        far[0] = total[2 * half : 3 * half].astype(far.dtype)
        far[1] = total[3 * half :].astype(far.dtype)
    else:
        outs[0][...] = total.astype(BF16)


def run_half(scalars, full, got, wa, wb, axis, deps, more=None, kind=BF16):
    groups, half, depth = got.shape
    width = wa.shape[1]
    tile = 4 * LANES
    w_spec = pl.BlockSpec((depth, tile), lambda i, sc: (0, i))
    part = lambda n: pl.BlockSpec((n, tile), lambda i, sc: (0, i))
    if axis:
        outs = [
            (part(half), (half, width), F32),
            (part(half), (half, width), F32),
            (pl.BlockSpec((2, half, tile), lambda i, sc: (0, 0, i)), (2, half, width), kind),
        ]
    else:
        outs = [(part(2 * groups * half), (2 * groups * half, width), BF16)]
    own = lambda v: (
        pl.BlockSpec((groups, 1, half, depth), lambda i, sc: (0, sc[0], 0, 0)),
        v.reshape(groups, 2, half, depth),
    )
    ins = [own(full), fixed(got), (w_spec, wa), (w_spec, wb)]
    if more is not None:
        ins += [own(more[0]), fixed(more[1])]
    return call(
        partial(half_kernel, axis), "half_rows", scalars, (width // tile,), ins,
        outs, [], deps, 8 * 1024**3, 0, 10 * 1024**2,
    )


def norm_kernel(x, gain, out):
    v = x[...].astype(F32)
    inv = lax.rsqrt(jnp.mean(v * v, -1, keepdims=True) + EPS)
    out[...] = (v * inv * gain[0:1, :]).astype(BF16)


def final_kernel(total, x0, x1, out):
    out[0] = x0[...].astype(F32) + total[0].astype(F32)
    out[1] = x1[...].astype(F32) + total[1].astype(F32)


def owner_kernel(own, far, near, x, gain, h1, normed, kept):
    total = own[...] + far[0].astype(F32) + near[...].astype(F32)
    out = x[...].astype(F32) + total
    low = out.astype(BF16)
    h1[...] = low
    kept[...] = total
    v = low.astype(F32)
    inv = lax.rsqrt(jnp.mean(v * v, -1, keepdims=True) + EPS)
    normed[...] = (v * inv * gain[0:1, :]).astype(BF16)


def owner_back_kernel(last, inner_width, own, far, near, v_in, g_in, gain, *refs):
    g = own[...] + far[0].astype(F32) + near[...].astype(F32)
    v = v_in[...].astype(F32)
    width = v.shape[1]
    inv = lax.rsqrt(jnp.mean(v * v, -1, keepdims=True) + EPS)
    scaled = v * inv
    p = g * gain[0:1, :]
    out = g_in[:, :width].astype(F32) + inv * (p - scaled * jnp.mean(p * scaled, -1, keepdims=True))
    if last:
        g_v, ggain = refs
        g_v[...] = out
    else:
        kept, rcol, g_v, ggain = refs
        low = out.astype(BF16)
        g_v[:, :width] = low
        r = rcol[:, 0:1]
        coef = r * r * jnp.sum(low.astype(F32) * kept[...], -1, keepdims=True) / inner_width
        shape = (v.shape[0], LANES)
        high, mid, small = [
            jnp.broadcast_to(part.astype(F32), shape) for part in split_three(coef)
        ]
        lane = iota(shape, 1)
        parts = jnp.where(lane == 0, high, jnp.where(lane == 1, mid, small))
        g_v[:, width:] = parts.astype(BF16)
    ggain[...] = jnp.zeros_like(ggain)
    ggain[0:1, :] = jnp.sum(g * scaled, 0, keepdims=True)


def run_plain(kernel, name, out_shape, operands, deps):
    count = len(operands)
    vmem = pl.BlockSpec(memory_space=pltpu.VMEM)

    def body(*refs):
        kernel(*refs[:count], *refs[count + len(deps) :])

    return pl.pallas_call(
        body,
        in_specs=[vmem] * count + [pl.BlockSpec(memory_space=pl.ANY)] * len(deps),
        out_shape=out_shape,
        compiler_params=pltpu.CompilerParams(vmem_limit_bytes=VMEM_LIMIT),
        cost_estimate=pl.CostEstimate(
            flops=3 * 1024**3, transcendentals=0, bytes_accessed=6 * 1024**2
        ),
        name=name,
    )(*operands, *deps)


def across(value, step):
    count = lax.axis_size("tensor")
    return lax.ppermute(value, "tensor", [(i, i ^ step) for i in range(count)])


def swap(value):
    return lax.ppermute(value, "section", [(0, 1), (1, 0)])


def reach(value, order):
    return value, across(value, 1 + order)


def widen(pair, order, *waits):
    near = jnp.stack([after(pair[0], *waits), pair[1]])
    return near, across(near, 2 - order)


def share(near, far):
    return [near, far, swap(near), swap(far)]


def spread(value, order):
    return share(*widen(reach(value, order), order))


def hand(outs, order):
    return outs[0], outs[1], across(outs[2], 2 - order)


def settle(held, order, *waits):
    own, near, far = held
    send = (after(near, *waits) + far[1].astype(F32)).astype(far.dtype)
    return (own, far, across(send, 1 + order)), send


def all_tensor(value):
    value = value + across(value, 1)
    return value + across(value, 2)


def cycle(value, steps):
    count = lax.axis_size("dp")
    return lax.ppermute(value, "dp", [(i, (i + steps) % count) for i in range(count)])


def pieces_dp(value):
    if lax.axis_size("dp") != 4:
        return [lax.all_gather(value, "dp", axis=0, tiled=True)]
    up, down = [value], [value]
    for _ in range(3):
        waits = (up[-1], down[-1])
        up.append(lax.ppermute(after(up[-1], *waits), "dp", [(i, i + 1) for i in range(3)]))
        down.append(lax.ppermute(after(down[-1], *waits), "dp", [(i + 1, i) for i in range(3)]))
    return up + down[1:]


def sum_dp(value, *waits):
    if lax.axis_size("dp") != 4:
        return lax.psum(value, "dp")
    got = [cycle(value, k) for k in (1, 2, 3)]
    return value + sum(after(part, *waits) for part in got)


def after(value, *waits):
    return lax.optimization_barrier((value, *waits))[0]


def on_device(
    x_in,
    d_out,
    doc_lengths,
    token_mask,
    gain_in,
    w_zx,
    w_bcdt,
    conv_x,
    conv_bc,
    dt_bias,
    a_log,
    d_skip,
    gain_inner,
    w_out,
):
    micro_count, local_rows, _, width = x_in.shape
    length = token_mask.shape[1]
    half = local_rows // 2
    rows = local_rows
    inner = conv_x.shape[2] // 2
    heads = dt_bias.shape[1] // 2
    state = conv_bc.shape[2] // 2
    chip_inner = 2 * inner
    full_inner = chip_inner * lax.axis_size("tensor")
    sec = lax.axis_index("section")
    ten = lax.axis_index("tensor")
    first = sec == 0
    micros = range(micro_count)

    def by_layer(own, other):
        return [jnp.where(first, own, other), jnp.where(first, other, own)]

    pad_to = lambda v, n: jnp.pad(v, ((0, 0), (0, n - v.shape[1])))
    pack = jnp.concatenate(
        [
            gain_in,
            pad_to(jnp.concatenate([conv_x[0], conv_bc[0]], 1), width),
            pad_to(gain_inner, width),
            pad_to(jnp.concatenate([dt_bias, a_log, d_skip], 1), width),
        ],
        0,
    )
    packs = by_layer(pack, swap(pack))
    gains = [jnp.broadcast_to(p[0:1], (8, width)) for p in packs]

    gate_w, x_w = w_zx[0, :, 0, :], w_zx[0, :, 1, :]
    ends = [jnp.concatenate([gate_w[:, at], x_w[:, at]], 1) for at in (slice(inner), slice(inner, None))]
    zx_own, zx_send = by_layer(*ends)
    bc_own = pad_to(w_bcdt[0], 2 * state + LANES)
    got = swap(jnp.concatenate([zx_send, bc_own], 1))
    zx_shards = by_layer(jnp.concatenate([zx_own, bc_own], 1), got)
    wo_own, wo_send = by_layer(w_out[0, :inner].T, w_out[0, inner:].T)
    wo_shards = by_layer(wo_own, swap(wo_send))
    first_parts = pieces_dp(zx_shards[0])

    rows_at = lambda v, m: jnp.where(first, v[m, :half, 0, :], v[m, half:, 0, :])
    early_in = (first_parts[1], first_parts[4]) if len(first_parts) > 1 else (zx_shards[0],)
    xs = [rows_at(after(x_in, *(early_in if m else zx_shards[:1])), m) for m in micros]
    gs = [rows_at(d_out, m) for m in micros]
    wide = lambda kind, n=0: jax.ShapeDtypeStruct((half, width + n), kind)
    small = jax.ShapeDtypeStruct((16, width), F32)
    rows_of = lambda v: lax.all_gather(v, ("tensor", "section"), axis=0, tiled=True)
    pieces0 = [
        [rows_of(run_plain(norm_kernel, "norm_rows", wide(BF16), (xs[m], gains[0]), ()))]
        for m in micros
    ]
    later = lambda v: lax.all_gather(after(v, *first_parts), "dp", axis=0, tiled=True)
    wo_t0, wo_t1 = later(wo_shards[0]), later(wo_shards[1])
    w1 = later(zx_shards[1])

    doc_lengths, token_mask, *packs = lax.optimization_barrier(
        (doc_lengths, token_mask, *packs, *early_in)
    )[:4]
    scalars, lives = [], []
    for m in micros:
        e0 = doc_lengths[m, 0, 0]
        e1 = e0 + doc_lengths[m, 0, 1]
        scalars.append(jnp.stack([sec, ten, e0, e1, lax.axis_index("dp")]).astype(jnp.int32))
        lives.append(jnp.broadcast_to(token_mask[m].astype(F32), (length, LANES)))
    places = scalars[0]

    layers = []
    for layer in range(2):
        p = packs[layer]
        pick = lambda row, start, count: jnp.where(
            first, p[row : row + 1, start : start + count],
            p[row : row + 1, start + count : start + 2 * count],
        )
        taps = jnp.concatenate(
            [
                jnp.where(first, p[1:6, :inner], p[1:6, inner:chip_inner]),
                p[1:6, chip_inner : chip_inner + 2 * state],
            ],
            1,
        )
        cp = jnp.pad(taps, ((0, 3), (0, 0)))
        bias = pad_to(pick(7, 0, heads), LANES)
        rate = pad_to(-jnp.exp(pick(7, 2 * heads, heads)), LANES)
        hp = jnp.concatenate([bias, rate, jnp.zeros((6, LANES), F32)], 0)
        skip = jnp.broadcast_to(pick(7, 4 * heads, heads).reshape(heads, 1), (heads, HEAD))
        chp = jnp.concatenate(
            [skip.reshape(1, inner), pick(6, 0, inner), jnp.zeros((6, inner), F32)], 0
        )
        layers.append(dict(cp=cp, hp=hp, chp=chp))
    early, late = layers

    def fwd(k, m, pieces, gno, deps, *waits):
        order = None if len(pieces) == 1 else 0
        *nrm, proj, y, st, gated, stats = run_fwd(
            scalars[m], pieces, order, k["w"], k["cp"], k["hp"], k["chp"], lives[m], gno,
            inner, state, heads, deps,
        )
        held = after(stats, *waits)
        part = held + swap(held)
        sums = [part] + [across(part, n) for n in (1, 2, 3)]
        nrm = nrm[0] if nrm else pieces[0]
        return dict(nrm=nrm, proj=proj, y=y, st=st, gated=gated, stats=stats, sums=sums)

    def scale(k, m, r, deps):
        r["no"], send, r["rc"] = run_scale(
            scalars[m], r["gated"], r["sums"], k["chp"], rows, full_inner, deps
        )
        r["sent"] = swap(send)

    def project(k, m, r, deps, axis):
        return run_half(
            scalars[m], r["no"], r["sent"], k["wo"], k["wo_other"], axis, deps, kind=F32
        )

    def project_both(k, r0, r1, deps):
        return run_half(
            scalars[0], r0["no"], r0["sent"], k["wo"], k["wo_other"], 0, deps, (r1["no"], r1["sent"])
        )[0]

    def back(k, m, rows_in, order, r, deps, *waits):
        out = run_bwd(
            scalars[m], rows_in, order, r["proj"], r["y"], r["st"], r["rc"], lives[m],
            k["cp"], k["hp"], k["chp"], inner, state, heads, rows, width, deps,
        )
        gz, gzsend, gpack = out[-3:]
        return gz, swap(after(gzsend, *waits)), gpack, out[0]

    def unproject(k, m, gz, got, deps):
        return run_half(scalars[m], gz, got, k["w_t"], k["w_t_other"], 2, deps)

    def middle(m, parts, deps):
        return run_plain(
            owner_kernel, "owner_mid", (wide(BF16), wide(BF16), wide(F32)),
            (*parts, xs[m], gains[1]), deps,
        )

    early["w"], late["w"] = first_parts, [w1]
    near_g = [reach(after(gs[m], *first_parts), m) for m in micros]

    a0 = fwd(early, 0, pieces0[0], None, ())
    early["wo_t"], late["wo_t"] = wo_t0, wo_t1
    wide_g = [widen(near_g[m], m, a0["stats"]) for m in micros]
    a1 = fwd(early, 1, pieces0[1], None, [a0["stats"]] + [pair[1] for pair in near_g])
    early["wo"] = after(wo_t0, a1["stats"]).T
    early["wo_other"] = swap(early["wo"])
    scale(early, 0, a0, [a1["stats"]] + [pair[1] for pair in wide_g])
    pieces_g = [share(*wide_g[m]) for m in micros]
    outs0 = project(early, 0, a0, (), 2)
    held0 = hand(outs0, 0)
    scale(early, 1, a1, [outs0[0]])
    outs1 = project(early, 1, a1, (), 1)
    held1 = hand(outs1, 1)
    gno0, gout1_0 = run_gn(scalars[0], pieces_g[0], 0, late["wo_t"], width, [outs1[0]])
    parts0, sent0 = settle(held0, 0, gno0)
    gno1, gout1_1 = run_gn(scalars[1], pieces_g[1], 1, late["wo_t"], width, [gno0, sent0])
    parts1, sent1 = settle(held1, 1, gno1)
    h_0, normed_0, u_0 = middle(0, parts0, [gno1])
    pair0 = reach(normed_0, 0)
    h_1, normed_1, u_1 = middle(1, parts1, [normed_0])
    pair1 = reach(normed_1, 0)
    wide0 = widen(pair0, 0, normed_1)
    late["w_t"], late["wo"] = run_turn(places, late["w"], late["wo_t"], [wide0[0]])
    wide1 = widen(pair1, 0, late["wo"])
    early["w_t"], _ = run_turn(places, early["w"], early["wo_t"], [late["wo"], wide1[0]])
    late["wo_other"] = swap(after(late["wo"], wide1[0]))
    late["w_t_other"] = swap(after(late["w_t"], early["w_t"]))
    early["w_t_other"] = swap(early["w_t"])

    b0 = fwd(late, 0, share(wide0[0], after(wide0[1], early["w_t"])), gno0, [early["w_t"]], wide1[1])
    last1 = share(wide1[0], after(wide1[1], b0["stats"]))
    b1 = fwd(late, 1, last1, gno1, [b0["stats"]])
    scale(late, 0, b0, [b1["stats"], early["w_t_other"]])
    gz0, got0, pack0, _ = back(late, 0, (gno0, b0["rc"]), None, b0, [b0["no"], b1["sums"][0]], *b1["sums"][1:])
    scale(late, 1, b1, [pack0])
    outs0 = unproject(late, 0, gz0, got0, [b1["no"]])
    held0 = hand(outs0, 0)
    gz1, got1, pack1, _ = back(late, 1, (gno1, b1["rc"]), None, b1, [outs0[0]])
    parts0, sent0 = settle(held0, 0, pack1)
    g_wo1 = run_outer(
        places, [(gout1_0, b0["no"]), (gout1_1, b1["no"])], None, True, BF16, [pack1, sent0]
    )
    outs1 = unproject(late, 1, gz1, got1, [g_wo1])
    held1 = hand(outs1, 0)

    own_at = ten * rows + sec * half
    rcol = lambda r: lax.dynamic_slice_in_dim(r["rc"], own_at, half, 0)

    def turn(m, parts, h, u, r, deps):
        return run_plain(
            partial(owner_back_kernel, False, full_inner), "owner_back",
            (wide(BF16, LANES), small), (*parts, h, gs[m], gains[1], u, rcol(r)), deps,
        )

    gh_0, gain1_0 = turn(0, parts0, h_0, u_0, a0, [outs1[0]])
    pair0 = reach(gh_0, 0)
    w1_out = run_outer(
        places, [(b0["nrm"], gz0), (b1["nrm"], gz1)], None, True, BF16, [gh_0]
    )
    parts1, sent1 = settle(held1, 0, w1_out, pair0[1])
    wide0 = widen(pair0, 0, w1_out, sent1)
    final = project_both(late, b0, b1, [w1_out, sent1, wide0[0]])
    gh_1, gain1_1 = turn(1, parts1, h_1, u_1, a1, [final])
    pair1 = reach(gh_1, 0)
    turned0 = share(wide0[0], after(wide0[1], gh_1))
    spill = lambda g, axis: lax.psum_scatter(g, "dp", scatter_dimension=axis, tiled=True)
    wo1_sum = spill(g_wo1, 0)
    w1_sum = spill(after(w1_out, sent1), 0)
    over_tensor = lambda v: lax.psum_scatter(v, "tensor", scatter_dimension=0, tiled=True)
    sums = over_tensor(after(final, gh_1))
    tiny1 = pack0 + pack1 + gain1_0 + gain1_1

    wide1 = widen(pair1, 0)
    gz0, got0, pack0, gout0_0 = back(
        early, 0, (turned0, early["wo_t"]), 0, a0, [gh_1, wo1_sum, wide1[0]], wide1[1]
    )
    outs0 = unproject(early, 0, gz0, got0, [pack0, wide1[0]])
    held0 = hand(outs0, 0)
    g_w0 = run_outer(places, [(a0["nrm"], gz0)], None, True, F32, [outs0[0]])
    turned1 = share(wide1[0], after(wide1[1], g_w0))
    gno0_1, gout0_1, cc0_1 = run_gn(scalars[1], turned1, 0, early["wo_t"], width, [g_w0, w1_sum])
    gz1, got1, pack1, _ = back(early, 1, (gno0_1, cc0_1), None, a1, [gno0_1])
    w0_out = run_outer(places, [(a1["nrm"], gz1)], g_w0, True, BF16, [pack1, held0[2]])
    w0_sum = spill(w0_out, 0)
    outs1 = unproject(early, 1, gz1, got1, [w0_out])
    held1 = hand(outs1, 0)
    parts0, _ = settle(held0, 0, pack1)
    g_wo0 = run_outer(
        places, [(gout0_0, a0["no"]), (gout0_1, a1["no"])], None, True, BF16, [outs1[0]]
    )
    wo0_sum = spill(after(g_wo0, w0_sum), 0)
    parts1, sent1 = settle(held1, 0, g_wo0)

    def last(m, parts, gh, deps):
        return run_plain(
            partial(owner_back_kernel, True, full_inner), "owner_last", (wide(F32), small),
            (*parts, xs[m], gh, gains[0]), deps,
        )

    gv_0, gain0_0 = last(0, parts0, gh_0, [sent1, g_wo0])
    finals = run_plain(
        final_kernel, "owner_out", jax.ShapeDtypeStruct((2, half, width), F32),
        (sums.reshape(2, half, width), h_0, h_1), [gv_0],
    )
    out_act = run_join(places, finals, swap(finals))
    gv_1, gain0_1 = last(1, parts1, gh_1, [out_act])
    tiny0 = pack0 + pack1 + gain0_0 + gain0_1

    both = jnp.stack([gv_0, gv_1])
    mine, theirs = by_layer(both[:, :, : width // 2], both[:, :, width // 2 :])
    grad_in = run_join(places, mine, swap(theirs))

    def owned(parts):
        kept, sent = by_layer(parts[0], parts[1])
        return kept, swap(sent)

    kept, got = owned([v[:, : 2 * inner] for v in (w0_sum, w1_sum)])
    grad_w_zx = run_weave(places, kept, got)[None]
    kept, sent = by_layer(tiny0, tiny1)
    mine = sum_dp(kept + swap(sent), grad_in, grad_w_zx)
    shared = all_tensor(mine)
    grad_w_out = jnp.concatenate(by_layer(*owned([wo0_sum, wo1_sum])), 1).T[None].astype(F32)
    cut = lambda v: after(v, got)[:, 2 * inner : 2 * inner + w_bcdt.shape[2]]
    kept, got = owned([cut(v) for v in (w0_sum, w1_sum)])
    shard = kept.astype(F32) + got.astype(F32)
    for bit in (1, 2):
        shard = shard + across(shard.astype(BF16), bit).astype(F32)
    grad_w_bcdt = shard[None]
    return (
        out_act,
        grad_in,
        shared[0:1],
        grad_w_zx,
        grad_w_bcdt,
        mine[None, 1:6, :chip_inner],
        shared[None, 1:6, chip_inner : chip_inner + 2 * state],
        mine[7:8, : 2 * heads],
        mine[8:9, : 2 * heads],
        mine[9:10, : 2 * heads],
        mine[6:7, :chip_inner],
        grad_w_out,
    )


def solution(mesh):
    return jax.shard_map(
        on_device,
        mesh=mesh,
        in_specs=(
            P(None, "tensor", "dp", None),
            P(None, "tensor", "dp", None),
            P(None, "dp", None),
            P(None, None, "dp"),
            P("section", None),
            P("section", "dp", None, "tensor"),
            P("section", "dp", None),
            P("section", None, "tensor"),
            P("section", None, None),
            P("section", "tensor"),
            P("section", "tensor"),
            P("section", "tensor"),
            P("section", "tensor"),
            P("section", "tensor", "dp"),
        ),
        out_specs=(
            P(None, "tensor", "dp", None),
            P(None, "tensor", "dp", "section"),
            P("section", None),
            P("section", "dp", None, "tensor"),
            P("section", "dp", None),
            P("section", None, "tensor"),
            P("section", None, None),
            P("section", "tensor"),
            P("section", "tensor"),
            P("section", "tensor"),
            P("section", "tensor"),
            P("section", "tensor", "dp"),
        ),
        check_vma=False,
    )
```

```python
from functools import partial

import jax
import jax.numpy as jnp
from jax import lax
from jax.experimental import pallas as pl
from jax.experimental.pallas import tpu as pltpu
from jax.sharding import PartitionSpec as P

EPS = 1e-05
F32 = jnp.float32
BF16 = jnp.bfloat16
HEAD = 64
CHUNK = 128
LANES = 128
VMEM_LIMIT = 56 * 1024 * 1024
NN = (((1,), (0,)), ((), ()))
NT = (((1,), (1,)), ((), ()))
TN = (((0,), (0,)), ((), ()))


def mm(left, right, dims=NN):
    return lax.dot_general(left, right, dims, preferred_element_type=F32)


def sigmoid(value):
    return 0.5 * jnp.tanh(0.5 * value) + 0.5


def softplus(value):
    return jnp.maximum(value, 0.0) + jnp.log1p(jnp.exp(-jnp.abs(value)))


def iota(shape, dim):
    return lax.broadcasted_iota(jnp.int32, shape, dim)


def split_two(value):
    high = value.astype(BF16)
    return high, (value - high.astype(F32)).astype(BF16)


def split_three(value):
    high = value.astype(BF16)
    rest = value - high.astype(F32)
    mid = rest.astype(BF16)
    return high, mid, (rest - mid.astype(F32)).astype(BF16)


def fold_rows(value):
    rows = value.shape[0]
    return jnp.sum(value.reshape(rows // 8, 8, value.shape[1]), 0)


def doc_of(places, e0, e1):
    return (places >= e0).astype(jnp.int32) + (places >= e1).astype(jnp.int32)


def same_behind(places, steps, e0, e1):
    crossed = ((places >= e0) & (places < e0 + steps)) | ((places >= e1) & (places < e1 + steps))
    return jnp.where(crossed, 0.0, 1.0)


def same_ahead(places, steps, e0, e1):
    crossed = ((places < e0) & (places >= e0 - steps)) | ((places < e1) & (places >= e1 - steps))
    return jnp.where(crossed, 0.0, 1.0)


def chunk_decays(log_decay, tri):
    high, mid, low = split_three(log_decay)
    cum = mm(jnp.concatenate([tri, tri, tri], 1), jnp.concatenate([high, mid, low], 0))
    return cum, cum.T


def column(values, at):
    return jnp.broadcast_to(values[:, at : at + 1], (values.shape[0], LANES))


def conv_tile(ubuf, cp, tile, rows, masks):
    lanes = slice(tile * LANES, (tile + 1) * LANES)
    summed = cp[4:5, lanes] + cp[3:4, lanes] * ubuf[8 : 8 + rows, lanes]
    for steps in (1, 2, 3):
        shifted = ubuf[8 - steps : 8 - steps + rows, lanes] * masks[steps - 1]
        summed = summed + cp[3 - steps : 4 - steps, lanes] * shifted
    return summed


def bring(out, blocks, step, sec, ten, order):
    half = out.shape[0] // 2
    mine = pl.multiple_of(sec * half, half)
    theirs = pl.multiple_of((1 - sec) * half, half)
    far = (jnp.bitwise_xor(ten, step) >> (1 - order)) & 1
    width = out.shape[1]
    for k in range(2):

        @pl.when(far == k)
        def _(k=k):
            out[pl.ds(mine, half), :] = blocks[k][0, :, :width]
            out[pl.ds(theirs, half), :] = blocks[2 + k][0, :, :width]


def piece_spec(shape, order):
    return pl.BlockSpec(
        (1,) + shape[1:], lambda i, sc: ((jnp.bitwise_xor(sc[1], i) >> order) & 1, 0, 0)
    )


def shard_place(at, k):
    place = at - k if k < 4 else at + (k - 3)
    return place, (place >= 0) & (place < 4)


def fwd_kernel(with_dot, shards, inner, state, heads, order, sc, *refs):
    gathered = order is None
    pieces, refs = (refs[:1], refs[1:]) if gathered else (refs[:4], refs[4:])
    if shards > 1:
        parts, refs, whole_w = refs[:shards], refs[shards:-1], refs[-1]

        @pl.when(pl.program_id(0) == 0)
        def _():
            size = parts[0].shape[0]
            for k in range(shards):
                place, held = shard_place(sc[4], k)

                @pl.when(held)
                def _(k=k, place=place):
                    whole_w[pl.ds(pl.multiple_of(place * size, size), size), :] = parts[k][...]

        refs = (whole_w, *refs)
    w, cp, hp, chp, live = refs[:5]
    refs = refs[5:]
    if with_dot:
        gno, refs = refs[0], refs[1:]
    if gathered:
        nrm = pieces[0]
    else:
        nrm, refs = refs[0], refs[1:]
    proj, y_out, st, gated_out, stats, carry, ubuf, act = refs
    step = pl.program_id(0)
    sec, ten, e0, e1 = sc[0], sc[1], sc[2], sc[3]
    rows = nrm.shape[0]
    wide = inner + 2 * state
    tiles = wide // LANES
    pairs = inner // LANES

    @pl.when(step == 0)
    def _():
        carry[...] = jnp.zeros_like(carry)
        ubuf[0:8, :] = jnp.zeros((8, wide), F32)

    if not gathered:
        bring(nrm, pieces, step, sec, ten, order)
    proj[...] = mm(nrm[...], w[...])
    lv = live[...]
    dt_at = slice(inner + wide, inner + wide + LANES)
    offset = ten * (2 * heads) + sec * heads
    proj[:, dt_at] = pltpu.roll(proj[:, dt_at], (LANES - offset) % LANES, 1) + hp[0:1, :]
    places = rows * step + iota((rows, LANES), 0)
    masks = [same_behind(places, steps, e0, e1) for steps in (1, 2, 3)]
    for tile in range(tiles):
        lanes = slice(tile * LANES, (tile + 1) * LANES)
        at = slice(inner + tile * LANES, inner + (tile + 1) * LANES)
        u = proj[:, at] * lv
        proj[:, at] = u
        ubuf[8 : 8 + rows, lanes] = u
    for tile in range(tiles):
        lanes = slice(tile * LANES, (tile + 1) * LANES)
        pre = conv_tile(ubuf, cp, tile, rows, masks)
        act[:, lanes] = (pre * sigmoid(pre)).astype(BF16)
    ubuf[0:8, :] = ubuf[rows : rows + 8, :]

    low_half = iota((CHUNK, LANES), 1) < HEAD
    tri = (iota((CHUNK, CHUNK), 0) >= iota((CHUNK, CHUNK), 1)).astype(F32).astype(BF16)
    gated_sq = []
    gated_dot = []
    for c in range(rows // CHUNK):
        r0 = c * CHUNK
        at = slice(r0, r0 + CHUNK)
        base = rows * step + r0
        t_at = base + iota((CHUNK, CHUNK), 0)
        s_at = base + iota((CHUNK, CHUNK), 1)
        id_t = doc_of(t_at, e0, e1)
        usable = (t_at >= s_at) & (id_t == doc_of(s_at, e0, e1))
        id_prev = doc_of(base - 1, e0, e1)
        id_end = doc_of(base + CHUNK - 1, e0, e1)
        from_prev = jnp.where(id_t == id_prev, 1.0, 0.0)
        tail_same = jnp.where(id_t == id_end, 1.0, 0.0)
        linked = jnp.where(id_end == id_prev, 1.0, 0.0).astype(F32)
        dt = softplus(proj[at, dt_at]) * live[at, :]
        cum, cum_t = chunk_decays(dt * hp[1:2, :], tri)
        b_in = act[at, inner : inner + state]
        c_in = act[at, inner + state : wide]
        scores = jnp.where(usable, mm(c_in, b_in, NT), 0.0)
        sq = jnp.zeros((CHUNK, LANES), F32)
        rd = jnp.zeros((CHUNK, LANES), F32)
        for k in range(pairs):
            lanes = slice(k * LANES, (k + 1) * LANES)
            mixed, fine, cums = [], [], []
            for h in (2 * k, 2 * k + 1):
                cum_col = column(cum, h)
                cums.append(cum_col)
                decay = jnp.exp(jnp.minimum(cum_col - cum_t[h : h + 1, :], 0.0))
                high, low = split_two(decay * scores)
                mixed.append(high)
                fine.append(low)
            cum_e = jnp.where(low_half, cums[0], cums[1])
            dt_e = jnp.where(low_half, column(dt, 2 * k), column(dt, 2 * k + 1))
            x_in = act[at, lanes].astype(F32)
            xdt = x_in * dt_e
            both = jnp.concatenate([jnp.where(low_half, xdt, 0.0), jnp.where(low_half, 0.0, xdt)], 0)
            both, both_low = split_two(both)
            mixed = jnp.concatenate(mixed, 1)
            within = mm(mixed, both)
            old = carry[:, lanes]
            old_high, old_low = split_two(old)
            st[c, :, lanes] = old_high
            entering = jnp.exp(cum_e) * from_prev
            across = mm(c_in, old_high) * entering
            cum_end = cum_e[CHUNK - 1 : CHUNK, :]
            to_end = jnp.exp(cum_end - cum_e) * tail_same
            if with_dot:
                added = mm(b_in, (xdt * to_end).astype(BF16), TN)
            else:
                into = jnp.concatenate(split_two(xdt * to_end), 0)
                added = mm(jnp.concatenate([b_in, b_in], 0), into, TN)
            carry[:, lanes] = old * (jnp.exp(cum_end) * linked) + added
            y = within + across + chp[0:1, lanes] * x_in
            y_out[at, lanes] = y
            if not with_dot:
                y = y + mm(jnp.concatenate(fine, 1), both) + mm(mixed, both_low)
                y = y + mm(c_in, old_low) * entering
            gate = proj[at, lanes]
            gated = y * (gate * sigmoid(gate))
            gated_out[at, lanes] = gated
            sq = sq + gated * gated
            if with_dot:
                rd = rd + gated * chp[1:2, lanes] * gno[at, lanes]
        gated_sq.append(sq)
        gated_dot.append(rd)
    ones = jnp.ones((8, LANES), F32)
    exact = partial(
        lax.dot_general,
        dimension_numbers=NT,
        precision=lax.Precision.HIGHEST,
        preferred_element_type=F32,
    )
    total = exact(ones, jnp.concatenate(gated_sq, 0))
    if with_dot:
        dots = exact(ones, jnp.concatenate(gated_dot, 0))
        total = jnp.where(iota((8, rows), 0) == 0, total, dots)
    stats[...] = total


def call(kernel, name, scalars, grid, ins, outs, scratch, deps, flops, extra, moved):
    count = len(ins)
    specs = [spec for spec, _ in ins] + [pl.BlockSpec(memory_space=pl.ANY)] * len(deps)

    def body(sc, *refs):
        kernel(sc, *refs[:count], *refs[count + len(deps) :])

    return pl.pallas_call(
        body,
        out_shape=tuple(jax.ShapeDtypeStruct(shape, kind) for _, shape, kind in outs),
        grid_spec=pltpu.PrefetchScalarGridSpec(
            num_scalar_prefetch=1,
            grid=grid,
            in_specs=specs,
            out_specs=tuple(spec for spec, _, _ in outs),
            scratch_shapes=scratch,
        ),
        compiler_params=pltpu.CompilerParams(
            dimension_semantics=("arbitrary",) * len(grid), vmem_limit_bytes=VMEM_LIMIT
        ),
        cost_estimate=pl.CostEstimate(flops=flops, transcendentals=extra, bytes_accessed=moved),
        name=name,
    )(scalars, *[operand for _, operand in ins], *deps)


def whole(shape):
    return pl.BlockSpec(shape, lambda i, sc: (0,) * len(shape))


def fixed(array):
    return (whole(array.shape), array)


def bring_coef(out, blocks, width, step, sec, ten, order):
    half = out.shape[0] // 2
    mine = pl.multiple_of(sec * half, half)
    theirs = pl.multiple_of((1 - sec) * half, half)
    far = (jnp.bitwise_xor(ten, step) >> (1 - order)) & 1
    for k in range(2):

        @pl.when(far == k)
        def _(k=k):
            for at, block in ((mine, blocks[k]), (theirs, blocks[2 + k])):
                parts = block[0, :, width:].astype(F32)
                total = parts[:, 0:1] + parts[:, 1:2] + parts[:, 2:3]
                out[pl.ds(at, half), :] = jnp.broadcast_to(total, (half, LANES))


def turn_kernel(count, sc, *refs):
    parts, wo_t, w_t, wo = refs[:count], *refs[count:]
    if count == 1:
        w_t[...] = parts[0][...].T
    else:
        for k in range(count):
            place, held = shard_place(sc[4], k)

            @pl.when(held & (place == pl.program_id(0)))
            def _(k=k):
                w_t[...] = parts[k][...].T

    wo[...] = wo_t[...].T


def run_turn(scalars, parts, wo_t, deps):
    depth, cols = wo_t.shape[0], parts[0].shape[1]
    rows = depth // 4
    by_row = lambda n: pl.BlockSpec((rows, n), lambda i, sc: (i, 0))
    by_col = lambda n: pl.BlockSpec((n, rows), lambda i, sc: (0, i))
    if len(parts) == 1:
        ins = [(by_row(cols), parts[0])]
    else:
        ins = [fixed(part) for part in parts]
    return call(
        partial(turn_kernel, len(parts)), "turn_weights", scalars, (4,),
        ins + [(by_row(wo_t.shape[1]), wo_t)],
        [
            (by_col(cols), (cols, depth), BF16),
            (by_col(wo_t.shape[1]), (wo_t.shape[1], depth), BF16),
        ],
        [], deps, 4 * 1024**3, 0, 10 * 1024 * 1024,
    )


def outer_kernel(count, start, sc, *refs):
    total = mm(refs[0][...], refs[1][...], TN)
    for k in range(1, count):
        total = total + mm(refs[2 * k][...], refs[2 * k + 1][...], TN)
    if start:
        total = total + refs[2 * count][...]
    refs[-1][...] = total.astype(refs[-1].dtype)


def run_outer(scalars, pairs, start, tall, kind, deps):
    depth = pairs[0][0].shape[0]
    rows, cols = pairs[0][0].shape[1], pairs[0][1].shape[1]
    tile = 3 * LANES if tall else 4 * LANES
    cut = pl.BlockSpec((depth, tile), lambda i, sc: (0, i))
    if tall:
        grid, out = (rows // tile,), pl.BlockSpec((tile, cols), lambda i, sc: (i, 0))
        ins = [item for a, b in pairs for item in ((cut, a), fixed(b))]
    else:
        grid, out = (cols // tile,), pl.BlockSpec((rows, tile), lambda i, sc: (0, i))
        ins = [item for a, b in pairs for item in (fixed(a), (cut, b))]
    if start is not None:
        ins.append((out, start))
    return call(
        partial(outer_kernel, len(pairs), start is not None), "outer_rows", scalars, grid, ins,
        [(out, (rows, cols), kind)], [], deps, 9 * 1024**3 * len(pairs), 0, 16 * 1024 * 1024,
    )[0]


def join_kernel(sc, mine, theirs, out):
    half = mine.shape[1]
    out[0, pl.ds(sc[0] * half, half), 0, :] = mine[0]
    out[0, pl.ds((1 - sc[0]) * half, half), 0, :] = theirs[0]


def run_join(scalars, mine, theirs):
    count, half, width = mine.shape
    spec = pl.BlockSpec((1, half, width), lambda i, sc: (i, 0, 0))
    return call(
        join_kernel, "join_rows", scalars, (count,), [(spec, mine), (spec, theirs)],
        [
            (
                pl.BlockSpec((1, 2 * half, 1, width), lambda i, sc: (i, 0, 0, 0)),
                (count, 2 * half, 1, width),
                F32,
            )
        ],
        [], [], 0, 0, 16 * 1024 * 1024,
    )[0]


def weave_kernel(sc, mine, theirs, out):
    size = mine.shape[1] // 2
    own = pl.ds(pl.multiple_of(sc[0] * size, LANES), size)
    other = pl.ds(pl.multiple_of((1 - sc[0]) * size, LANES), size)
    for k in range(2):
        out[:, k, own] = mine[:, k * size : (k + 1) * size].astype(F32)
        out[:, k, other] = theirs[:, k * size : (k + 1) * size].astype(F32)


def run_weave(scalars, mine, theirs):
    depth, width = mine.shape
    rows = depth if depth % 32 else depth // 4
    spec = pl.BlockSpec((rows, width), lambda i, sc: (i, 0))
    return call(
        weave_kernel, "weave_cols", scalars, (depth // rows,), [(spec, mine), (spec, theirs)],
        [(pl.BlockSpec((rows, 2, width), lambda i, sc: (i, 0, 0)), (depth, 2, width), F32)],
        [], [], 0, 0, 5 * 1024 * 1024,
    )[0]


def run_fwd(scalars, pieces, order, w, cp, hp, chp, live, gno, inner, state, heads, deps):
    width = pieces[0].shape[-1]
    length = live.shape[0]
    steps = 4
    rows = length // steps
    cols = w[0].shape[1]
    chunks = rows // CHUNK
    by_row = lambda n: pl.BlockSpec((rows, n), lambda i, sc: (i, 0))
    if order is None:
        ins, outs = [(by_row(width), pieces[0])], []
    else:
        ins = [(piece_spec(piece.shape, order), piece) for piece in pieces]
        outs = [(by_row(width), (length, width), BF16)]
    ins += [fixed(part) for part in w]
    ins += [fixed(cp), fixed(hp), fixed(chp), (by_row(LANES), live)]
    joined = [pltpu.VMEM((width, cols), BF16)] if len(w) > 1 else []
    if gno is not None:
        ins.append((by_row(inner), gno))
    return call(
        partial(fwd_kernel, gno is not None, len(w), inner, state, heads, order), "layer_fwd", scalars, (steps,),
        ins,
        outs
        + [
            (by_row(cols), (length, cols), F32),
            (by_row(inner), (length, inner), F32),
            (pl.BlockSpec((chunks, state, inner), lambda i, sc: (i, 0, 0)), (length // CHUNK, state, inner), BF16),
            (by_row(inner), (length, inner), F32),
            (pl.BlockSpec((8, rows), lambda i, sc: (0, i)), (8, length), F32),
        ],
        [
            pltpu.VMEM((state, inner), F32),
            pltpu.VMEM((rows + 8, inner + 2 * state), F32),
            pltpu.VMEM((rows, inner + 2 * state), BF16),
        ]
        + joined,
        deps, 24 * 1024**3, length * inner * 8, 24 * 1024**2,
    )


def scale_kernel(inner_width, sc, gated, s0, s1, s2, s3, chp, no_out, send, rc):
    rows = gated.shape[0]
    half = rows // 2
    theirs = pl.multiple_of((1 - sc[0]) * half, half)
    total = (s0[...] + s1[...]) + (s2[...] + s3[...])
    inv = lax.rsqrt(total / inner_width + EPS)
    coef = jnp.concatenate([total[1:8], total[0:1]], 0) * (inv * inv * inv) / inner_width
    both = jnp.where(iota(total.shape, 0) == 0, inv, pltpu.roll(coef, 1, 0))
    for c in range(rows // CHUNK):
        at = slice(c * CHUNK, (c + 1) * CHUNK)
        cols = jnp.concatenate([both[:, at]] * (CHUNK // 8), 0).T
        rc[at, :] = cols
        col = column(cols, 0)
        for k in range(gated.shape[1] // LANES):
            lanes = slice(k * LANES, (k + 1) * LANES)
            no_out[at, lanes] = (gated[at, lanes] * col * chp[1:2, lanes]).astype(BF16)
    send[0] = no_out[pl.ds(theirs, half), :]


def run_scale(scalars, gated, sums, chp, rows, inner_width, deps):
    length, inner = gated.shape
    steps = length // rows
    by_row = lambda n: pl.BlockSpec((rows, n), lambda i, sc: (i, 0))
    by_lane = pl.BlockSpec((8, rows), lambda i, sc: (0, i))
    return call(
        partial(scale_kernel, inner_width), "scale_rows", scalars, (steps,),
        [(by_row(inner), gated)] + [(by_lane, part) for part in sums] + [fixed(chp)],
        [
            (by_row(inner), (length, inner), BF16),
            (pl.BlockSpec((1, rows // 2, inner), lambda i, sc: (i, 0, 0)), (steps, rows // 2, inner), BF16),
            (by_row(LANES), (length, LANES), F32),
        ],
        [], deps, 4 * 1024**3, 0, 8 * 1024**2,
    )


def bwd_kernel(inner, state, heads, order, sc, *refs):
    if order is None:
        gno, cc, proj, halo, y_in, st, rc, live, cp, hp, chp = refs[:11]
        refs = refs[11:]
    else:
        pieces, wo_t = refs[:4], refs[4]
        proj, halo, y_in, st, rc, live, cp, hp, chp = refs[5:14]
        gout, gno, cc = refs[14], refs[-2], refs[-1]
        refs = refs[15:-2]
    gz, gzsend, gpack, dstate, ubuf, gbuf, acc_c, acc_h, acc_n, acc_d = refs
    step = pl.program_id(0)
    steps = pl.num_programs(0)
    block = steps - 1 - step
    sec, ten, e0, e1 = sc[0], sc[1], sc[2], sc[3]
    offset = ten * (2 * heads) + sec * heads
    rows = y_in.shape[0]
    half = rows // 2
    wide = inner + 2 * state
    tiles = wide // LANES
    pairs = inner // LANES
    theirs = pl.multiple_of((1 - sec) * half, half)

    @pl.when(step == 0)
    def _():
        dstate[...] = jnp.zeros_like(dstate)
        gbuf[rows : rows + 8, :] = jnp.zeros((8, wide), F32)
        acc_c[...] = jnp.zeros_like(acc_c)
        acc_h[...] = jnp.zeros_like(acc_h)
        acc_n[...] = jnp.zeros_like(acc_n)
        acc_d[...] = jnp.zeros_like(acc_d)

    if order is not None:
        bring(gout, pieces, block, sec, ten, order)
        bring_coef(cc, pieces, gout.shape[1], block, sec, ten, order)
        gno[...] = mm(gout[...], wo_t[...])

    ubuf[0:8, :] = jnp.where(block == 0, 0.0, halo[:, inner : inner + wide])
    ubuf[8 : 8 + rows, :] = proj[:, inner : inner + wide]
    places = rows * block + iota((rows, LANES), 0)
    masks = [same_behind(places, steps_, e0, e1) for steps_ in (1, 2, 3)]

    low_half = iota((CHUNK, LANES), 1) < HEAD
    row_at = iota((CHUNK, CHUNK), 0)
    col_at = iota((CHUNK, CHUNK), 1)
    tri = (row_at >= col_at).astype(F32).astype(BF16)
    tri_rev = (row_at <= col_at).astype(F32).astype(BF16)
    tri_strict = (row_at > col_at).astype(F32).astype(BF16)
    sums = jnp.concatenate([tri_rev, tri_rev, tri_strict, tri_strict], 1)
    to_head = [
        (iota((LANES, LANES), 1) == 2 * k + (iota((LANES, LANES), 0) >= HEAD).astype(jnp.int32))
        .astype(F32)
        .astype(BF16)
        for k in range(pairs)
    ]

    for c in reversed(range(rows // CHUNK)):
        r0 = c * CHUNK
        at = slice(r0, r0 + CHUNK)
        cmasks = [m[at, :] for m in masks]
        acts, slopes = [], []
        for tile in range(tiles):
            lanes = slice(tile * LANES, (tile + 1) * LANES)
            pre = cp[4:5, lanes] + cp[3:4, lanes] * ubuf[8 + r0 : 8 + r0 + CHUNK, lanes]
            for n in (1, 2, 3):
                shifted = ubuf[8 + r0 - n : 8 + r0 - n + CHUNK, lanes] * cmasks[n - 1]
                pre = pre + cp[3 - n : 4 - n, lanes] * shifted
            sig = sigmoid(pre)
            acts.append((pre * sig).astype(BF16))
            slopes.append(sig * (1.0 + pre * (1.0 - sig)))
        b_in, c_in = acts[pairs], acts[pairs + 1]
        base = rows * block + r0
        id_s = doc_of(base + row_at, e0, e1)
        usable = (row_at <= col_at) & (id_s == doc_of(base + col_at, e0, e1))
        id_prev = doc_of(base - 1, e0, e1)
        id_end = doc_of(base + CHUNK - 1, e0, e1)
        from_prev = jnp.where(id_s == id_prev, 1.0, 0.0)
        tail_same = jnp.where(id_s == id_end, 1.0, 0.0)
        linked = jnp.where(id_end == id_prev, 1.0, 0.0).astype(F32)
        lv = live[at, :]
        dt_in = proj[at, inner + wide : inner + wide + LANES]
        dt = softplus(dt_in) * lv
        log_decay = dt * hp[1:2, :]
        cum, cum_t = chunk_decays(log_decay, tri)
        scores = jnp.where(usable, mm(b_in, c_in, NT), 0.0)
        inv = column(rc[at, :], 0)
        coef = column(cc[at, :], 1)
        d_scores = jnp.zeros((CHUNK, CHUNK), F32)
        gb = jnp.zeros((CHUNK, state), F32)
        gc = jnp.zeros((CHUNK, state), F32)
        r1 = jnp.zeros((CHUNK, LANES), F32)
        r2 = jnp.zeros((CHUNK, LANES), F32)
        r3 = jnp.zeros((CHUNK, LANES), F32)
        kept = jnp.zeros((8, LANES), F32)
        for k in range(pairs):
            lanes = slice(k * LANES, (k + 1) * LANES)
            gate = proj[at, lanes]
            sig = sigmoid(gate)
            silu = gate * sig
            y = y_in[at, lanes]
            gated = y * silu
            g_no = gno[at, lanes]
            gain = chp[1:2, lanes]
            skip = chp[0:1, lanes]
            scaled = gated * inv
            acc_n[:, lanes] += fold_rows(g_no * scaled)
            gg = inv * (g_no * gain) - gated * coef
            gy = gg * silu
            gz[at, lanes] = (gg * y * (sig * (1.0 + gate * (1.0 - sig)))).astype(BF16)
            x_in = acts[k].astype(F32)
            acc_d[:, lanes] += fold_rows(gy * x_in)
            dt_e = jnp.where(low_half, column(dt, 2 * k), column(dt, 2 * k + 1))
            gy_b = gy.astype(BF16)
            gy_f = gy_b.astype(F32)
            xdt_b = (x_in * dt_e).astype(BF16)
            xdt_f = xdt_b.astype(F32)
            gy_halves = [jnp.where(low_half, gy_f, 0.0).astype(BF16), jnp.where(low_half, 0.0, gy_f).astype(BF16)]
            mixed, cums = [], []
            for n in (0, 1):
                h = 2 * k + n
                cum_col = column(cum, h)
                cums.append(cum_col)
                decay = jnp.exp(jnp.minimum(cum_t[h : h + 1, :] - cum_col, 0.0))
                mixed.append((decay * scores).astype(BF16))
                d_scores = d_scores + decay * mm(xdt_b, gy_halves[n], NT)
            cum_e = jnp.where(low_half, cums[0], cums[1])
            gx_in = mm(jnp.concatenate(mixed, 1), jnp.concatenate(gy_halves, 0))
            cum_end = cum_e[CHUNK - 1 : CHUNK, :]
            to_end = jnp.exp(cum_end - cum_e) * tail_same
            entering = jnp.exp(cum_e) * from_prev
            s_in = st[c, :, lanes]
            d_out = dstate[:, lanes]
            d_out_b = d_out.astype(BF16)
            gx_st = mm(b_in, d_out_b) * to_end
            gb = gb + mm((xdt_f * to_end).astype(BF16), d_out_b, NT)
            gye = (gy * entering).astype(BF16)
            gc = gc + mm(gye, s_in, NT)
            dec = jnp.exp(cum_end) * linked
            prod = fold_rows(s_in.astype(F32) * d_out) * dec
            p_hi, p_lo = split_two(prod)
            kept = kept + mm(p_hi, to_head[k]) + mm(p_lo, to_head[k])
            dstate[:, lanes] = d_out * dec + mm(c_in, gye, TN)
            gx = gx_in + gx_st
            t_hi, t_lo = split_two(gy_f * (y - skip * x_in) - xdt_f * gx_in)
            pair2 = jnp.concatenate([to_head[k], to_head[k]], 0)
            r1 = r1 + mm(jnp.concatenate([t_hi, t_lo], 1), pair2)
            t_hi, t_lo = split_two(x_in * gx)
            r2 = r2 + mm(jnp.concatenate([t_hi, t_lo], 1), pair2)
            t_hi, t_lo = split_two(x_in * gx_st)
            r3 = r3 + mm(jnp.concatenate([t_hi, t_lo], 1), pair2)
            gbuf[at, lanes] = (gx * dt_e + gy * skip) * slopes[k]
        d_scores = jnp.where(usable, d_scores, 0.0).astype(BF16)
        gb = gb + mm(d_scores, c_in)
        gc = gc + mm(d_scores, b_in, TN)
        for n in range(state // LANES):
            b_at = slice(inner + n * LANES, inner + (n + 1) * LANES)
            c_at = slice(inner + state + n * LANES, inner + state + (n + 1) * LANES)
            gbuf[at, b_at] = gb * slopes[pairs]
            gbuf[at, c_at] = gc * slopes[pairs + 1]
        a_hi, a_lo = split_two(r1)
        b_hi, b_lo = split_two(dt * r3)
        g_ld = mm(sums, jnp.concatenate([a_hi, a_lo, b_hi, b_lo], 0)) + jnp.sum(kept, 0, keepdims=True)
        g_dt = (r2 + g_ld * hp[1:2, :]) * (sigmoid(dt_in) * lv)
        acc_h[0:8, :] += fold_rows(g_dt)
        acc_h[8:16, :] += fold_rows(g_ld * log_decay)
        gz[at, inner + wide : inner + wide + LANES] = pltpu.roll(g_dt, offset, 1).astype(BF16)

    ahead = [same_ahead(places, n, e0, e1) for n in (1, 2, 3)]
    lv = live[...]
    for tile in range(tiles):
        lanes = slice(tile * LANES, (tile + 1) * LANES)
        gp = gbuf[0:rows, lanes]
        gu = cp[3:4, lanes] * gp
        acc_c[24:32, lanes] += fold_rows(gp * ubuf[8 : 8 + rows, lanes])
        acc_c[32:40, lanes] += fold_rows(gp)
        for n in (1, 2, 3):
            gu = gu + cp[3 - n : 4 - n, lanes] * (gbuf[n : n + rows, lanes] * ahead[n - 1])
            shifted = ubuf[8 - n : 8 - n + rows, lanes] * masks[n - 1]
            acc_c[8 * (3 - n) : 8 * (4 - n), lanes] += fold_rows(gp * shifted)
        at = slice(inner + tile * LANES, inner + (tile + 1) * LANES)
        gz[:, at] = (gu * lv).astype(BF16)
    gbuf[rows : rows + 8, :] = gbuf[0:8, :]
    gzsend[0] = gz[pl.ds(theirs, half), :]

    @pl.when(step == steps - 1)
    def _():
        gpack[...] = jnp.zeros_like(gpack)
        own = pl.ds(pl.multiple_of(sec * inner, LANES), inner)
        for n in range(5):
            line = jnp.sum(acc_c[8 * n : 8 * n + 8, :], 0, keepdims=True)
            gpack[1 + n : 2 + n, own] = line[:, :inner]
            gpack[1 + n : 2 + n, 2 * inner : 2 * inner + 2 * state] = line[:, inner:]
        gpack[6:7, own] = jnp.sum(acc_n[...], 0, keepdims=True)
        skips = jnp.zeros((8, LANES), F32)
        for k in range(pairs):
            d_hi, d_mid, d_low = split_three(acc_d[:, k * LANES : (k + 1) * LANES])
            skips = skips + (mm(d_hi, to_head[k]) + mm(d_mid, to_head[k]) + mm(d_low, to_head[k]))
        heads_sums = [acc_h[0:8, :], acc_h[8:16, :], skips]
        for n in range(3):
            line = jnp.sum(pltpu.roll(heads_sums[n], sec * heads, 1), 0, keepdims=True)
            gpack[7 + n : 8 + n, 0:LANES] = line


def run_bwd(scalars, rows_in, order, proj, y, st, rc, live, cp, hp, chp, inner, state, heads, rows, width, deps):
    length, cols = proj.shape
    steps = length // rows
    half = rows // 2
    chunks = rows // CHUNK
    wide = inner + 2 * state
    back = lambda i: steps - 1 - i
    by_row = lambda n: pl.BlockSpec((rows, n), lambda i, sc: (back(i), 0))
    halo = pl.BlockSpec((8, cols), lambda i, sc: (jnp.maximum(back(i) * (rows // 8) - 1, 0), 0))
    scratch = [
        pltpu.VMEM((state, inner), F32),
        pltpu.VMEM((rows + 8, wide), F32),
        pltpu.VMEM((rows + 8, wide), F32),
        pltpu.VMEM((40, wide), F32),
        pltpu.VMEM((16, LANES), F32),
        pltpu.VMEM((8, inner), F32),
        pltpu.VMEM((8, inner), F32),
    ]
    if order is None:
        gno, cc = rows_in
        ins, outs = [(by_row(inner), gno), (by_row(LANES), cc)], []
    else:
        pieces, wo_t = rows_in
        shape = pieces[0].shape
        spec = pl.BlockSpec(
            (1,) + shape[1:],
            lambda i, sc: ((jnp.bitwise_xor(sc[1], back(i)) >> order) & 1, 0, 0),
        )
        ins = [(spec, piece) for piece in pieces] + [fixed(wo_t)]
        outs = [(by_row(width), (length, width), BF16)]
        scratch += [pltpu.VMEM((rows, inner), F32), pltpu.VMEM((rows, LANES), F32)]
    ins += [
        (by_row(cols), proj),
        (halo, proj),
        (by_row(inner), y),
        (pl.BlockSpec((chunks, state, inner), lambda i, sc: (back(i), 0, 0)), st),
        (by_row(LANES), rc),
        (by_row(LANES), live),
        fixed(cp),
        fixed(hp),
        fixed(chp),
    ]
    outs += [
        (by_row(cols), (length, cols), BF16),
        (pl.BlockSpec((1, half, cols), lambda i, sc: (back(i), 0, 0)), (steps, half, cols), BF16),
        (whole((16, width)), (16, width), F32),
    ]
    return call(
        partial(bwd_kernel, inner, state, heads, order), "layer_bwd", scalars, (steps,),
        ins, outs, scratch, deps, 28 * 1024**3, length * inner * 12, 24 * 1024**2,
    )


def gn_kernel(order, sc, *refs):
    pieces, w, gno, gout = refs[:4], refs[4], refs[5], refs[6]
    step, sec, ten = pl.program_id(0), sc[0], sc[1]
    bring(gout, pieces, step, sec, ten, order)
    if len(refs) > 7:
        bring_coef(refs[7], pieces, gout.shape[1], step, sec, ten, order)
    gno[...] = mm(gout[...], w[...])


def run_gn(scalars, pieces, order, w, width, deps):
    half, cols = pieces[0].shape[1:]
    inner = w.shape[1]
    rows, length = 2 * half, 8 * half
    by_row = lambda n: pl.BlockSpec((rows, n), lambda i, sc: (i, 0))
    outs = [(by_row(inner), (length, inner), F32), (by_row(width), (length, width), BF16)]
    if cols > width:
        outs.append((by_row(LANES), (length, LANES), F32))
    return call(
        partial(gn_kernel, order), "grad_rows", scalars, (length // rows,),
        [(piece_spec(piece.shape, order), piece) for piece in pieces] + [fixed(w)],
        outs, [], deps, 8 * 1024**3, 0, 18 * 1024**2,
    )


def half_kernel(axis, sc, kept, got, wa, wb, *outs):
    half = got.shape[1]
    if axis:
        groups = [jnp.bitwise_xor(sc[1], k) for k in (0, 3 - axis, axis, 3)]
        left = jnp.concatenate([kept[g, 0] for g in groups], 0)
        right = jnp.concatenate([got[g] for g in groups], 0)
    else:
        kept1, got1, *outs = outs
        left = jnp.concatenate([ref[g, 0] for g in range(4) for ref in (kept, kept1)], 0)
        right = jnp.concatenate([ref[g] for g in range(4) for ref in (got, got1)], 0)
    total = mm(jnp.concatenate([left, right], 1), jnp.concatenate([wa[...], wb[...]], 0))
    if axis:
        own, near, far = outs
        own[...] = total[:half]
        near[...] = total[half : 2 * half]
        far[0] = total[2 * half : 3 * half].astype(far.dtype)
        far[1] = total[3 * half :].astype(far.dtype)
    else:
        outs[0][...] = total.astype(BF16)


def run_half(scalars, full, got, wa, wb, axis, deps, more=None, kind=BF16):
    groups, half, depth = got.shape
    width = wa.shape[1]
    tile = 4 * LANES
    w_spec = pl.BlockSpec((depth, tile), lambda i, sc: (0, i))
    part = lambda n: pl.BlockSpec((n, tile), lambda i, sc: (0, i))
    if axis:
        outs = [
            (part(half), (half, width), F32),
            (part(half), (half, width), F32),
            (pl.BlockSpec((2, half, tile), lambda i, sc: (0, 0, i)), (2, half, width), kind),
        ]
    else:
        outs = [(part(2 * groups * half), (2 * groups * half, width), BF16)]
    own = lambda v: (
        pl.BlockSpec((groups, 1, half, depth), lambda i, sc: (0, sc[0], 0, 0)),
        v.reshape(groups, 2, half, depth),
    )
    ins = [own(full), fixed(got), (w_spec, wa), (w_spec, wb)]
    if more is not None:
        ins += [own(more[0]), fixed(more[1])]
    return call(
        partial(half_kernel, axis), "half_rows", scalars, (width // tile,), ins,
        outs, [], deps, 8 * 1024**3, 0, 10 * 1024**2,
    )


def norm_kernel(x, gain, out):
    v = x[...].astype(F32)
    inv = lax.rsqrt(jnp.mean(v * v, -1, keepdims=True) + EPS)
    out[...] = (v * inv * gain[0:1, :]).astype(BF16)


def final_kernel(total, x0, x1, out):
    out[0] = x0[...].astype(F32) + total[0].astype(F32)
    out[1] = x1[...].astype(F32) + total[1].astype(F32)


def owner_kernel(own, far, near, x, gain, h1, normed, kept):
    total = own[...] + far[0].astype(F32) + near[...].astype(F32)
    out = x[...].astype(F32) + total
    low = out.astype(BF16)
    h1[...] = low
    kept[...] = total
    v = low.astype(F32)
    inv = lax.rsqrt(jnp.mean(v * v, -1, keepdims=True) + EPS)
    normed[...] = (v * inv * gain[0:1, :]).astype(BF16)


def owner_back_kernel(last, inner_width, own, far, near, v_in, g_in, gain, *refs):
    g = own[...] + far[0].astype(F32) + near[...].astype(F32)
    v = v_in[...].astype(F32)
    width = v.shape[1]
    inv = lax.rsqrt(jnp.mean(v * v, -1, keepdims=True) + EPS)
    scaled = v * inv
    p = g * gain[0:1, :]
    out = g_in[:, :width].astype(F32) + inv * (p - scaled * jnp.mean(p * scaled, -1, keepdims=True))
    if last:
        g_v, ggain = refs
        g_v[...] = out
    else:
        kept, rcol, g_v, ggain = refs
        low = out.astype(BF16)
        g_v[:, :width] = low
        r = rcol[:, 0:1]
        coef = r * r * jnp.sum(low.astype(F32) * kept[...], -1, keepdims=True) / inner_width
        shape = (v.shape[0], LANES)
        high, mid, small = [
            jnp.broadcast_to(part.astype(F32), shape) for part in split_three(coef)
        ]
        lane = iota(shape, 1)
        parts = jnp.where(lane == 0, high, jnp.where(lane == 1, mid, small))
        g_v[:, width:] = parts.astype(BF16)
    ggain[...] = jnp.zeros_like(ggain)
    ggain[0:1, :] = jnp.sum(g * scaled, 0, keepdims=True)


def run_plain(kernel, name, out_shape, operands, deps):
    count = len(operands)
    vmem = pl.BlockSpec(memory_space=pltpu.VMEM)

    def body(*refs):
        kernel(*refs[:count], *refs[count + len(deps) :])

    return pl.pallas_call(
        body,
        in_specs=[vmem] * count + [pl.BlockSpec(memory_space=pl.ANY)] * len(deps),
        out_shape=out_shape,
        compiler_params=pltpu.CompilerParams(vmem_limit_bytes=VMEM_LIMIT),
        cost_estimate=pl.CostEstimate(
            flops=3 * 1024**3, transcendentals=0, bytes_accessed=6 * 1024**2
        ),
        name=name,
    )(*operands, *deps)


def across(value, step):
    count = lax.axis_size("tensor")
    return lax.ppermute(value, "tensor", [(i, i ^ step) for i in range(count)])


def swap(value):
    return lax.ppermute(value, "section", [(0, 1), (1, 0)])


def reach(value, order):
    return value, across(value, 1 + order)


def widen(pair, order, *waits):
    near = jnp.stack([after(pair[0], *waits), pair[1]])
    return near, across(near, 2 - order)


def share(near, far):
    return [near, far, swap(near), swap(far)]


def spread(value, order):
    return share(*widen(reach(value, order), order))


def hand(outs, order):
    return outs[0], outs[1], across(outs[2], 2 - order)


def settle(held, order, *waits):
    own, near, far = held
    send = (after(near, *waits) + far[1].astype(F32)).astype(far.dtype)
    return (own, far, across(send, 1 + order)), send


def all_tensor(value):
    return (value + across(value, 1)) + (across(value, 2) + across(value, 3))


def cycle(value, steps):
    count = lax.axis_size("dp")
    return lax.ppermute(value, "dp", [(i, (i + steps) % count) for i in range(count)])


def pieces_dp(value):
    if lax.axis_size("dp") != 4:
        return [lax.all_gather(value, "dp", axis=0, tiled=True)]
    up, down = [value], [value]
    for _ in range(3):
        waits = (up[-1], down[-1])
        up.append(lax.ppermute(after(up[-1], *waits), "dp", [(i, i + 1) for i in range(3)]))
        down.append(lax.ppermute(after(down[-1], *waits), "dp", [(i + 1, i) for i in range(3)]))
    return up + down[1:]


def sum_dp(value, *waits):
    if lax.axis_size("dp") != 4:
        return lax.psum(value, "dp")
    got = [cycle(value, k) for k in (1, 2, 3)]
    return value + sum(after(part, *waits) for part in got)


def after(value, *waits):
    return lax.optimization_barrier((value, *waits))[0]


def on_device(
    x_in,
    d_out,
    doc_lengths,
    token_mask,
    gain_in,
    w_zx,
    w_bcdt,
    conv_x,
    conv_bc,
    dt_bias,
    a_log,
    d_skip,
    gain_inner,
    w_out,
):
    micro_count, local_rows, _, width = x_in.shape
    length = token_mask.shape[1]
    half = local_rows // 2
    rows = local_rows
    inner = conv_x.shape[2] // 2
    heads = dt_bias.shape[1] // 2
    state = conv_bc.shape[2] // 2
    chip_inner = 2 * inner
    full_inner = chip_inner * lax.axis_size("tensor")
    sec = lax.axis_index("section")
    ten = lax.axis_index("tensor")
    first = sec == 0
    micros = range(micro_count)

    def by_layer(own, other):
        return [jnp.where(first, own, other), jnp.where(first, other, own)]

    pad_to = lambda v, n: jnp.pad(v, ((0, 0), (0, n - v.shape[1])))
    pack = jnp.concatenate(
        [
            gain_in,
            pad_to(jnp.concatenate([conv_x[0], conv_bc[0]], 1), width),
            pad_to(gain_inner, width),
            pad_to(jnp.concatenate([dt_bias, a_log, d_skip], 1), width),
        ],
        0,
    )
    packs = by_layer(pack, swap(pack))
    gains = [jnp.broadcast_to(p[0:1], (8, width)) for p in packs]

    gate_w, x_w = w_zx[0, :, 0, :], w_zx[0, :, 1, :]
    ends = [jnp.concatenate([gate_w[:, at], x_w[:, at]], 1) for at in (slice(inner), slice(inner, None))]
    zx_own, zx_send = by_layer(*ends)
    bc_own = pad_to(w_bcdt[0], 2 * state + LANES)
    got = swap(jnp.concatenate([zx_send, bc_own], 1))
    zx_shards = by_layer(jnp.concatenate([zx_own, bc_own], 1), got)
    wo_own, wo_send = by_layer(w_out[0, :inner].T, w_out[0, inner:].T)
    wo_shards = by_layer(wo_own, swap(wo_send))
    first_parts = pieces_dp(zx_shards[0])

    rows_at = lambda v, m: jnp.where(first, v[m, :half, 0, :], v[m, half:, 0, :])
    early_in = (first_parts[1], first_parts[4]) if len(first_parts) > 1 else (zx_shards[0],)
    xs = [rows_at(after(x_in, *(early_in if m else zx_shards[:1])), m) for m in micros]
    gs = [rows_at(d_out, m) for m in micros]
    wide = lambda kind, n=0: jax.ShapeDtypeStruct((half, width + n), kind)
    small = jax.ShapeDtypeStruct((16, width), F32)
    rows_of = lambda v: lax.all_gather(v, ("tensor", "section"), axis=0, tiled=True)
    pieces0 = [
        [rows_of(run_plain(norm_kernel, "norm_rows", wide(BF16), (xs[m], gains[0]), ()))]
        for m in micros
    ]
    later = lambda v: lax.all_gather(after(v, *first_parts), "dp", axis=0, tiled=True)
    wo_t0, wo_t1 = later(wo_shards[0]), later(wo_shards[1])
    w1 = later(zx_shards[1])

    doc_lengths, token_mask, *packs = lax.optimization_barrier(
        (doc_lengths, token_mask, *packs, *early_in)
    )[:4]
    scalars, lives = [], []
    for m in micros:
        e0 = doc_lengths[m, 0, 0]
        e1 = e0 + doc_lengths[m, 0, 1]
        scalars.append(jnp.stack([sec, ten, e0, e1, lax.axis_index("dp")]).astype(jnp.int32))
        lives.append(jnp.broadcast_to(token_mask[m].astype(F32), (length, LANES)))
    places = scalars[0]

    layers = []
    for layer in range(2):
        p = packs[layer]
        pick = lambda row, start, count: jnp.where(
            first, p[row : row + 1, start : start + count],
            p[row : row + 1, start + count : start + 2 * count],
        )
        taps = jnp.concatenate(
            [
                jnp.where(first, p[1:6, :inner], p[1:6, inner:chip_inner]),
                p[1:6, chip_inner : chip_inner + 2 * state],
            ],
            1,
        )
        cp = jnp.pad(taps, ((0, 3), (0, 0)))
        bias = pad_to(pick(7, 0, heads), LANES)
        rate = pad_to(-jnp.exp(pick(7, 2 * heads, heads)), LANES)
        hp = jnp.concatenate([bias, rate, jnp.zeros((6, LANES), F32)], 0)
        skip = jnp.broadcast_to(pick(7, 4 * heads, heads).reshape(heads, 1), (heads, HEAD))
        chp = jnp.concatenate(
            [skip.reshape(1, inner), pick(6, 0, inner), jnp.zeros((6, inner), F32)], 0
        )
        layers.append(dict(cp=cp, hp=hp, chp=chp))
    early, late = layers

    def fwd(k, m, pieces, gno, deps, *waits):
        order = None if len(pieces) == 1 else 0
        *nrm, proj, y, st, gated, stats = run_fwd(
            scalars[m], pieces, order, k["w"], k["cp"], k["hp"], k["chp"], lives[m], gno,
            inner, state, heads, deps,
        )
        held = after(stats, *waits)
        part = held + swap(held)
        sums = [part] + [across(part, n) for n in (1, 2, 3)]
        nrm = nrm[0] if nrm else pieces[0]
        return dict(nrm=nrm, proj=proj, y=y, st=st, gated=gated, stats=stats, sums=sums)

    def scale(k, m, r, deps):
        r["no"], send, r["rc"] = run_scale(
            scalars[m], r["gated"], r["sums"], k["chp"], rows, full_inner, deps
        )
        r["sent"] = swap(send)

    def project(k, m, r, deps, axis):
        return run_half(
            scalars[m], r["no"], r["sent"], k["wo"], k["wo_other"], axis, deps, kind=F32
        )

    def project_both(k, r0, r1, deps):
        return run_half(
            scalars[0], r0["no"], r0["sent"], k["wo"], k["wo_other"], 0, deps, (r1["no"], r1["sent"])
        )[0]

    def back(k, m, rows_in, order, r, deps, *waits):
        out = run_bwd(
            scalars[m], rows_in, order, r["proj"], r["y"], r["st"], r["rc"], lives[m],
            k["cp"], k["hp"], k["chp"], inner, state, heads, rows, width, deps,
        )
        gz, gzsend, gpack = out[-3:]
        return gz, swap(after(gzsend, *waits)), gpack, out[0]

    def unproject(k, m, gz, got, deps):
        return run_half(scalars[m], gz, got, k["w_t"], k["w_t_other"], 2, deps)

    def middle(m, parts, deps):
        return run_plain(
            owner_kernel, "owner_mid", (wide(BF16), wide(BF16), wide(F32)),
            (*parts, xs[m], gains[1]), deps,
        )

    early["w"], late["w"] = first_parts, [w1]
    near_g = [reach(after(gs[m], *first_parts), m) for m in micros]

    a0 = fwd(early, 0, pieces0[0], None, ())
    early["wo_t"], late["wo_t"] = wo_t0, wo_t1
    wide_g = [widen(near_g[m], m, a0["stats"]) for m in micros]
    a1 = fwd(early, 1, pieces0[1], None, [a0["stats"]] + [pair[1] for pair in near_g])
    early["wo"] = after(wo_t0, a1["stats"]).T
    early["wo_other"] = swap(early["wo"])
    scale(early, 0, a0, [a1["stats"]] + [pair[1] for pair in wide_g])
    pieces_g = [share(*wide_g[m]) for m in micros]
    outs0 = project(early, 0, a0, (), 2)
    held0 = hand(outs0, 0)
    scale(early, 1, a1, [outs0[0]])
    outs1 = project(early, 1, a1, (), 1)
    held1 = hand(outs1, 1)
    gno0, gout1_0 = run_gn(scalars[0], pieces_g[0], 0, late["wo_t"], width, [outs1[0]])
    parts0, sent0 = settle(held0, 0, gno0)
    gno1, gout1_1 = run_gn(scalars[1], pieces_g[1], 1, late["wo_t"], width, [gno0, sent0])
    parts1, sent1 = settle(held1, 1, gno1)
    h_0, normed_0, u_0 = middle(0, parts0, [gno1])
    pair0 = reach(normed_0, 0)
    h_1, normed_1, u_1 = middle(1, parts1, [normed_0])
    pair1 = reach(normed_1, 0)
    wide0 = widen(pair0, 0, normed_1)
    late["w_t"], late["wo"] = run_turn(places, late["w"], late["wo_t"], [wide0[0]])
    wide1 = widen(pair1, 0, late["wo"])
    early["w_t"], _ = run_turn(places, early["w"], early["wo_t"], [late["wo"], wide1[0]])
    late["wo_other"] = swap(after(late["wo"], wide1[0]))
    late["w_t_other"] = swap(after(late["w_t"], early["w_t"]))
    early["w_t_other"] = swap(early["w_t"])

    b0 = fwd(late, 0, share(wide0[0], after(wide0[1], early["w_t"])), gno0, [early["w_t"]], wide1[1])
    last1 = share(wide1[0], after(wide1[1], b0["stats"]))
    b1 = fwd(late, 1, last1, gno1, [b0["stats"]])
    scale(late, 0, b0, [b1["stats"], early["w_t_other"]])
    gz0, got0, pack0, _ = back(late, 0, (gno0, b0["rc"]), None, b0, [b0["no"], b1["sums"][0]], *b1["sums"][1:])
    scale(late, 1, b1, [pack0])
    outs0 = unproject(late, 0, gz0, got0, [b1["no"]])
    held0 = hand(outs0, 0)
    gz1, got1, pack1, _ = back(late, 1, (gno1, b1["rc"]), None, b1, [outs0[0]])
    parts0, sent0 = settle(held0, 0, pack1)
    g_wo1 = run_outer(
        places, [(gout1_0, b0["no"]), (gout1_1, b1["no"])], None, True, BF16, [pack1, sent0]
    )
    outs1 = unproject(late, 1, gz1, got1, [g_wo1])
    held1 = hand(outs1, 0)

    own_at = ten * rows + sec * half
    rcol = lambda r: lax.dynamic_slice_in_dim(r["rc"], own_at, half, 0)

    def turn(m, parts, h, u, r, deps):
        return run_plain(
            partial(owner_back_kernel, False, full_inner), "owner_back",
            (wide(BF16, LANES), small), (*parts, h, gs[m], gains[1], u, rcol(r)), deps,
        )

    gh_0, gain1_0 = turn(0, parts0, h_0, u_0, a0, [outs1[0]])
    pair0 = reach(gh_0, 0)
    w1_out = run_outer(
        places, [(b0["nrm"], gz0), (b1["nrm"], gz1)], None, True, BF16, [gh_0]
    )
    parts1, sent1 = settle(held1, 0, w1_out, pair0[1])
    wide0 = widen(pair0, 0, w1_out, sent1)
    final = project_both(late, b0, b1, [w1_out, sent1, wide0[0]])
    gh_1, gain1_1 = turn(1, parts1, h_1, u_1, a1, [final])
    pair1 = reach(gh_1, 0)
    turned0 = share(wide0[0], after(wide0[1], gh_1))
    spill = lambda g, axis: lax.psum_scatter(g, "dp", scatter_dimension=axis, tiled=True)
    wo1_sum = spill(g_wo1, 0)
    w1_sum = spill(after(w1_out, sent1), 0)
    over_tensor = lambda v: lax.psum_scatter(v, "tensor", scatter_dimension=0, tiled=True)
    sums = over_tensor(after(final, gh_1))
    tiny1 = pack0 + pack1 + gain1_0 + gain1_1

    wide1 = widen(pair1, 0)
    gz0, got0, pack0, gout0_0 = back(
        early, 0, (turned0, early["wo_t"]), 0, a0, [gh_1, wo1_sum, wide1[0]], wide1[1]
    )
    outs0 = unproject(early, 0, gz0, got0, [pack0, wide1[0]])
    held0 = hand(outs0, 0)
    g_w0 = run_outer(places, [(a0["nrm"], gz0)], None, True, F32, [outs0[0]])
    turned1 = share(wide1[0], after(wide1[1], g_w0))
    gno0_1, gout0_1, cc0_1 = run_gn(scalars[1], turned1, 0, early["wo_t"], width, [g_w0, w1_sum])
    gz1, got1, pack1, _ = back(early, 1, (gno0_1, cc0_1), None, a1, [gno0_1])
    w0_out = run_outer(places, [(a1["nrm"], gz1)], g_w0, True, BF16, [pack1, held0[2]])
    w0_sum = spill(w0_out, 0)
    outs1 = unproject(early, 1, gz1, got1, [w0_out])
    held1 = hand(outs1, 0)
    parts0, _ = settle(held0, 0, pack1)
    g_wo0 = run_outer(
        places, [(gout0_0, a0["no"]), (gout0_1, a1["no"])], None, True, BF16, [outs1[0]]
    )
    wo0_sum = spill(after(g_wo0, w0_sum), 0)
    parts1, sent1 = settle(held1, 0, g_wo0)

    def last(m, parts, gh, deps):
        return run_plain(
            partial(owner_back_kernel, True, full_inner), "owner_last", (wide(F32), small),
            (*parts, xs[m], gh, gains[0]), deps,
        )

    gv_0, gain0_0 = last(0, parts0, gh_0, [sent1, g_wo0])
    finals = run_plain(
        final_kernel, "owner_out", jax.ShapeDtypeStruct((2, half, width), F32),
        (sums.reshape(2, half, width), h_0, h_1), [gv_0],
    )
    out_act = run_join(places, finals, swap(finals))
    gv_1, gain0_1 = last(1, parts1, gh_1, [out_act])
    tiny0 = pack0 + pack1 + gain0_0 + gain0_1

    both = jnp.stack([gv_0, gv_1])
    mine, theirs = by_layer(both[:, :, : width // 2], both[:, :, width // 2 :])
    grad_in = run_join(places, mine, swap(theirs))

    def owned(parts):
        kept, sent = by_layer(parts[0], parts[1])
        return kept, swap(sent)

    kept, got = owned([v[:, : 2 * inner] for v in (w0_sum, w1_sum)])
    grad_w_zx = run_weave(places, kept, got)[None]
    kept, sent = by_layer(tiny0, tiny1)
    mine = sum_dp(kept + swap(sent), grad_in, grad_w_zx)
    shared = all_tensor(mine)
    grad_w_out = jnp.concatenate(by_layer(*owned([wo0_sum, wo1_sum])), 1).T[None].astype(F32)
    cut = lambda v: after(v, got)[:, 2 * inner : 2 * inner + w_bcdt.shape[2]]
    kept, got = owned([cut(v) for v in (w0_sum, w1_sum)])
    shard = kept.astype(F32) + got.astype(F32)
    low = shard.astype(BF16)
    for k in (1, 2, 3):
        shard = shard + across(low, k).astype(F32)
    grad_w_bcdt = shard[None]
    return (
        out_act,
        grad_in,
        shared[0:1],
        grad_w_zx,
        grad_w_bcdt,
        mine[None, 1:6, :chip_inner],
        shared[None, 1:6, chip_inner : chip_inner + 2 * state],
        mine[7:8, : 2 * heads],
        mine[8:9, : 2 * heads],
        mine[9:10, : 2 * heads],
        mine[6:7, :chip_inner],
        grad_w_out,
    )


def solution(mesh):
    return jax.shard_map(
        on_device,
        mesh=mesh,
        in_specs=(
            P(None, "tensor", "dp", None),
            P(None, "tensor", "dp", None),
            P(None, "dp", None),
            P(None, None, "dp"),
            P("section", None),
            P("section", "dp", None, "tensor"),
            P("section", "dp", None),
            P("section", None, "tensor"),
            P("section", None, None),
            P("section", "tensor"),
            P("section", "tensor"),
            P("section", "tensor"),
            P("section", "tensor"),
            P("section", "tensor", "dp"),
        ),
        out_specs=(
            P(None, "tensor", "dp", None),
            P(None, "tensor", "dp", "section"),
            P("section", None),
            P("section", "dp", None, "tensor"),
            P("section", "dp", None),
            P("section", None, "tensor"),
            P("section", None, None),
            P("section", "tensor"),
            P("section", "tensor"),
            P("section", "tensor"),
            P("section", "tensor"),
            P("section", "tensor", "dp"),
        ),
        check_vma=False,
    )
```
